32 devices in a mesh: seq: 2 (over x), batch: 4 (over y, core), head: 4 (over z).
Axes of the slice: x: 2, y: 2, z: 4, core: 2. Of those that a mesh axis runs over, the one named last changes fastest.
Arguments:
- hidden: bfloat16 [4, 256, 16384], P('batch', None, 'seq'), may hold values from -760 to 760
- gain: float32 [16384], P('seq'), may hold values from 0.5 to 1.5
- key_weight: bfloat16 [16384, 1024], P('seq', 'head'), may hold values from -0.046875 to 0.046875
- value_weight: bfloat16 [16384, 1024], P('seq', 'head'), may hold values from -0.046875 to 0.046875
- positions: int32 [4, 256], P('batch', 'seq'), may hold values from 0 to 32767
- initial_basis: float32 [2048, 256], P('head'), may hold values from -6 to 6
Outputs:
- basis: float32 [2048, 256], P('head')
The draws below stay inside these ranges and needn't reach their ends.
All inputs are finite; a program needn't handle non-finite values.
Results may differ from the reference program's by a relative error of at most 0.0063.
Values may be sent and summed in bfloat16 or wider, within the bound.
A program may use at most 64 MiB of HBM per device.

```python
import math
import jax
import jax.numpy as jnp
from jax import lax

D = 16384
KV_HEADS = 8
HEAD_DIM = 128
RANK = 256
ITERS = 4
SEQ_LEN = 256
SEQS = 4
JOINT = 2048


def draw_hidden(key, part):
    subkeys = jax.random.split(key, 4)
    full_shape = (SEQS, SEQ_LEN, D)
    group_width = D // 64
    block_scale = jnp.exp(jax.random.uniform(subkeys[1], (SEQS, SEQ_LEN, 64, 1), jnp.float32, math.log(0.3), math.log(3.0)))
    rising = jnp.exp(math.log(3.0) * jnp.arange(D, dtype=jnp.float32) / D) * jax.random.uniform(subkeys[2], (D,), jnp.float32, 0.7, 1.4)
    token_scale = jnp.exp(jax.random.uniform(subkeys[0], (SEQS, SEQ_LEN, 1), jnp.float32, 0.0, math.log(10.0)))
    base = jnp.clip(jax.random.normal(subkeys[3], full_shape, jnp.float32), -6.0, 6.0)
    values = (base.reshape(SEQS, SEQ_LEN, 64, group_width) * block_scale).reshape(full_shape)
    return (values * rising * token_scale).astype(jnp.bfloat16)


def with_ends(drawn, own_key, low, largest):
    dims = drawn.shape
    spot = [jax.random.randint(jax.random.fold_in(own_key, axis), (), 0, dims[axis]) for axis in range(len(dims))]
    drawn = drawn.at[tuple(spot)].set(low)
    longest = dims.index(max(dims))
    spot[longest] = (spot[longest] + 1) % dims[longest]
    return drawn.at[tuple(spot)].set(largest)


def steps_of(key, extent, cuts, low, high):
    level, own = 1.0, jax.random.fold_in(key, 6)
    for axis_at, shards_of in cuts:
        heights = jnp.exp(jax.random.uniform(jax.random.fold_in(own, axis_at), (shards_of,), jnp.float32, low / len(cuts), high / len(cuts)))
        level = level * jnp.repeat(heights, extent[axis_at] // shards_of).reshape([-1 if axis == axis_at else 1 for axis in range(len(extent))])
    return level


def scatter_about(key, dims, width, limit, pieces=(), held_as=jnp.bfloat16):
    loudness = steps_of(key, dims, pieces, -0.22, 0.18) if pieces else 1.0
    values = jax.random.normal(key, dims, jnp.float32) * width * loudness
    return jnp.minimum(jnp.maximum(values, -limit), limit).astype(held_as)


def setup_inputs(seed: int = 0) -> dict:
    seeds = jax.random.split(jax.random.key(seed), 7)
    hidden = draw_hidden(jax.random.fold_in(seeds[6], 71), 0)
    gain = jnp.clip(1.0 + 0.1 * jax.random.normal(seeds[1], (D,), jnp.float32), 0.5, 1.5)
    key_weight = scatter_about(seeds[2], (D, KV_HEADS * HEAD_DIM), D ** -0.5, 0.046875, ((0, 2), (1, 4)))
    value_weight = scatter_about(seeds[3], (D, KV_HEADS * HEAD_DIM), D ** -0.5, 0.046875, ((0, 2), (1, 4)))
    positions = with_ends(jax.random.randint(seeds[4], (SEQS, SEQ_LEN), 0, 32768), jax.random.fold_in(seeds[4], 1), 0, 32767).astype(jnp.int32)
    initial_basis = scatter_about(seeds[5], (JOINT, RANK), 1.0, 6.0, ((0, 4),), jnp.float32)
    return {"hidden": hidden, "gain": gain, "key_weight": key_weight, "value_weight": value_weight, "positions": positions, "initial_basis": initial_basis}


EPSILON = 1e-05
ROTARY_BASE = 500000.0

def rotary(head_rows, position_row):
    half_width = head_rows.shape[-1] // 2
    index_row = jnp.arange(half_width, dtype=jnp.float32)
    frequency = jnp.exp(index_row * (-math.log(ROTARY_BASE) / half_width))
    angles = position_row.astype(jnp.float32)[:, None] * frequency[None, :]
    cosine = jnp.cos(angles)[:, None, :]
    sine_part = jnp.sin(angles)[:, None, :]
    first_half = head_rows[..., :half_width]
    second_half = head_rows[..., half_width:]
    return jnp.concatenate([first_half * cosine - second_half * sine_part, second_half * cosine + first_half * sine_part], axis=-1)

def joint_of(hidden_rows, gain, key_weight, value_weight, position_row):
    widened = hidden_rows.astype(jnp.float32)
    squares = lax.optimization_barrier(jnp.sum(widened * widened, axis=1))
    inverse_scale = lax.rsqrt(squares / D + EPSILON)
    scaled = (widened * gain).astype(jnp.bfloat16)
    key_proj = jnp.dot(scaled.astype(jnp.float32), key_weight.astype(jnp.float32), preferred_element_type=jnp.float32) * inverse_scale[:, None]
    value_proj = jnp.dot(scaled.astype(jnp.float32), value_weight.astype(jnp.float32), preferred_element_type=jnp.float32) * inverse_scale[:, None]
    length = hidden_rows.shape[0]
    key_rows = rotary(key_proj.reshape(length, -1, HEAD_DIM), position_row)
    value_rows = value_proj.reshape(length, -1, HEAD_DIM)
    return jnp.stack([key_rows, value_rows], axis=2).reshape(length, -1).astype(jnp.bfloat16)

def reference(hidden, gain, key_weight, value_weight, positions, initial_basis):

    def add_sequence(total, items):
        hidden_rows, position_row = items
        joint_rows = joint_of(hidden_rows, gain, key_weight, value_weight, position_row)
        return (total + jnp.dot(joint_rows.T.astype(jnp.float32), joint_rows.astype(jnp.float32), preferred_element_type=jnp.float32), None)
    total, unused = lax.scan(add_sequence, jnp.zeros((JOINT, JOINT), jnp.float32), (hidden, positions))
    covariance = total / (SEQS * SEQ_LEN)
    basis = initial_basis
    for iteration in range(ITERS):
        images = jnp.dot(covariance.astype(jnp.float32), basis.astype(jnp.float32), precision=lax.Precision.HIGHEST, preferred_element_type=jnp.float32)
        gram_matrix = jnp.dot(images.T.astype(jnp.float32), images.astype(jnp.float32), precision=lax.Precision.HIGHEST, preferred_element_type=jnp.float32) / JOINT
        factor = jnp.linalg.cholesky(gram_matrix)
        basis = lax.linalg.triangular_solve(factor, images, left_side=False, lower=True, transpose_a=True)
    return basis
```

```python
import functools
import math

import jax
import jax.numpy as jnp
from jax import lax
from jax.experimental import pallas as pl
from jax.experimental.pallas import tpu as pltpu
from jax.sharding import PartitionSpec as P

D = 16384
HEAD_DIM = 128
ITERS = 4


EPSILON = 1e-05
ROTARY_BASE = 500000.0


def rotary(head_rows, position_row):
    half_width = head_rows.shape[-1] // 2
    index_row = jnp.arange(half_width, dtype=jnp.float32)
    frequency = jnp.exp(index_row * (-math.log(ROTARY_BASE) / half_width))
    angles = position_row.astype(jnp.float32)[:, None] * frequency[None, :]
    cosine = jnp.cos(angles)[:, None, :]
    sine_part = jnp.sin(angles)[:, None, :]
    first_half = head_rows[..., :half_width]
    second_half = head_rows[..., half_width:]
    return jnp.concatenate(
        [
            first_half * cosine - second_half * sine_part,
            second_half * cosine + first_half * sine_part,
        ],
        axis=-1,
    )


def whole_of(basis_block):
    return lax.all_gather(basis_block, "head", axis=0, tiled=True)


def total_squares(local_squares, local_tokens):
    all_squares = lax.psum(local_squares, "seq")
    return lax.dynamic_slice_in_dim(all_squares, lax.axis_index("seq") * local_tokens, local_tokens)


def gram_of(images):
    return lax.dot_general(
        images,
        images,
        (((0,), (0,)), ((), ())),
        precision=lax.Precision.HIGHEST,
        preferred_element_type=jnp.float32,
    )


def orthonormal(images, gram_matrix):
    factor = jnp.linalg.cholesky(gram_matrix)
    return lax.linalg.triangular_solve(
        factor, images, left_side=False, lower=True, transpose_a=True
    )


LANES = 128
SUBLANES = 8


def dot_of(left, right, left_axis, right_axis, precision=None):
    return lax.dot_general(
        left,
        right,
        (((left_axis,), (right_axis,)), ((), ())),
        precision=precision,
        preferred_element_type=jnp.float32,
    )


def exact(left, right, left_axis, right_axis):
    return dot_of(left, right, left_axis, right_axis, lax.Precision.HIGHEST)


def halves_of(value):
    high = value.astype(jnp.bfloat16)
    return high, (value - high.astype(jnp.float32)).astype(jnp.bfloat16)


def thrice(left, right, left_axis, right_axis):
    left_high, left_low = halves_of(left)
    right_high, right_low = halves_of(right)
    return (
        dot_of(left_high, right_high, left_axis, right_axis)
        + dot_of(left_high, right_low, left_axis, right_axis)
        + dot_of(left_low, right_high, left_axis, right_axis)
    )


def inverse_factor(matrix):
    size = matrix.shape[0]
    shape = (SUBLANES, size)
    rows = lax.broadcasted_iota(jnp.int32, shape, 0)
    lanes = lax.broadcasted_iota(jnp.int32, shape, 1)
    groups = size // SUBLANES
    tiles = [matrix[SUBLANES * g : SUBLANES * (g + 1)] for g in range(groups)]
    out = []

    def row_of(value, at):
        return jnp.broadcast_to(value[at : at + 1, :], shape)

    def lane_of(value, at):
        return jnp.broadcast_to(value[:, at : at + 1], shape)

    def total(terms):
        terms = list(terms)
        while len(terms) > 1:
            terms = [terms[i] + terms[i + 1] if i + 1 < len(terms) else terms[i] for i in range(0, len(terms), 2)]
        return terms[0]

    block = [lane_of(tiles[0], j) for j in range(SUBLANES)]
    for own in range(groups):
        pivot = own * SUBLANES
        last_group = own + 1 == groups
        if not last_group:
            below = [lane_of(tiles[own + 1], pivot + j) for j in range(SUBLANES)]
            after = [lane_of(tiles[own + 1], pivot + SUBLANES + j) for j in range(SUBLANES)]
        factor = [None] * SUBLANES
        turned, weighted = [], []
        for k in range(0, SUBLANES, 2):
            one, two = block[k], block[k + 1]
            first, cross, last = row_of(one, k), row_of(two, k), row_of(two, k + 1)
            scale = 1.0 / (first * last - cross * cross)
            top = (one * last - two * cross) * scale
            low = (two * first - one * cross) * scale
            top_row, low_row = first * scale, last * scale
            mixed = cross * scale
            here, next_ = rows == k, rows == k + 1
            pair = here | next_
            top = jnp.where(here, -low_row, jnp.where(next_, mixed, top))
            low = jnp.where(here, mixed, jnp.where(next_, -top_row, low))
            heads = {}
            for j in range(SUBLANES):
                if j in (k, k + 1):
                    continue
                x, y = row_of(block[j], k), row_of(block[j], k + 1)
                heads[j] = (x, y)
                block[j] = jnp.where(pair, 0.0, block[j]) - (top * x + low * y)
            block[k], block[k + 1] = -top, -low
            ratio = cross / first
            top_scale, low_scale = lax.rsqrt(first), lax.rsqrt(last - ratio * cross)
            for j in range(k):
                x, y = heads[j]
                base = factor[j]
                factor[j] = jnp.where(here, x * top_scale, jnp.where(next_, (y - ratio * x) * low_scale, base))
            factor[k] = jnp.where(here, top_scale, jnp.where(next_, -ratio * low_scale, 0.0))
            factor[k + 1] = jnp.where(next_, low_scale, 0.0)
            if not last_group:
                t1 = total([below[k]] + [heads[j][0] * below[j] for j in range(k)])
                t2 = total([below[k + 1]] + [heads[j][1] * below[j] for j in range(k)])
                turned += [t1, t2]
                weighted += [(t1 * last - t2 * cross) * scale, (t2 * first - t1 * cross) * scale]
        inside = (lanes >= pivot) & (lanes < pivot + SUBLANES)
        held = jnp.where(inside, jnp.where(lanes == rows + pivot, 1.0, 0.0), tiles[own])
        spread = [row_of(held, j) for j in range(SUBLANES)]
        result = total([factor[j] * spread[j] for j in range(SUBLANES)])
        out.append(jnp.where(lanes < pivot + SUBLANES, result, 0.0))
        if last_group:
            break
        mixed = total([block[j] * spread[j] for j in range(SUBLANES)])
        mixes = [row_of(mixed, j) for j in range(SUBLANES)]
        following = [
            after[j] - total([turned[m] * row_of(weighted[m], j) for m in range(SUBLANES)])
            for j in range(SUBLANES)
        ]
        columns = [
            [below[j]] + [lane_of(tiles[g], pivot + j) for g in range(own + 2, groups)]
            for j in range(SUBLANES)
        ]
        for g in range(own + 1, groups):
            changes = [columns[j][g - own - 1] * mixes[j] for j in range(SUBLANES)]
            tiles[g] = jnp.where(inside, 0.0, tiles[g]) - total(changes)
        block = following
    return jnp.concatenate(out, axis=0)


def iterate_kernel(
    joint_ref, basis_ref, out_ref, high_ref, low_ref, rows_ref, gram_ref
):
    tokens, joint = joint_ref.shape
    rank = basis_ref.shape[1]
    panels = rank // LANES
    strip = 256
    for start in range(0, tokens, strip):
        kernel_rows = dot_of(joint_ref[start : start + strip, :], joint_ref[...], 1, 1) * (1.0 / tokens)
        high, low = halves_of(kernel_rows)
        high_ref[start : start + strip, :] = high
        low_ref[start : start + strip, :] = low
    basis_high, basis_low = halves_of(basis_ref[...])
    rows_ref[...] = dot_of(joint_ref[...], basis_high, 1, 0) + dot_of(joint_ref[...], basis_low, 1, 0)

    def step(iteration, carry):
        rows_high, rows_low = halves_of(rows_ref[...])
        images = (
            dot_of(high_ref[...], rows_high, 1, 0)
            + dot_of(high_ref[...], rows_low, 1, 0)
            + dot_of(low_ref[...], rows_high, 1, 0)
        )
        images_high, images_low = halves_of(images)
        gram_ref[...] = (
            dot_of(rows_high, images_high, 0, 0)
            + dot_of(rows_high, images_low, 0, 0)
            + dot_of(rows_low, images_high, 0, 0)
        ) * (1.0 / (tokens * joint))

        @pl.when(iteration < ITERS - 1)
        def _():
            rows_ref[...] = images

        for panel in range(panels):
            start, end = panel * LANES, (panel + 1) * LANES
            inverse = inverse_factor(gram_ref[start:end, start:end])
            columns = thrice(rows_ref[:, start:end], inverse, 1, 1)
            rows_ref[:, start:end] = columns
            if end < rank:
                scaled = exact(inverse, gram_ref[start:end, end:], 1, 0)
                gram_ref[end:, end:] -= exact(scaled, scaled, 0, 0)
                rows_ref[:, end:] -= thrice(columns, scaled, 1, 0)
        return carry

    lax.fori_loop(0, ITERS, step, 0)
    rows_high, rows_low = halves_of(rows_ref[...])
    width = out_ref.shape[0]
    own = joint_ref[:, pl.ds(pl.multiple_of(lax.axis_index("head") * width, width), width)]
    out_ref[...] = (dot_of(own, rows_high, 0, 0) + dot_of(own, rows_low, 0, 0)) * (1.0 / tokens)


def iterate(joint_all, basis_all):
    tokens, joint = joint_all.shape
    rank = basis_all.shape[1]
    return pl.pallas_call(
        iterate_kernel,
        out_shape=jax.ShapeDtypeStruct((joint // lax.axis_size("head"), rank), jnp.float32),
        in_specs=[pl.BlockSpec(memory_space=pltpu.VMEM)] * 2,
        out_specs=pl.BlockSpec(memory_space=pltpu.VMEM),
        scratch_shapes=[
            pltpu.VMEM((tokens, tokens), jnp.bfloat16),
            pltpu.VMEM((tokens, tokens), jnp.bfloat16),
            pltpu.VMEM((tokens, rank), jnp.float32),
            pltpu.VMEM((rank, rank), jnp.float32),
        ],
        compiler_params=pltpu.CompilerParams(vmem_limit_bytes=40 * 2**20),
    )(joint_all, basis_all)


def project_kernel(hidden_ref, gain_ref, key_ref, value_ref, partial_ref, squares_ref):
    key_columns = key_ref.shape[1]

    @pl.when(pl.program_id(0) == 0)
    def _():
        partial_ref[...] = jnp.zeros_like(partial_ref)
        squares_ref[...] = jnp.zeros_like(squares_ref)

    widened = hidden_ref[...].astype(jnp.float32)
    scaled = (widened * gain_ref[...]).astype(jnp.bfloat16)
    partial_ref[:, :key_columns] += dot_of(scaled, key_ref[...], 1, 0)
    partial_ref[:, key_columns:] += dot_of(scaled, value_ref[...], 1, 0)
    squared = widened * widened
    total = squares_ref[...]
    for start in range(0, squared.shape[1], LANES):
        total = total + squared[:, start : start + LANES]
    squares_ref[...] = total


def project(hidden_rows, gain, key_weight, value_weight):
    tokens, depth = hidden_rows.shape
    key_columns, value_columns = key_weight.shape[1], value_weight.shape[1]
    chunk = math.gcd(depth, 1024)
    return pl.pallas_call(
        project_kernel,
        grid=(depth // chunk,),
        out_shape=(
            jax.ShapeDtypeStruct((tokens, key_columns + value_columns), jnp.float32),
            jax.ShapeDtypeStruct((tokens, LANES), jnp.float32),
        ),
        in_specs=[
            pl.BlockSpec((tokens, chunk), lambda step: (0, step)),
            pl.BlockSpec((1, chunk), lambda step: (0, step)),
            pl.BlockSpec((chunk, key_columns), lambda step: (step, 0)),
            pl.BlockSpec((chunk, value_columns), lambda step: (step, 0)),
        ],
        out_specs=(
            pl.BlockSpec((tokens, key_columns + value_columns), lambda step: (0, 0)),
            pl.BlockSpec((tokens, LANES), lambda step: (0, 0)),
        ),
        compiler_params=pltpu.CompilerParams(
            dimension_semantics=("arbitrary",), vmem_limit_bytes=60 * 2**20
        ),
    )(hidden_rows, gain[None, :], key_weight, value_weight)


def gather_kernel(
    heads,
    partial_ref,
    squares_ref,
    cosine_ref,
    sine_ref,
    basis_ref,
    out_ref,
    whole_ref,
    peer_partial,
    peer_squares,
    swap_sems,
    z_sems,
    x_sems,
    y_sems,
    x_half_sems,
    y_half_sems,
    core_sems,
):
    x, b, z = lax.axis_index("seq"), lax.axis_index("batch"), lax.axis_index("head")
    local, width = peer_partial.shape
    half = width // 2
    rank = basis_ref.shape[1]
    piece = width // 8
    other_x, other_y = 1 - x, (b + 2) % 4
    partner = b + 1 - 2 * (b % 2)
    x_peer, y_peer, core_peer = (other_x, b, z), (x, other_y, z), (x, partner, z)

    def z_peer(d):
        return (x, b, (z + d) % heads)

    barrier = pltpu.get_barrier_semaphore()
    peers = [x_peer, y_peer, core_peer] + [z_peer(d) for d in range(1, heads)]
    for peer in peers:
        pl.semaphore_signal(barrier, inc=1, device_id=peer, device_id_type=pl.DeviceIdType.MESH)
    pl.semaphore_wait(barrier, len(peers))

    def copy(source, target, sems, peer):
        return pltpu.make_async_remote_copy(
            src_ref=source,
            dst_ref=target,
            send_sem=sems.at[0],
            recv_sem=sems.at[1],
            device_id=peer,
            device_id_type=pl.DeviceIdType.MESH,
        )

    def region(xs, bs, zs, start=0, size=width):
        row = pl.multiple_of((xs * 4 + bs) * local, local)
        column = pl.multiple_of(zs * width + start, half)
        return out_ref.at[pl.ds(row, local), pl.ds(column, size)]

    def piece_of(xs, bs, zs, start=0, size=rank):
        row = pl.multiple_of(zs * width + (xs * 4 + bs) * piece, piece)
        return whole_ref.at[pl.ds(row, piece), pl.ds(start, size)]

    started = []

    def send(area, sems, peer):
        going = copy(area, area, sems, peer)
        going.start()
        started.append(going)

    def arrive(area, sems, peer):
        copy(area, area, sems, peer).wait_recv()

    def source(d):
        return (z + heads - d) % heads

    order = [0] + sorted(range(1, heads), key=lambda d: (min(d, heads - d), d))
    own_piece = basis_ref.at[pl.ds(pl.multiple_of((x * 4 + b) * piece, piece), piece), :]
    for d in range(1, heads):
        going = copy(own_piece, piece_of(x, b, z), z_sems.at[1, d], z_peer(d))
        going.start()
        started.append(going)

    away = pl.ds(pl.multiple_of(other_x * local, local), local)
    mine = pl.ds(pl.multiple_of(x * local, local), local)
    swaps = [
        copy(partial_ref.at[away, :], peer_partial, swap_sems.at[0], x_peer),
        copy(squares_ref.at[away, :], peer_squares, swap_sems.at[1], x_peer),
    ]
    for swap in swaps:
        swap.start()
    whole_ref[pl.ds(pl.multiple_of(z * width, width), width), :] = basis_ref[...]
    for swap in swaps:
        swap.wait()
    squares = jnp.sum(squares_ref[mine, :] + peer_squares[...], axis=1, keepdims=True)
    projected = (partial_ref[mine, :] + peer_partial[...]) * lax.rsqrt(squares / D + EPSILON)
    row = pl.multiple_of((x * 4 + b) * local, local)
    for g in range(half // HEAD_DIM):
        key = projected[:, g * HEAD_DIM : (g + 1) * HEAD_DIM]
        turned = key * cosine_ref[...] + pltpu.roll(key, HEAD_DIM // 2, 1) * sine_ref[...]
        value = projected[:, half + g * HEAD_DIM : half + (g + 1) * HEAD_DIM]
        column = pl.multiple_of(z * width + 2 * g * HEAD_DIM, HEAD_DIM)
        out_ref[pl.ds(row, local), pl.ds(column, HEAD_DIM)] = turned.astype(jnp.bfloat16)
        column = pl.multiple_of(z * width + (2 * g + 1) * HEAD_DIM, HEAD_DIM)
        out_ref[pl.ds(row, local), pl.ds(column, HEAD_DIM)] = value.astype(jnp.bfloat16)

    for d in range(1, heads):
        send(region(x, b, z), z_sems.at[0, d], z_peer(d))

    def spread(kind, area, middle, d):
        mine = area(x, b, source(d))
        if d:
            arrive(mine, z_sems.at[kind, d], z_peer(d))
        send(mine, x_sems.at[kind, d], x_peer)
        send(mine, y_sems.at[kind, d], y_peer)
        send(mine, core_sems.at[kind, d, 0], core_peer)

    def relay(kind, area, middle, d):
        s = source(d)
        arrive(area(other_x, b, s), x_sems.at[kind, d], x_peer)
        send(area(other_x, b, s, middle, middle), y_half_sems.at[kind, d], y_peer)
        send(area(other_x, b, s), core_sems.at[kind, d, 1], core_peer)
        arrive(area(x, other_y, s), y_sems.at[kind, d], y_peer)
        send(area(x, other_y, s, 0, middle), x_half_sems.at[kind, d], x_peer)
        send(area(x, other_y, s), core_sems.at[kind, d, 2], core_peer)

    def finish(kind, area, middle, d):
        s = source(d)
        arrive(area(other_x, other_y, s, 0, middle), x_half_sems.at[kind, d], x_peer)
        arrive(area(other_x, other_y, s, middle, middle), y_half_sems.at[kind, d], y_peer)
        send(area(other_x, other_y, s), core_sems.at[kind, d, 3], core_peer)

    joint, pieces = (0, region, half), (1, piece_of, rank // 2)
    items = [joint + (0,)] + [pieces + (d,) for d in order[1:]] + [joint + (d,) for d in order[1:]]
    for turn in range(len(items) + 2):
        if turn < len(items):
            spread(*items[turn])
        if 1 <= turn < len(items) + 1:
            relay(*items[turn - 1])
        if turn >= 2:
            finish(*items[turn - 2])
    far = (partner + 2) % 4
    for kind, area, middle, d in items:
        s = source(d)
        places = [(x, partner), (other_x, partner), (x, far), (other_x, far)]
        for place, (xs, bs) in enumerate(places):
            arrive(area(xs, bs, s), core_sems.at[kind, d, place], core_peer)
    for going in started:
        going.wait_send()


def gather(partial, squares, positions, basis, heads, tokens):
    local, width = positions.shape[0], partial.shape[1]
    half_width = HEAD_DIM // 2
    frequency = jnp.exp(
        jnp.arange(half_width, dtype=jnp.float32) * (-math.log(ROTARY_BASE) / half_width)
    )
    angles = positions.astype(jnp.float32)[:, None] * frequency[None, :]
    cosine, sine = jnp.cos(angles), jnp.sin(angles)
    dma = pltpu.SemaphoreType.DMA
    return pl.pallas_call(
        functools.partial(gather_kernel, heads),
        out_shape=(
            jax.ShapeDtypeStruct((tokens, heads * width), jnp.bfloat16),
            jax.ShapeDtypeStruct((heads * width, basis.shape[1]), jnp.float32),
        ),
        in_specs=[pl.BlockSpec(memory_space=pltpu.VMEM)] * 5,
        out_specs=(pl.BlockSpec(memory_space=pltpu.VMEM),) * 2,
        scratch_shapes=[
            pltpu.VMEM((local, width), jnp.float32),
            pltpu.VMEM((local, LANES), jnp.float32),
            dma((2, 2)),
            dma((2, heads, 2)),
            dma((2, heads, 2)),
            dma((2, heads, 2)),
            dma((2, heads, 2)),
            dma((2, heads, 2)),
            dma((2, heads, 4, 2)),
        ],
        compiler_params=pltpu.CompilerParams(
            collective_id=0, has_side_effects=True, vmem_limit_bytes=24 * 2**20
        ),
    )(
        partial,
        squares,
        jnp.concatenate([cosine, cosine], axis=1),
        jnp.concatenate([-sine, sine], axis=1),
        basis,
    )


def body(hidden, gain, key_weight, value_weight, positions, initial_basis):
    hidden_rows = hidden[0]
    local_tokens = positions.shape[1]
    seqs, batches, heads = lax.axis_size("seq"), lax.axis_size("batch"), lax.axis_size("head")
    tokens = local_tokens * seqs * batches
    if seqs == 2 and batches == 4 and tokens <= initial_basis.shape[0] * heads:
        partial, squares = project(hidden_rows, gain, key_weight, value_weight)
        return iterate(*gather(partial, squares, positions[0], initial_basis, heads, tokens))
    widened = hidden_rows.astype(jnp.float32)
    scaled = (widened * gain).astype(jnp.bfloat16)
    local_squares = jnp.sum(widened * widened, axis=1)
    key_columns = key_weight.shape[1]
    weights = jnp.concatenate([key_weight, value_weight], axis=1)
    own_squares = total_squares(local_squares, local_tokens)
    projected = lax.psum_scatter(
        jnp.dot(scaled, weights, preferred_element_type=jnp.float32),
        "seq",
        scatter_dimension=0,
        tiled=True,
    )
    inverse_scale = lax.rsqrt(own_squares / D + EPSILON)
    projected = projected * inverse_scale[:, None]
    key_rows = rotary(projected[:, :key_columns].reshape(local_tokens, -1, HEAD_DIM), positions[0])
    value_rows = projected[:, key_columns:].reshape(local_tokens, -1, HEAD_DIM)
    joint_rows = (
        jnp.stack([key_rows, value_rows], axis=2).reshape(local_tokens, -1).astype(jnp.bfloat16)
    )
    partial_value = lax.dot_general(
        joint_rows,
        lax.all_gather(joint_rows, "head", axis=1, tiled=True),
        (((0,), (0,)), ((), ())),
        preferred_element_type=jnp.float32,
    )
    token_total = local_tokens * lax.axis_size("seq") * lax.axis_size("batch")
    basis_block = initial_basis
    covariance = lax.psum(partial_value, ("seq", "batch")) / token_total
    for iteration in range(ITERS):
        whole_basis = whole_of(basis_block)
        images = jnp.dot(
            covariance,
            whole_basis,
            precision=lax.Precision.HIGHEST,
            preferred_element_type=jnp.float32,
        )
        gram_matrix = lax.psum(gram_of(images), "head") / whole_basis.shape[0]
        basis_block = orthonormal(images, gram_matrix)
    return basis_block


def solution(mesh):
    return jax.shard_map(
        body,
        mesh=mesh,
        in_specs=(
            P("batch", None, "seq"),
            P("seq"),
            P("seq", "head"),
            P("seq", "head"),
            P("batch", "seq"),
            P("head", None),
        ),
        out_specs=P("head", None),
        check_vma=False,
    )
```

```python
import functools
import math

import jax
import jax.numpy as jnp
from jax import lax
from jax.experimental import pallas as pl
from jax.experimental.pallas import tpu as pltpu
from jax.sharding import PartitionSpec as P

D = 16384
HEAD_DIM = 128
ITERS = 4


EPSILON = 1e-05
ROTARY_BASE = 500000.0


def rotary(head_rows, position_row):
    half_width = head_rows.shape[-1] // 2
    index_row = jnp.arange(half_width, dtype=jnp.float32)
    frequency = jnp.exp(index_row * (-math.log(ROTARY_BASE) / half_width))
    angles = position_row.astype(jnp.float32)[:, None] * frequency[None, :]
    cosine = jnp.cos(angles)[:, None, :]
    sine_part = jnp.sin(angles)[:, None, :]
    first_half = head_rows[..., :half_width]
    second_half = head_rows[..., half_width:]
    return jnp.concatenate(
        [
            first_half * cosine - second_half * sine_part,
            second_half * cosine + first_half * sine_part,
        ],
        axis=-1,
    )


def whole_of(basis_block):
    return lax.all_gather(basis_block, "head", axis=0, tiled=True)


def total_squares(local_squares, local_tokens):
    all_squares = lax.psum(local_squares, "seq")
    return lax.dynamic_slice_in_dim(all_squares, lax.axis_index("seq") * local_tokens, local_tokens)


def gram_of(images):
    return lax.dot_general(
        images,
        images,
        (((0,), (0,)), ((), ())),
        precision=lax.Precision.HIGHEST,
        preferred_element_type=jnp.float32,
    )


def orthonormal(images, gram_matrix):
    factor = jnp.linalg.cholesky(gram_matrix)
    return lax.linalg.triangular_solve(
        factor, images, left_side=False, lower=True, transpose_a=True
    )


LANES = 128
SUBLANES = 8


def dot_of(left, right, left_axis, right_axis, precision=None):
    return lax.dot_general(
        left,
        right,
        (((left_axis,), (right_axis,)), ((), ())),
        precision=precision,
        preferred_element_type=jnp.float32,
    )


def exact(left, right, left_axis, right_axis):
    return dot_of(left, right, left_axis, right_axis, lax.Precision.HIGHEST)


def halves_of(value):
    high = value.astype(jnp.bfloat16)
    return high, (value - high.astype(jnp.float32)).astype(jnp.bfloat16)


def thrice(left, right, left_axis, right_axis):
    left_high, left_low = halves_of(left)
    right_high, right_low = halves_of(right)
    return (
        dot_of(left_high, right_high, left_axis, right_axis)
        + dot_of(left_high, right_low, left_axis, right_axis)
        + dot_of(left_low, right_high, left_axis, right_axis)
    )


def inverse_factor(matrix):
    size = matrix.shape[0]
    shape = (SUBLANES, size)
    rows = lax.broadcasted_iota(jnp.int32, shape, 0)
    lanes = lax.broadcasted_iota(jnp.int32, shape, 1)
    groups = size // SUBLANES
    tiles = [matrix[SUBLANES * g : SUBLANES * (g + 1)] for g in range(groups)]
    out = []

    def row_of(value, at):
        return jnp.broadcast_to(value[at : at + 1, :], shape)

    def lane_of(value, at):
        return jnp.broadcast_to(value[:, at : at + 1], shape)

    def total(terms):
        terms = list(terms)
        while len(terms) > 1:
            terms = [terms[i] + terms[i + 1] if i + 1 < len(terms) else terms[i] for i in range(0, len(terms), 2)]
        return terms[0]

    block = [lane_of(tiles[0], j) for j in range(SUBLANES)]
    for own in range(groups):
        pivot = own * SUBLANES
        last_group = own + 1 == groups
        if not last_group:
            below = [lane_of(tiles[own + 1], pivot + j) for j in range(SUBLANES)]
            after = [lane_of(tiles[own + 1], pivot + SUBLANES + j) for j in range(SUBLANES)]
        factor = [None] * SUBLANES
        turned, weighted = [], []
        for k in range(0, SUBLANES, 2):
            one, two = block[k], block[k + 1]
            first, cross, last = row_of(one, k), row_of(two, k), row_of(two, k + 1)
            scale = 1.0 / (first * last - cross * cross)
            top = (one * last - two * cross) * scale
            low = (two * first - one * cross) * scale
            top_row, low_row = first * scale, last * scale
            mixed = cross * scale
            here, next_ = rows == k, rows == k + 1
            pair = here | next_
            top = jnp.where(here, -low_row, jnp.where(next_, mixed, top))
            low = jnp.where(here, mixed, jnp.where(next_, -top_row, low))
            heads = {}
            for j in range(SUBLANES):
                if j in (k, k + 1):
                    continue
                x, y = row_of(block[j], k), row_of(block[j], k + 1)
                heads[j] = (x, y)
                block[j] = jnp.where(pair, 0.0, block[j]) - (top * x + low * y)
            block[k], block[k + 1] = -top, -low
            ratio = cross / first
            top_scale, low_scale = lax.rsqrt(first), lax.rsqrt(last - ratio * cross)
            for j in range(k):
                x, y = heads[j]
                base = factor[j]
                factor[j] = jnp.where(here, x * top_scale, jnp.where(next_, (y - ratio * x) * low_scale, base))
            factor[k] = jnp.where(here, top_scale, jnp.where(next_, -ratio * low_scale, 0.0))
            factor[k + 1] = jnp.where(next_, low_scale, 0.0)
            if not last_group:
                t1 = total([below[k]] + [heads[j][0] * below[j] for j in range(k)])
                t2 = total([below[k + 1]] + [heads[j][1] * below[j] for j in range(k)])
                turned += [t1, t2]
                weighted += [(t1 * last - t2 * cross) * scale, (t2 * first - t1 * cross) * scale]
        inside = (lanes >= pivot) & (lanes < pivot + SUBLANES)
        held = jnp.where(inside, jnp.where(lanes == rows + pivot, 1.0, 0.0), tiles[own])
        spread = [row_of(held, j) for j in range(SUBLANES)]
        result = total([factor[j] * spread[j] for j in range(SUBLANES)])
        out.append(jnp.where(lanes < pivot + SUBLANES, result, 0.0))
        if last_group:
            break
        mixed = total([block[j] * spread[j] for j in range(SUBLANES)])
        mixes = [row_of(mixed, j) for j in range(SUBLANES)]
        following = [
            after[j] - total([turned[m] * row_of(weighted[m], j) for m in range(SUBLANES)])
            for j in range(SUBLANES)
        ]
        columns = [
            [below[j]] + [lane_of(tiles[g], pivot + j) for g in range(own + 2, groups)]
            for j in range(SUBLANES)
        ]
        for g in range(own + 1, groups):
            changes = [columns[j][g - own - 1] * mixes[j] for j in range(SUBLANES)]
            tiles[g] = jnp.where(inside, 0.0, tiles[g]) - total(changes)
        block = following
    return jnp.concatenate(out, axis=0)


def iterate_kernel(
    joint_ref, basis_ref, out_ref, high_ref, low_ref, rows_ref, gram_ref
):
    tokens, joint = joint_ref.shape
    rank = basis_ref.shape[1]
    panels = rank // LANES
    strip = 256
    for start in range(0, tokens, strip):
        kernel_rows = dot_of(joint_ref[start : start + strip, :], joint_ref[...], 1, 1) * (1.0 / tokens)
        high, low = halves_of(kernel_rows)
        high_ref[start : start + strip, :] = high
        low_ref[start : start + strip, :] = low
    basis_high, basis_low = halves_of(basis_ref[...])
    rows_ref[...] = dot_of(joint_ref[...], basis_high, 1, 0) + dot_of(joint_ref[...], basis_low, 1, 0)

    def step(iteration, carry):
        rows_high, rows_low = halves_of(rows_ref[...])
        images = (
            dot_of(high_ref[...], rows_high, 1, 0)
            + dot_of(high_ref[...], rows_low, 1, 0)
            + dot_of(low_ref[...], rows_high, 1, 0)
        )
        images_high, images_low = halves_of(images)
        gram_ref[...] = (
            dot_of(rows_high, images_high, 0, 0)
            + dot_of(rows_high, images_low, 0, 0)
            + dot_of(rows_low, images_high, 0, 0)
        ) * (1.0 / (tokens * joint))

        @pl.when(iteration < ITERS - 1)
        def _():
            rows_ref[...] = images

        for panel in range(panels):
            start, end = panel * LANES, (panel + 1) * LANES
            inverse = inverse_factor(gram_ref[start:end, start:end])
            columns = thrice(rows_ref[:, start:end], inverse, 1, 1)
            rows_ref[:, start:end] = columns
            if end < rank:
                scaled = exact(inverse, gram_ref[start:end, end:], 1, 0)
                gram_ref[end:, end:] -= exact(scaled, scaled, 0, 0)
                rows_ref[:, end:] -= thrice(columns, scaled, 1, 0)
        return carry

    lax.fori_loop(0, ITERS, step, 0)
    rows_high, rows_low = halves_of(rows_ref[...])
    width = out_ref.shape[0]
    own = joint_ref[:, pl.ds(pl.multiple_of(lax.axis_index("head") * width, width), width)]
    out_ref[...] = (dot_of(own, rows_high, 0, 0) + dot_of(own, rows_low, 0, 0)) * (1.0 / tokens)


def iterate(joint_all, basis_all):
    tokens, joint = joint_all.shape
    rank = basis_all.shape[1]
    return pl.pallas_call(
        iterate_kernel,
        out_shape=jax.ShapeDtypeStruct((joint // lax.axis_size("head"), rank), jnp.float32),
        in_specs=[pl.BlockSpec(memory_space=pltpu.VMEM)] * 2,
        out_specs=pl.BlockSpec(memory_space=pltpu.VMEM),
        scratch_shapes=[
            pltpu.VMEM((tokens, tokens), jnp.bfloat16),
            pltpu.VMEM((tokens, tokens), jnp.bfloat16),
            pltpu.VMEM((tokens, rank), jnp.float32),
            pltpu.VMEM((rank, rank), jnp.float32),
        ],
        compiler_params=pltpu.CompilerParams(vmem_limit_bytes=40 * 2**20),
    )(joint_all, basis_all)


def collect_kernel(
    heads,
    hidden_ref,
    gain_ref,
    key_ref,
    value_ref,
    cosine_ref,
    sine_ref,
    basis_ref,
    out_ref,
    whole_ref,
    hidden_rows,
    gain_row,
    key_rows,
    value_rows,
    partial,
    peer_partial,
    squares,
    peer_squares,
    load_sems,
    half_sems,
    swap_sems,
    z_sems,
    x_sems,
    y_sems,
    x_half_sems,
    y_half_sems,
    core_sems,
):
    x, b, z = lax.axis_index("seq"), lax.axis_index("batch"), lax.axis_index("head")
    local, width = peer_partial.shape
    half = width // 2
    rank = whole_ref.shape[1]
    piece = width // 8
    depth = gain_row.shape[1]
    chunks = load_sems.shape[1]
    chunk = depth // chunks
    other_x, other_y = 1 - x, (b + 2) % 4
    partner = b + 1 - 2 * (b % 2)
    x_peer, y_peer, core_peer = (other_x, b, z), (x, other_y, z), (x, partner, z)
    away = pl.ds(pl.multiple_of(other_x * local, local), local)
    mine = pl.ds(pl.multiple_of(x * local, local), local)

    def z_peer(d):
        return (x, b, (z + d) % heads)

    own_block = whole_ref.at[pl.ds(pl.multiple_of(z * width, width), width), :]
    basis_load = pltpu.make_async_copy(basis_ref, own_block, half_sems.at[2, 0])
    gain_load = pltpu.make_async_copy(gain_ref, gain_row, half_sems.at[2, 1])

    def span(c):
        return pl.ds(c * chunk, chunk)

    def token_load(kind, area, c):
        return pltpu.make_async_copy(
            hidden_ref.at[area, span(c)], hidden_rows.at[area, span(c)], half_sems.at[kind, c]
        )

    away_loads = [token_load(0, away, c) for c in range(chunks)]
    mine_loads = [token_load(1, mine, c) for c in range(chunks)]
    key_loads = [
        pltpu.make_async_copy(key_ref.at[span(c), :], key_rows.at[span(c), :], load_sems.at[0, c])
        for c in range(chunks)
    ]
    value_loads = [
        pltpu.make_async_copy(
            value_ref.at[span(c), :], value_rows.at[span(c), :], load_sems.at[1, c]
        )
        for c in range(chunks)
    ]
    basis_load.start()
    gain_load.start()
    for c in range(chunks):
        away_loads[c].start()
        key_loads[c].start()
    for load in value_loads + mine_loads:
        load.start()

    barrier = pltpu.get_barrier_semaphore()
    peers = [x_peer, y_peer, core_peer] + [z_peer(d) for d in range(1, heads)]
    for peer in peers:
        pl.semaphore_signal(barrier, inc=1, device_id=peer, device_id_type=pl.DeviceIdType.MESH)
    pl.semaphore_wait(barrier, len(peers))

    def copy(source, target, sems, peer):
        return pltpu.make_async_remote_copy(
            src_ref=source,
            dst_ref=target,
            send_sem=sems.at[0],
            recv_sem=sems.at[1],
            device_id=peer,
            device_id_type=pl.DeviceIdType.MESH,
        )

    def region(xs, bs, zs, start=0, size=width):
        row = pl.multiple_of((xs * 4 + bs) * local, local)
        column = pl.multiple_of(zs * width + start, half)
        return out_ref.at[pl.ds(row, local), pl.ds(column, size)]

    def piece_of(xs, bs, zs, start=0, size=rank):
        row = pl.multiple_of(zs * width + (xs * 4 + bs) * piece, piece)
        return whole_ref.at[pl.ds(row, piece), pl.ds(start, size)]

    started = []

    def send(area, sems, peer):
        going = copy(area, area, sems, peer)
        going.start()
        started.append(going)

    def arrive(area, sems, peer):
        copy(area, area, sems, peer).wait_recv()

    def source(d):
        return (z + heads - d) % heads

    def spread(kind, area, middle, d):
        own = area(x, b, source(d))
        if d:
            arrive(own, z_sems.at[kind, d], z_peer(d))
        send(own, x_sems.at[kind, d], x_peer)
        send(own, y_sems.at[kind, d], y_peer)
        send(own, core_sems.at[kind, d, 0], core_peer)

    def relay(kind, area, middle, d):
        s = source(d)
        arrive(area(other_x, b, s), x_sems.at[kind, d], x_peer)
        send(area(other_x, b, s, middle, middle), y_half_sems.at[kind, d], y_peer)
        send(area(other_x, b, s), core_sems.at[kind, d, 1], core_peer)
        arrive(area(x, other_y, s), y_sems.at[kind, d], y_peer)
        send(area(x, other_y, s, 0, middle), x_half_sems.at[kind, d], x_peer)
        send(area(x, other_y, s), core_sems.at[kind, d, 2], core_peer)

    def finish(kind, area, middle, d):
        s = source(d)
        arrive(area(other_x, other_y, s, 0, middle), x_half_sems.at[kind, d], x_peer)
        arrive(area(other_x, other_y, s, middle, middle), y_half_sems.at[kind, d], y_peer)
        send(area(other_x, other_y, s), core_sems.at[kind, d, 3], core_peer)

    order = [0] + sorted(range(1, heads), key=lambda d: (min(d, heads - d), d))
    joint = [(0, region, half, d) for d in order]
    pieces = [(1, piece_of, rank // 2, d) for d in order[1:]]

    basis_load.wait()
    for d in order[1:]:
        send(piece_of(x, b, z), z_sems.at[1, d], z_peer(d))

    def prepare(area, c, total):
        widened = hidden_rows[area, span(c)].astype(jnp.float32)
        scaled = (widened * gain_row[:, span(c)]).astype(jnp.bfloat16)
        hidden_rows[area, span(c)] = scaled
        squared = widened * widened
        for start in range(0, chunk, LANES):
            total = total + squared[:, start : start + LANES]
        return scaled, total

    def across(total):
        ones = jnp.ones((SUBLANES, LANES), jnp.float32)
        return exact(ones, total, 1, 1)

    def swap(source_ref, target_ref, index):
        going = copy(source_ref, target_ref, swap_sems.at[index], x_peer)
        going.start()
        return going

    gain_load.wait()
    away_total = jnp.zeros((local, LANES), jnp.float32)
    sums = jnp.zeros((local, half), jnp.float32)
    for c in range(chunks):
        away_loads[c].wait()
        scaled, away_total = prepare(away, c, away_total)
        key_loads[c].wait()
        sums = sums + dot_of(scaled, key_rows[span(c), :], 1, 0)
    partial[:, :half] = sums
    squares[...] = across(away_total)
    swaps = [
        swap(squares, peer_squares, 0),
        swap(partial.at[:, pl.ds(0, half)], peer_partial.at[:, pl.ds(0, half)], 1),
    ]
    for item in pieces:
        spread(*item)
    sums = jnp.zeros((local, half), jnp.float32)
    for c in range(chunks):
        value_loads[c].wait()
        sums = sums + dot_of(hidden_rows[away, span(c)], value_rows[span(c), :], 1, 0)
    partial[:, half:] = sums
    swaps.append(swap(partial.at[:, pl.ds(half, half)], peer_partial.at[:, pl.ds(half, half)], 2))
    for item in pieces:
        relay(*item)
    mine_total = jnp.zeros((local, LANES), jnp.float32)
    key_sums = jnp.zeros((local, half), jnp.float32)
    value_sums = jnp.zeros((local, half), jnp.float32)
    for c in range(chunks):
        mine_loads[c].wait()
        scaled, mine_total = prepare(mine, c, mine_total)
        key_sums = key_sums + dot_of(scaled, key_rows[span(c), :], 1, 0)
        value_sums = value_sums + dot_of(scaled, value_rows[span(c), :], 1, 0)
    own_squares = across(mine_total)
    for item in pieces:
        finish(*item)

    swaps[0].wait()
    eighths = jnp.full((SUBLANES, LANES), 1.0 / SUBLANES, jnp.float32)
    inverse_scale = lax.rsqrt(exact(own_squares + peer_squares[...], eighths, 0, 0) / D + EPSILON)
    row = pl.multiple_of((x * 4 + b) * local, local)
    swaps[1].wait()
    for g in range(half // HEAD_DIM):
        spot = slice(g * HEAD_DIM, (g + 1) * HEAD_DIM)
        key = (key_sums[:, spot] + peer_partial[:, spot]) * inverse_scale
        turned = key * cosine_ref[...] + pltpu.roll(key, HEAD_DIM // 2, 1) * sine_ref[...]
        column = pl.multiple_of(z * width + 2 * g * HEAD_DIM, HEAD_DIM)
        out_ref[pl.ds(row, local), pl.ds(column, HEAD_DIM)] = turned.astype(jnp.bfloat16)
    swaps[2].wait()
    for g in range(half // HEAD_DIM):
        spot = slice(g * HEAD_DIM, (g + 1) * HEAD_DIM)
        there = slice(half + g * HEAD_DIM, half + (g + 1) * HEAD_DIM)
        value = (value_sums[:, spot] + peer_partial[:, there]) * inverse_scale
        column = pl.multiple_of(z * width + (2 * g + 1) * HEAD_DIM, HEAD_DIM)
        out_ref[pl.ds(row, local), pl.ds(column, HEAD_DIM)] = value.astype(jnp.bfloat16)

    for d in order[1:]:
        send(region(x, b, z), z_sems.at[0, d], z_peer(d))
    for turn in range(len(joint) + 2):
        if turn < len(joint):
            spread(*joint[turn])
        if 1 <= turn < len(joint) + 1:
            relay(*joint[turn - 1])
        if turn >= 2:
            finish(*joint[turn - 2])
    far = (partner + 2) % 4
    for kind, area, middle, d in pieces + joint:
        s = source(d)
        places = [(x, partner), (other_x, partner), (x, far), (other_x, far)]
        for place, (xs, bs) in enumerate(places):
            arrive(area(xs, bs, s), core_sems.at[kind, d, place], core_peer)
    for going in started:
        going.wait_send()


def collect(hidden_rows, gain, key_weight, value_weight, positions, basis, heads, tokens):
    depth = hidden_rows.shape[1]
    local = positions.shape[0]
    half, width = key_weight.shape[1], key_weight.shape[1] + value_weight.shape[1]
    half_width = HEAD_DIM // 2
    chunks = 4
    frequency = jnp.exp(
        jnp.arange(half_width, dtype=jnp.float32) * (-math.log(ROTARY_BASE) / half_width)
    )
    angles = positions.astype(jnp.float32)[:, None] * frequency[None, :]
    cosine, sine = jnp.cos(angles), jnp.sin(angles)
    dma = pltpu.SemaphoreType.DMA
    anywhere = pl.BlockSpec(memory_space=pltpu.HBM)
    inside = pl.BlockSpec(memory_space=pltpu.VMEM)
    return pl.pallas_call(
        functools.partial(collect_kernel, heads),
        out_shape=(
            jax.ShapeDtypeStruct((tokens, heads * width), jnp.bfloat16),
            jax.ShapeDtypeStruct((heads * width, basis.shape[1]), jnp.float32),
        ),
        in_specs=[anywhere] * 4 + [inside] * 2 + [anywhere],
        out_specs=(inside,) * 2,
        scratch_shapes=[
            pltpu.VMEM(hidden_rows.shape, jnp.bfloat16),
            pltpu.VMEM((1, depth), jnp.float32),
            pltpu.VMEM(key_weight.shape, jnp.bfloat16),
            pltpu.VMEM(value_weight.shape, jnp.bfloat16),
            pltpu.VMEM((local, width), jnp.float32),
            pltpu.VMEM((local, width), jnp.float32),
            pltpu.VMEM((SUBLANES, local), jnp.float32),
            pltpu.VMEM((SUBLANES, local), jnp.float32),
            dma((2, chunks)),
            dma((3, chunks)),
            dma((3, 2)),
            dma((2, heads, 2)),
            dma((2, heads, 2)),
            dma((2, heads, 2)),
            dma((2, heads, 2)),
            dma((2, heads, 2)),
            dma((2, heads, 4, 2)),
        ],
        compiler_params=pltpu.CompilerParams(
            collective_id=0, has_side_effects=True, vmem_limit_bytes=45 * 2**20
        ),
    )(
        hidden_rows,
        gain[None, :],
        key_weight,
        value_weight,
        jnp.concatenate([cosine, cosine], axis=1),
        jnp.concatenate([-sine, sine], axis=1),
        basis,
    )


def body(hidden, gain, key_weight, value_weight, positions, initial_basis):
    hidden_rows = hidden[0]
    local_tokens = positions.shape[1]
    seqs, batches, heads = lax.axis_size("seq"), lax.axis_size("batch"), lax.axis_size("head")
    tokens = local_tokens * seqs * batches
    if seqs == 2 and batches == 4 and tokens <= initial_basis.shape[0] * heads:
        return iterate(
            *collect(
                hidden_rows,
                gain,
                key_weight,
                value_weight,
                positions[0],
                initial_basis,
                heads,
                tokens,
            )
        )
    widened = hidden_rows.astype(jnp.float32)
    scaled = (widened * gain).astype(jnp.bfloat16)
    local_squares = jnp.sum(widened * widened, axis=1)
    key_columns = key_weight.shape[1]
    weights = jnp.concatenate([key_weight, value_weight], axis=1)
    own_squares = total_squares(local_squares, local_tokens)
    projected = lax.psum_scatter(
        jnp.dot(scaled, weights, preferred_element_type=jnp.float32),
        "seq",
        scatter_dimension=0,
        tiled=True,
    )
    inverse_scale = lax.rsqrt(own_squares / D + EPSILON)
    projected = projected * inverse_scale[:, None]
    key_rows = rotary(projected[:, :key_columns].reshape(local_tokens, -1, HEAD_DIM), positions[0])
    value_rows = projected[:, key_columns:].reshape(local_tokens, -1, HEAD_DIM)
    joint_rows = (
        jnp.stack([key_rows, value_rows], axis=2).reshape(local_tokens, -1).astype(jnp.bfloat16)
    )
    partial_value = lax.dot_general(
        joint_rows,
        lax.all_gather(joint_rows, "head", axis=1, tiled=True),
        (((0,), (0,)), ((), ())),
        preferred_element_type=jnp.float32,
    )
    token_total = local_tokens * lax.axis_size("seq") * lax.axis_size("batch")
    basis_block = initial_basis
    covariance = lax.psum(partial_value, ("seq", "batch")) / token_total
    for iteration in range(ITERS):
        whole_basis = whole_of(basis_block)
        images = jnp.dot(
            covariance,
            whole_basis,
            precision=lax.Precision.HIGHEST,
            preferred_element_type=jnp.float32,
        )
        gram_matrix = lax.psum(gram_of(images), "head") / whole_basis.shape[0]
        basis_block = orthonormal(images, gram_matrix)
    return basis_block


def solution(mesh):
    return jax.shard_map(
        body,
        mesh=mesh,
        in_specs=(
            P("batch", None, "seq"),
            P("seq"),
            P("seq", "head"),
            P("seq", "head"),
            P("batch", "seq"),
            P("head", None),
        ),
        out_specs=P("head", None),
        check_vma=False,
    )
```

```python
import functools
import math

import jax
import jax.numpy as jnp
from jax import lax
from jax.experimental import pallas as pl
from jax.experimental.pallas import tpu as pltpu
from jax.sharding import PartitionSpec as P

D = 16384
HEAD_DIM = 128
ITERS = 4


EPSILON = 1e-05
ROTARY_BASE = 500000.0


def rotary(head_rows, position_row):
    half_width = head_rows.shape[-1] // 2
    index_row = jnp.arange(half_width, dtype=jnp.float32)
    frequency = jnp.exp(index_row * (-math.log(ROTARY_BASE) / half_width))
    angles = position_row.astype(jnp.float32)[:, None] * frequency[None, :]
    cosine = jnp.cos(angles)[:, None, :]
    sine_part = jnp.sin(angles)[:, None, :]
    first_half = head_rows[..., :half_width]
    second_half = head_rows[..., half_width:]
    return jnp.concatenate(
        [
            first_half * cosine - second_half * sine_part,
            second_half * cosine + first_half * sine_part,
        ],
        axis=-1,
    )


def whole_of(basis_block):
    return lax.all_gather(basis_block, "head", axis=0, tiled=True)


def total_squares(local_squares, local_tokens):
    all_squares = lax.psum(local_squares, "seq")
    return lax.dynamic_slice_in_dim(all_squares, lax.axis_index("seq") * local_tokens, local_tokens)


def gram_of(images):
    return lax.dot_general(
        images,
        images,
        (((0,), (0,)), ((), ())),
        precision=lax.Precision.HIGHEST,
        preferred_element_type=jnp.float32,
    )


def orthonormal(images, gram_matrix):
    factor = jnp.linalg.cholesky(gram_matrix)
    return lax.linalg.triangular_solve(
        factor, images, left_side=False, lower=True, transpose_a=True
    )


LANES = 128
SUBLANES = 8


def dot_of(left, right, left_axis, right_axis, precision=None):
    return lax.dot_general(
        left,
        right,
        (((left_axis,), (right_axis,)), ((), ())),
        precision=precision,
        preferred_element_type=jnp.float32,
    )


def exact(left, right, left_axis, right_axis):
    return dot_of(left, right, left_axis, right_axis, lax.Precision.HIGHEST)


def halves_of(value):
    high = value.astype(jnp.bfloat16)
    return high, (value - high.astype(jnp.float32)).astype(jnp.bfloat16)


def thrice(left, right, left_axis, right_axis):
    left_high, left_low = halves_of(left)
    right_high, right_low = halves_of(right)
    return (
        dot_of(left_high, right_high, left_axis, right_axis)
        + dot_of(left_high, right_low, left_axis, right_axis)
        + dot_of(left_low, right_high, left_axis, right_axis)
    )


def inverse_factor(matrix):
    size = matrix.shape[0]
    shape = (SUBLANES, size)
    rows = lax.broadcasted_iota(jnp.int32, shape, 0)
    lanes = lax.broadcasted_iota(jnp.int32, shape, 1)
    groups = size // SUBLANES
    tiles = [matrix[SUBLANES * g : SUBLANES * (g + 1)] for g in range(groups)]
    out = []

    def row_of(value, at):
        return jnp.broadcast_to(value[at : at + 1, :], shape)

    def lane_of(value, at):
        return jnp.broadcast_to(value[:, at : at + 1], shape)

    def total(terms):
        terms = list(terms)
        while len(terms) > 1:
            terms = [terms[i] + terms[i + 1] if i + 1 < len(terms) else terms[i] for i in range(0, len(terms), 2)]
        return terms[0]

    block = [lane_of(tiles[0], j) for j in range(SUBLANES)]
    for own in range(groups):
        pivot = own * SUBLANES
        last_group = own + 1 == groups
        if not last_group:
            below = [lane_of(tiles[own + 1], pivot + j) for j in range(SUBLANES)]
            after = [lane_of(tiles[own + 1], pivot + SUBLANES + j) for j in range(SUBLANES)]
        factor = [None] * SUBLANES
        turned, weighted = [], []
        for k in range(0, SUBLANES, 2):
            one, two = block[k], block[k + 1]
            first, cross, last = row_of(one, k), row_of(two, k), row_of(two, k + 1)
            scale = 1.0 / (first * last - cross * cross)
            top = (one * last - two * cross) * scale
            low = (two * first - one * cross) * scale
            top_row, low_row = first * scale, last * scale
            mixed = cross * scale
            here, next_ = rows == k, rows == k + 1
            pair = here | next_
            top = jnp.where(here, -low_row, jnp.where(next_, mixed, top))
            low = jnp.where(here, mixed, jnp.where(next_, -top_row, low))
            heads = {}
            for j in range(SUBLANES):
                if j in (k, k + 1):
                    continue
                x, y = row_of(block[j], k), row_of(block[j], k + 1)
                heads[j] = (x, y)
                block[j] = jnp.where(pair, 0.0, block[j]) - (top * x + low * y)
            block[k], block[k + 1] = -top, -low
            ratio = cross / first
            top_scale, low_scale = lax.rsqrt(first), lax.rsqrt(last - ratio * cross)
            for j in range(k):
                x, y = heads[j]
                base = factor[j]
                factor[j] = jnp.where(here, x * top_scale, jnp.where(next_, (y - ratio * x) * low_scale, base))
            factor[k] = jnp.where(here, top_scale, jnp.where(next_, -ratio * low_scale, 0.0))
            factor[k + 1] = jnp.where(next_, low_scale, 0.0)
            if not last_group:
                t1 = total([below[k]] + [heads[j][0] * below[j] for j in range(k)])
                t2 = total([below[k + 1]] + [heads[j][1] * below[j] for j in range(k)])
                turned += [t1, t2]
                weighted += [(t1 * last - t2 * cross) * scale, (t2 * first - t1 * cross) * scale]
        inside = (lanes >= pivot) & (lanes < pivot + SUBLANES)
        held = jnp.where(inside, jnp.where(lanes == rows + pivot, 1.0, 0.0), tiles[own])
        spread = [row_of(held, j) for j in range(SUBLANES)]
        result = total([factor[j] * spread[j] for j in range(SUBLANES)])
        out.append(jnp.where(lanes < pivot + SUBLANES, result, 0.0))
        if last_group:
            break
        mixed = total([block[j] * spread[j] for j in range(SUBLANES)])
        mixes = [row_of(mixed, j) for j in range(SUBLANES)]
        following = [
            after[j] - total([turned[m] * row_of(weighted[m], j) for m in range(SUBLANES)])
            for j in range(SUBLANES)
        ]
        columns = [
            [below[j]] + [lane_of(tiles[g], pivot + j) for g in range(own + 2, groups)]
            for j in range(SUBLANES)
        ]
        for g in range(own + 1, groups):
            changes = [columns[j][g - own - 1] * mixes[j] for j in range(SUBLANES)]
            tiles[g] = jnp.where(inside, 0.0, tiles[g]) - total(changes)
        block = following
    return jnp.concatenate(out, axis=0)


def iterate_kernel(high_ref, low_ref, start_ref, own_ref, out_ref, rows_ref, gram_ref, joint):
    tokens, rank = start_ref.shape
    panels = rank // LANES
    rows_ref[...] = start_ref[...]

    def step(iteration, carry):
        rows_high, rows_low = halves_of(rows_ref[...])
        images = (
            dot_of(high_ref[...], rows_high, 1, 0)
            + dot_of(high_ref[...], rows_low, 1, 0)
            + dot_of(low_ref[...], rows_high, 1, 0)
        )
        images_high, images_low = halves_of(images)
        gram_ref[...] = (
            dot_of(rows_high, images_high, 0, 0)
            + dot_of(rows_high, images_low, 0, 0)
            + dot_of(rows_low, images_high, 0, 0)
        ) * (1.0 / (tokens * joint))

        @pl.when(iteration < ITERS - 1)
        def _():
            rows_ref[...] = images

        for panel in range(panels):
            start, end = panel * LANES, (panel + 1) * LANES
            inverse = inverse_factor(gram_ref[start:end, start:end])
            columns = thrice(rows_ref[:, start:end], inverse, 1, 1)
            rows_ref[:, start:end] = columns
            if end < rank:
                scaled = exact(inverse, gram_ref[start:end, end:], 1, 0)
                gram_ref[end:, end:] -= exact(scaled, scaled, 0, 0)
                rows_ref[:, end:] -= thrice(columns, scaled, 1, 0)
        return carry

    lax.fori_loop(0, ITERS, step, 0)
    rows_high, rows_low = halves_of(rows_ref[...])
    own = own_ref[...]
    out_ref[...] = (dot_of(own, rows_high, 0, 0) + dot_of(own, rows_low, 0, 0)) * (1.0 / tokens)


def iterate(high, low, start, own, joint):
    tokens, rank = start.shape

    def kernel(*refs):
        iterate_kernel(*refs, joint)

    return pl.pallas_call(
        kernel,
        out_shape=jax.ShapeDtypeStruct((own.shape[1], rank), jnp.float32),
        in_specs=[pl.BlockSpec(memory_space=pltpu.VMEM)] * 4,
        out_specs=pl.BlockSpec(memory_space=pltpu.VMEM),
        scratch_shapes=[
            pltpu.VMEM((tokens, rank), jnp.float32),
            pltpu.VMEM((rank, rank), jnp.float32),
        ],
        compiler_params=pltpu.CompilerParams(vmem_limit_bytes=40 * 2**20),
    )(high, low, start, own)


def collect_kernel(
    heads,
    hidden_ref,
    gain_ref,
    key_ref,
    value_ref,
    cosine_ref,
    sine_ref,
    basis_ref,
    high_ref,
    low_ref,
    rows_ref,
    own_ref,
    out_ref,
    whole_ref,
    token_sums,
    hidden_rows,
    gain_row,
    key_rows,
    value_rows,
    partial,
    peer_partial,
    squares,
    peer_squares,
    load_sems,
    half_sems,
    swap_sems,
    z_sems,
    x_sems,
    y_sems,
    x_half_sems,
    y_half_sems,
    core_sems,
):
    x, b, z = lax.axis_index("seq"), lax.axis_index("batch"), lax.axis_index("head")
    local, width = peer_partial.shape
    half = width // 2
    rank = whole_ref.shape[1]
    piece = width // 8
    depth = gain_row.shape[1]
    chunks = load_sems.shape[1]
    chunk = depth // chunks
    other_x, other_y = 1 - x, (b + 2) % 4
    partner = b + 1 - 2 * (b % 2)
    x_peer, y_peer, core_peer = (other_x, b, z), (x, other_y, z), (x, partner, z)
    away = pl.ds(pl.multiple_of(other_x * local, local), local)
    mine = pl.ds(pl.multiple_of(x * local, local), local)

    def nearest(turn):
        if turn == 0 or heads != 4:
            return (z + turn) % heads
        side = z // 2
        inner = z + side * (3 - 2 * z)
        place = (1 + inner, 2 - 2 * inner, 3)[turn - 1]
        return 3 * side + (1 - 2 * side) * place

    sources = [nearest(turn) for turn in range(heads)]

    def z_peer(turn):
        return (x, b, sources[turn])

    own_block = whole_ref.at[pl.ds(pl.multiple_of(z * width, width), width), :]
    basis_load = pltpu.make_async_copy(basis_ref, own_block, half_sems.at[2, 0])
    gain_load = pltpu.make_async_copy(gain_ref, gain_row, half_sems.at[2, 1])

    def span(c):
        return pl.ds(c * chunk, chunk)

    def token_load(kind, area, c):
        return pltpu.make_async_copy(
            hidden_ref.at[area, span(c)], hidden_rows.at[area, span(c)], half_sems.at[kind, c]
        )

    away_loads = [token_load(0, away, c) for c in range(chunks)]
    mine_loads = [token_load(1, mine, c) for c in range(chunks)]
    key_loads = [
        pltpu.make_async_copy(key_ref.at[span(c), :], key_rows.at[span(c), :], load_sems.at[0, c])
        for c in range(chunks)
    ]
    value_loads = [
        pltpu.make_async_copy(
            value_ref.at[span(c), :], value_rows.at[span(c), :], load_sems.at[1, c]
        )
        for c in range(chunks)
    ]
    basis_load.start()
    gain_load.start()
    for c in range(chunks):
        away_loads[c].start()
        key_loads[c].start()
    for load in value_loads + mine_loads:
        load.start()

    barrier = pltpu.get_barrier_semaphore()
    peers = [x_peer, y_peer, core_peer] + [z_peer(d) for d in range(1, heads)]
    for peer in peers:
        pl.semaphore_signal(barrier, inc=1, device_id=peer, device_id_type=pl.DeviceIdType.MESH)
    pl.semaphore_wait(barrier, len(peers))

    def copy(source, target, sems, peer):
        return pltpu.make_async_remote_copy(
            src_ref=source,
            dst_ref=target,
            send_sem=sems.at[0],
            recv_sem=sems.at[1],
            device_id=peer,
            device_id_type=pl.DeviceIdType.MESH,
        )

    def region(xs, bs, zs, start=0, size=width):
        row = pl.multiple_of((xs * 4 + bs) * local, local)
        column = pl.multiple_of(zs * width + start, half)
        return out_ref.at[pl.ds(row, local), pl.ds(column, size)]

    def piece_of(xs, bs, zs, start=0, size=rank):
        row = pl.multiple_of(zs * width + (xs * 4 + bs) * piece, piece)
        return whole_ref.at[pl.ds(row, piece), pl.ds(start, size)]

    started = []

    def send(area, sems, peer):
        going = copy(area, area, sems, peer)
        going.start()
        started.append(going)

    def arrive(area, sems, peer):
        copy(area, area, sems, peer).wait_recv()

    def send_z(area, kind, turn):
        going = pltpu.make_async_remote_copy(
            src_ref=area,
            dst_ref=area,
            send_sem=z_sems.at[kind, sources[turn], 0],
            recv_sem=z_sems.at[kind, z, 1],
            device_id=z_peer(turn),
            device_id_type=pl.DeviceIdType.MESH,
        )
        going.start()
        started.append(going)

    def spread(kind, area, middle, turn):
        s = sources[turn]
        own = area(x, b, s)
        if turn:
            arrive(own, z_sems.at[kind, s], z_peer(turn))
        send(own, x_sems.at[kind, turn], x_peer)
        send(own, y_sems.at[kind, turn], y_peer)
        send(own, core_sems.at[kind, turn, 0], core_peer)

    def relay(kind, area, middle, turn):
        s = sources[turn]
        arrive(area(other_x, b, s), x_sems.at[kind, turn], x_peer)
        beyond = area(other_x, b, s, middle, middle) if middle else area(other_x, b, s)
        send(beyond, y_half_sems.at[kind, turn], y_peer)
        send(area(other_x, b, s), core_sems.at[kind, turn, 1], core_peer)
        arrive(area(x, other_y, s), y_sems.at[kind, turn], y_peer)
        if middle:
            send(area(x, other_y, s, 0, middle), x_half_sems.at[kind, turn], x_peer)
        send(area(x, other_y, s), core_sems.at[kind, turn, 2], core_peer)

    def finish(kind, area, middle, turn):
        s = sources[turn]
        if middle:
            arrive(area(other_x, other_y, s, 0, middle), x_half_sems.at[kind, turn], x_peer)
        beyond = area(other_x, other_y, s, middle, middle) if middle else area(other_x, other_y, s)
        arrive(beyond, y_half_sems.at[kind, turn], y_peer)
        send(area(other_x, other_y, s), core_sems.at[kind, turn, 3], core_peer)

    far = (partner + 2) % 4

    def gathered(kind, area, middle, turn):
        places = [(x, partner), (other_x, partner), (x, far), (other_x, far)]
        for place, (xs, bs) in enumerate(places):
            arrive(area(xs, bs, sources[turn]), core_sems.at[kind, turn, place], core_peer)

    joint = [(0, region, half, turn) for turn in range(heads)]
    pieces = [(1, piece_of, 0, turn) for turn in range(1, heads)]
    tokens, strip = out_ref.shape[0], 256

    def accumulate(turn):
        place = pl.multiple_of(sources[turn] * width, width)
        block = out_ref[:, pl.ds(place, width)]
        basis_high, basis_low = halves_of(whole_ref[pl.ds(place, width), :])
        for start in range(0, tokens, strip):
            area = slice(start, start + strip)
            part = out_ref[area, pl.ds(place, width)]
            product = dot_of(part, block, 1, 1)
            rows = dot_of(part, basis_high, 1, 0) + dot_of(part, basis_low, 1, 0)
            if turn:
                product = product + token_sums[area, :]
                rows = rows + rows_ref[area, :]
            rows_ref[area, :] = rows
            if turn < heads - 1:
                token_sums[area, :] = product
            else:
                high, low = halves_of(product * (1.0 / tokens))
                high_ref[area, :] = high
                low_ref[area, :] = low
            if turn == 0:
                own_ref[area, :] = part

    basis_load.wait()
    for turn in range(1, heads):
        send_z(piece_of(x, b, z), 1, turn)

    def prepare(area, c, total):
        widened = hidden_rows[area, span(c)].astype(jnp.float32)
        scaled = (widened * gain_row[:, span(c)]).astype(jnp.bfloat16)
        hidden_rows[area, span(c)] = scaled
        squared = widened * widened
        for start in range(0, chunk, LANES):
            total = total + squared[:, start : start + LANES]
        return scaled, total

    def across(total):
        ones = jnp.ones((SUBLANES, LANES), jnp.float32)
        return exact(ones, total, 1, 1)

    def swap(source_ref, target_ref, index):
        going = copy(source_ref, target_ref, swap_sems.at[index], x_peer)
        going.start()
        return going

    gain_load.wait()
    away_total = jnp.zeros((local, LANES), jnp.float32)
    sums = jnp.zeros((local, half), jnp.float32)
    for c in range(chunks):
        away_loads[c].wait()
        scaled, away_total = prepare(away, c, away_total)
        key_loads[c].wait()
        sums = sums + dot_of(scaled, key_rows[span(c), :], 1, 0)
    partial[:, :half] = sums
    squares[...] = across(away_total)
    swaps = [
        swap(squares, peer_squares, 0),
        swap(partial.at[:, pl.ds(0, half)], peer_partial.at[:, pl.ds(0, half)], 1),
    ]
    for item in pieces:
        spread(*item)
    sums = jnp.zeros((local, half), jnp.float32)
    for c in range(chunks):
        value_loads[c].wait()
        sums = sums + dot_of(hidden_rows[away, span(c)], value_rows[span(c), :], 1, 0)
    partial[:, half:] = sums
    swaps.append(swap(partial.at[:, pl.ds(half, half)], peer_partial.at[:, pl.ds(half, half)], 2))
    for item in pieces:
        relay(*item)
    mine_total = jnp.zeros((local, LANES), jnp.float32)
    key_sums = jnp.zeros((local, half), jnp.float32)
    value_sums = jnp.zeros((local, half), jnp.float32)
    for c in range(chunks):
        mine_loads[c].wait()
        scaled, mine_total = prepare(mine, c, mine_total)
        key_sums = key_sums + dot_of(scaled, key_rows[span(c), :], 1, 0)
        value_sums = value_sums + dot_of(scaled, value_rows[span(c), :], 1, 0)
    own_squares = across(mine_total)
    for item in pieces:
        finish(*item)

    swaps[0].wait()
    eighths = jnp.full((SUBLANES, LANES), 1.0 / SUBLANES, jnp.float32)
    inverse_scale = lax.rsqrt(exact(own_squares + peer_squares[...], eighths, 0, 0) / D + EPSILON)
    row = pl.multiple_of((x * 4 + b) * local, local)
    swaps[1].wait()
    for g in range(half // HEAD_DIM):
        spot = slice(g * HEAD_DIM, (g + 1) * HEAD_DIM)
        key = (key_sums[:, spot] + peer_partial[:, spot]) * inverse_scale
        turned = key * cosine_ref[...] + pltpu.roll(key, HEAD_DIM // 2, 1) * sine_ref[...]
        column = pl.multiple_of(z * width + 2 * g * HEAD_DIM, HEAD_DIM)
        out_ref[pl.ds(row, local), pl.ds(column, HEAD_DIM)] = turned.astype(jnp.bfloat16)
    swaps[2].wait()
    for g in range(half // HEAD_DIM):
        spot = slice(g * HEAD_DIM, (g + 1) * HEAD_DIM)
        there = slice(half + g * HEAD_DIM, half + (g + 1) * HEAD_DIM)
        value = (value_sums[:, spot] + peer_partial[:, there]) * inverse_scale
        column = pl.multiple_of(z * width + (2 * g + 1) * HEAD_DIM, HEAD_DIM)
        out_ref[pl.ds(row, local), pl.ds(column, HEAD_DIM)] = value.astype(jnp.bfloat16)

    for turn in range(1, heads):
        send_z(region(x, b, z), 0, turn)
    for turn in range(len(joint) + 3):
        if turn < len(joint):
            spread(*joint[turn])
        if 1 <= turn < len(joint) + 1:
            relay(*joint[turn - 1])
        if 2 <= turn < len(joint) + 2:
            finish(*joint[turn - 2])
        if turn == 2:
            for item in pieces:
                gathered(*item)
        if turn >= 3:
            gathered(*joint[turn - 3])
            accumulate(turn - 3)
    for going in started:
        going.wait_send()


def collect(hidden_rows, gain, key_weight, value_weight, positions, basis, heads, tokens):
    depth = hidden_rows.shape[1]
    local = positions.shape[0]
    half, width = key_weight.shape[1], key_weight.shape[1] + value_weight.shape[1]
    half_width = HEAD_DIM // 2
    chunks = 4
    frequency = jnp.exp(
        jnp.arange(half_width, dtype=jnp.float32) * (-math.log(ROTARY_BASE) / half_width)
    )
    angles = positions.astype(jnp.float32)[:, None] * frequency[None, :]
    cosine, sine = jnp.cos(angles), jnp.sin(angles)
    dma = pltpu.SemaphoreType.DMA
    anywhere = pl.BlockSpec(memory_space=pltpu.HBM)
    inside = pl.BlockSpec(memory_space=pltpu.VMEM)
    return pl.pallas_call(
        functools.partial(collect_kernel, heads),
        out_shape=(
            jax.ShapeDtypeStruct((tokens, tokens), jnp.bfloat16),
            jax.ShapeDtypeStruct((tokens, tokens), jnp.bfloat16),
            jax.ShapeDtypeStruct((tokens, basis.shape[1]), jnp.float32),
            jax.ShapeDtypeStruct((tokens, width), jnp.bfloat16),
        ),
        in_specs=[anywhere] * 4 + [inside] * 2 + [anywhere],
        out_specs=(inside,) * 4,
        scratch_shapes=[
            pltpu.VMEM((tokens, heads * width), jnp.bfloat16),
            pltpu.VMEM((heads * width, basis.shape[1]), jnp.float32),
            pltpu.VMEM((tokens, tokens), jnp.float32),
            pltpu.VMEM(hidden_rows.shape, jnp.bfloat16),
            pltpu.VMEM((1, depth), jnp.float32),
            pltpu.VMEM(key_weight.shape, jnp.bfloat16),
            pltpu.VMEM(value_weight.shape, jnp.bfloat16),
            pltpu.VMEM((local, width), jnp.float32),
            pltpu.VMEM((local, width), jnp.float32),
            pltpu.VMEM((SUBLANES, local), jnp.float32),
            pltpu.VMEM((SUBLANES, local), jnp.float32),
            dma((2, chunks)),
            dma((3, chunks)),
            dma((3, 2)),
            dma((2, heads, 2)),
            dma((2, heads, 2)),
            dma((2, heads, 2)),
            dma((2, heads, 2)),
            dma((2, heads, 2)),
            dma((2, heads, 4, 2)),
        ],
        compiler_params=pltpu.CompilerParams(
            collective_id=0, has_side_effects=True, vmem_limit_bytes=45 * 2**20
        ),
    )(
        hidden_rows,
        gain[None, :],
        key_weight,
        value_weight,
        jnp.concatenate([cosine, cosine], axis=1),
        jnp.concatenate([-sine, sine], axis=1),
        basis,
    )


def body(hidden, gain, key_weight, value_weight, positions, initial_basis):
    hidden_rows = hidden[0]
    local_tokens = positions.shape[1]
    seqs, batches, heads = lax.axis_size("seq"), lax.axis_size("batch"), lax.axis_size("head")
    tokens = local_tokens * seqs * batches
    if seqs == 2 and batches == 4 and tokens <= initial_basis.shape[0] * heads:
        collected = collect(
            hidden_rows,
            gain,
            key_weight,
            value_weight,
            positions[0],
            initial_basis,
            heads,
            tokens,
        )
        return iterate(*collected, initial_basis.shape[0] * heads)
    widened = hidden_rows.astype(jnp.float32)
    scaled = (widened * gain).astype(jnp.bfloat16)
    local_squares = jnp.sum(widened * widened, axis=1)
    key_columns = key_weight.shape[1]
    weights = jnp.concatenate([key_weight, value_weight], axis=1)
    own_squares = total_squares(local_squares, local_tokens)
    projected = lax.psum_scatter(
        jnp.dot(scaled, weights, preferred_element_type=jnp.float32),
        "seq",
        scatter_dimension=0,
        tiled=True,
    )
    inverse_scale = lax.rsqrt(own_squares / D + EPSILON)
    projected = projected * inverse_scale[:, None]
    key_rows = rotary(projected[:, :key_columns].reshape(local_tokens, -1, HEAD_DIM), positions[0])
    value_rows = projected[:, key_columns:].reshape(local_tokens, -1, HEAD_DIM)
    joint_rows = (
        jnp.stack([key_rows, value_rows], axis=2).reshape(local_tokens, -1).astype(jnp.bfloat16)
    )
    partial_value = lax.dot_general(
        joint_rows,
        lax.all_gather(joint_rows, "head", axis=1, tiled=True),
        (((0,), (0,)), ((), ())),
        preferred_element_type=jnp.float32,
    )
    token_total = local_tokens * lax.axis_size("seq") * lax.axis_size("batch")
    basis_block = initial_basis
    covariance = lax.psum(partial_value, ("seq", "batch")) / token_total
    for iteration in range(ITERS):
        whole_basis = whole_of(basis_block)
        images = jnp.dot(
            covariance,
            whole_basis,
            precision=lax.Precision.HIGHEST,
            preferred_element_type=jnp.float32,
        )
        gram_matrix = lax.psum(gram_of(images), "head") / whole_basis.shape[0]
        basis_block = orthonormal(images, gram_matrix)
    return basis_block


def solution(mesh):
    return jax.shard_map(
        body,
        mesh=mesh,
        in_specs=(
            P("batch", None, "seq"),
            P("seq"),
            P("seq", "head"),
            P("seq", "head"),
            P("batch", "seq"),
            P("head", None),
        ),
        out_specs=P("head", None),
        check_vma=False,
    )
```

```python
import functools
import math

import jax
import jax.numpy as jnp
from jax import lax
from jax.experimental import pallas as pl
from jax.experimental.pallas import tpu as pltpu
from jax.sharding import PartitionSpec as P

D = 16384
HEAD_DIM = 128
ITERS = 4


EPSILON = 1e-05
ROTARY_BASE = 500000.0


def rotary(head_rows, position_row):
    half_width = head_rows.shape[-1] // 2
    index_row = jnp.arange(half_width, dtype=jnp.float32)
    frequency = jnp.exp(index_row * (-math.log(ROTARY_BASE) / half_width))
    angles = position_row.astype(jnp.float32)[:, None] * frequency[None, :]
    cosine = jnp.cos(angles)[:, None, :]
    sine_part = jnp.sin(angles)[:, None, :]
    first_half = head_rows[..., :half_width]
    second_half = head_rows[..., half_width:]
    return jnp.concatenate(
        [
            first_half * cosine - second_half * sine_part,
            second_half * cosine + first_half * sine_part,
        ],
        axis=-1,
    )


def whole_of(basis_block):
    return lax.all_gather(basis_block, "head", axis=0, tiled=True)


def total_squares(local_squares, local_tokens):
    all_squares = lax.psum(local_squares, "seq")
    return lax.dynamic_slice_in_dim(all_squares, lax.axis_index("seq") * local_tokens, local_tokens)


def gram_of(images):
    return lax.dot_general(
        images,
        images,
        (((0,), (0,)), ((), ())),
        precision=lax.Precision.HIGHEST,
        preferred_element_type=jnp.float32,
    )


def orthonormal(images, gram_matrix):
    factor = jnp.linalg.cholesky(gram_matrix)
    return lax.linalg.triangular_solve(
        factor, images, left_side=False, lower=True, transpose_a=True
    )


LANES = 128
SUBLANES = 8
AHEAD = True


def dot_of(left, right, left_axis, right_axis, precision=None):
    return lax.dot_general(
        left,
        right,
        (((left_axis,), (right_axis,)), ((), ())),
        precision=precision,
        preferred_element_type=jnp.float32,
    )


def exact(left, right, left_axis, right_axis):
    return dot_of(left, right, left_axis, right_axis, lax.Precision.HIGHEST)


def halves_of(value):
    high = value.astype(jnp.bfloat16)
    return high, (value - high.astype(jnp.float32)).astype(jnp.bfloat16)


def thrice(left, right, left_axis, right_axis):
    left_high, left_low = halves_of(left)
    right_high, right_low = halves_of(right)
    return (
        dot_of(left_high, right_high, left_axis, right_axis)
        + dot_of(left_high, right_low, left_axis, right_axis)
        + dot_of(left_low, right_high, left_axis, right_axis)
    )


def inverse_factor(matrix):
    size = matrix.shape[0]
    shape = (SUBLANES, size)
    rows = lax.broadcasted_iota(jnp.int32, shape, 0)
    lanes = lax.broadcasted_iota(jnp.int32, shape, 1)
    groups = size // SUBLANES
    tiles = [matrix[SUBLANES * g : SUBLANES * (g + 1)] for g in range(groups)]
    out = []

    def row_of(value, at):
        return jnp.broadcast_to(value[at : at + 1, :], shape)

    def lane_of(value, at):
        return jnp.broadcast_to(value[:, at : at + 1], shape)

    def total(terms):
        while len(terms) > 1:
            pairs = [terms[i] + terms[i + 1] for i in range(0, len(terms) - 1, 2)]
            terms = pairs + terms[2 * len(pairs) :]
        return terms[0]

    zero = jnp.zeros(shape, jnp.float32)
    for own in range(groups):
        pivot = own * SUBLANES
        block = [lane_of(tiles[own], pivot + j) for j in range(SUBLANES)]
        if AHEAD and own:
            block = following
        last_group = own + 1 == groups
        if not last_group:
            below = [lane_of(tiles[own + 1], pivot + j) for j in range(SUBLANES)]
            if AHEAD:
                after = [lane_of(tiles[own + 1], pivot + SUBLANES + j) for j in range(SUBLANES)]
        factor = [None] * SUBLANES
        turned, weighted = [], []
        for k in range(0, SUBLANES, 2):
            one, two = block[k], block[k + 1]
            if not AHEAD:
                one, two = one + zero, two + zero
            first, cross, last = row_of(one, k), row_of(two, k), row_of(two, k + 1)
            scale = 1.0 / (first * last - cross * cross)
            mixed = cross * scale
            here, next_ = rows == k, rows == k + 1
            pair = here | next_
            first_scaled, last_scaled = first * scale, last * scale
            top = one * last_scaled - two * mixed
            low = two * first_scaled - one * mixed
            top = jnp.where(here, -last_scaled, jnp.where(next_, mixed, top))
            low = jnp.where(here, mixed, jnp.where(next_, -first_scaled, low))
            heads = {}
            for j in range(SUBLANES):
                if j in (k, k + 1):
                    continue
                x, y = row_of(block[j], k), row_of(block[j], k + 1)
                heads[j] = (x, y)
                block[j] = jnp.where(pair, 0.0, block[j]) - (top * x + low * y)
            block[k], block[k + 1] = -top, -low
            ratio = cross / first
            top_scale, low_scale = lax.rsqrt(first), lax.rsqrt(last - ratio * cross)
            ratio_scale = ratio * low_scale
            for j in range(k):
                x, y = heads[j]
                lower = y * low_scale - x * ratio_scale
                factor[j] = jnp.where(here, x * top_scale, jnp.where(next_, lower, factor[j]))
            factor[k] = jnp.where(here, top_scale, jnp.where(next_, -ratio_scale, 0.0))
            factor[k + 1] = jnp.where(next_, low_scale, 0.0)
            if AHEAD and not last_group:
                t1 = total([below[k]] + [heads[j][0] * below[j] for j in range(k)])
                t2 = total([below[k + 1]] + [heads[j][1] * below[j] for j in range(k)])
                turned += [t1, t2]
                weighted += [t1 * last_scaled - t2 * mixed, t2 * first_scaled - t1 * mixed]
        inside = (lanes >= pivot) & (lanes < pivot + SUBLANES)
        held = jnp.where(inside, jnp.where(lanes == rows + pivot, 1.0, 0.0), tiles[own])
        spread = [row_of(held, j) for j in range(SUBLANES)]
        result = total([factor[j] * spread[j] for j in range(SUBLANES)])
        out.append(jnp.where(lanes < pivot + SUBLANES, result, 0.0))
        if last_group:
            break
        mixed = total([block[j] * spread[j] for j in range(SUBLANES)])
        mixes = [row_of(mixed, j) for j in range(SUBLANES)]
        if AHEAD:
            following = [
                after[j] - total([turned[m] * row_of(weighted[m], j) for m in range(SUBLANES)])
                for j in range(SUBLANES)
            ]
        columns = [
            [below[j]] + [lane_of(tiles[g], pivot + j) for g in range(own + 2, groups)]
            for j in range(SUBLANES)
        ]
        for g in range(own + 1, groups):
            changes = [columns[j][g - own - 1] * mixes[j] for j in range(SUBLANES)]
            tiles[g] = jnp.where(inside, 0.0, tiles[g]) - total(changes)
        yield
    yield jnp.concatenate(out, axis=0)


def factors_of(*matrices):
    running = [inverse_factor(matrix) for matrix in matrices]
    for _ in range(matrices[0].shape[0] // SUBLANES):
        results = [next(each) for each in running]
    return results


def iterate_kernel(
    high_ref, low_ref, start_ref, own_ref, out_ref, rows_ref, images_ref, gram_ref, factor_ref, joint
):
    rank, tokens = start_ref.shape
    scale = 1.0 / (tokens * joint)
    left, right = slice(0, rank // 2), slice(rank // 2, rank)

    def applied(rows):
        rows_high, rows_low = halves_of(rows)
        return (
            dot_of(rows_high, high_ref[...], 1, 0)
            + dot_of(rows_high, low_ref[...], 1, 0)
            + dot_of(rows_low, high_ref[...], 1, 0)
        )

    def gram_block(rows, images):
        return thrice(rows, images, 1, 1) * scale

    def reduced(factor):
        scaled = exact(factor, gram_ref[left, right], 1, 0)
        return scaled, gram_ref[right, right] - exact(scaled, scaled, 0, 0)

    images = applied(start_ref[...])
    images_ref[...] = images
    gram = gram_block(start_ref[...], images)
    gram_ref[...] = gram
    factor_ref[...] = factors_of(gram[left, left])[0]

    def step(iteration, carry):
        factor = factor_ref[...]
        scaled, rest = reduced(factor)
        first = thrice(factor, images_ref[left, :], 1, 0)
        first_images = applied(first)
        rest_factor, next_factor = factors_of(rest, gram_block(first, first_images))
        remaining = images_ref[right, :] - thrice(scaled, first, 0, 0)
        second = thrice(rest_factor, remaining, 1, 0)
        second_images = applied(second)
        rows_ref[left, :] = first
        rows_ref[right, :] = second
        gram_ref[left, right] = gram_block(first, second_images)
        gram_ref[right, right] = gram_block(second, second_images)
        images_ref[left, :] = first_images
        images_ref[right, :] = second_images
        factor_ref[...] = next_factor
        return carry

    lax.fori_loop(0, ITERS - 1, step, 0)
    rows_high, rows_low = halves_of(rows_ref[...])
    own = own_ref[...]
    loose = (dot_of(rows_high, own, 1, 0) + dot_of(rows_low, own, 1, 0)) * (1.0 / tokens)
    factor = factor_ref[...]
    scaled, rest = reduced(factor)
    first = thrice(factor, loose[left, :], 1, 0)
    out_ref[:, left] = thrice(loose[left, :], factor, 0, 1)
    second = loose[right, :] - thrice(scaled, first, 0, 0)
    out_ref[:, right] = thrice(second, factors_of(rest)[0], 0, 1)


def iterate(high, low, start, own, joint):
    rank, tokens = start.shape

    def kernel(*refs):
        iterate_kernel(*refs, joint)

    return pl.pallas_call(
        kernel,
        out_shape=jax.ShapeDtypeStruct((own.shape[1], rank), jnp.float32),
        in_specs=[pl.BlockSpec(memory_space=pltpu.VMEM)] * 4,
        out_specs=pl.BlockSpec(memory_space=pltpu.VMEM),
        scratch_shapes=[
            pltpu.VMEM((rank, tokens), jnp.float32),
            pltpu.VMEM((rank, tokens), jnp.float32),
            pltpu.VMEM((rank, rank), jnp.float32),
            pltpu.VMEM((rank // 2, rank // 2), jnp.float32),
        ],
        compiler_params=pltpu.CompilerParams(vmem_limit_bytes=40 * 2**20),
    )(high, low, start, own)


def collect_kernel(
    heads,
    hidden_ref,
    gain_ref,
    key_ref,
    value_ref,
    cosine_ref,
    sine_ref,
    basis_ref,
    high_ref,
    low_ref,
    rows_ref,
    own_ref,
    out_ref,
    whole_ref,
    token_sums,
    hidden_rows,
    gain_row,
    key_rows,
    value_rows,
    partial,
    peer_partial,
    squares,
    peer_squares,
    load_sems,
    half_sems,
    swap_sems,
    z_sems,
    x_sems,
    y_sems,
    x_half_sems,
    y_half_sems,
    core_sems,
):
    x, b, z = lax.axis_index("seq"), lax.axis_index("batch"), lax.axis_index("head")
    local, width = peer_partial.shape
    half = width // 2
    rank = whole_ref.shape[1]
    piece = width // 8
    depth = gain_row.shape[1]
    chunks = load_sems.shape[1]
    chunk = depth // chunks
    other_x, other_y = 1 - x, (b + 2) % 4
    partner = b + 1 - 2 * (b % 2)
    x_peer, y_peer, core_peer = (other_x, b, z), (x, other_y, z), (x, partner, z)
    away = pl.ds(pl.multiple_of(other_x * local, local), local)
    mine = pl.ds(pl.multiple_of(x * local, local), local)

    def nearest(turn):
        if turn == 0 or heads != 4:
            return (z + turn) % heads
        side = z // 2
        inner = z + side * (3 - 2 * z)
        place = (1 + inner, 2 - 2 * inner, 3)[turn - 1]
        return 3 * side + (1 - 2 * side) * place

    sources = [nearest(turn) for turn in range(heads)]

    def z_peer(turn):
        return (x, b, sources[turn])

    own_block = whole_ref.at[pl.ds(pl.multiple_of(z * width, width), width), :]
    basis_load = pltpu.make_async_copy(basis_ref, own_block, half_sems.at[2, 0])
    gain_load = pltpu.make_async_copy(gain_ref, gain_row, half_sems.at[2, 1])

    def span(c):
        return pl.ds(c * chunk, chunk)

    def token_load(kind, area, c):
        return pltpu.make_async_copy(
            hidden_ref.at[area, span(c)], hidden_rows.at[area, span(c)], half_sems.at[kind, c]
        )

    away_loads = [token_load(0, away, c) for c in range(chunks)]
    mine_loads = [token_load(1, mine, c) for c in range(chunks)]
    key_loads = [
        pltpu.make_async_copy(key_ref.at[span(c), :], key_rows.at[span(c), :], load_sems.at[0, c])
        for c in range(chunks)
    ]
    value_loads = [
        pltpu.make_async_copy(
            value_ref.at[span(c), :], value_rows.at[span(c), :], load_sems.at[1, c]
        )
        for c in range(chunks)
    ]
    basis_load.start()
    gain_load.start()
    for c in range(chunks):
        away_loads[c].start()
        key_loads[c].start()
    for load in value_loads + mine_loads:
        load.start()

    barrier = pltpu.get_barrier_semaphore()
    peers = [x_peer, y_peer, core_peer] + [z_peer(d) for d in range(1, heads)]
    for peer in peers:
        pl.semaphore_signal(barrier, inc=1, device_id=peer, device_id_type=pl.DeviceIdType.MESH)
    pl.semaphore_wait(barrier, len(peers))

    def copy(source, target, sems, peer):
        return pltpu.make_async_remote_copy(
            src_ref=source,
            dst_ref=target,
            send_sem=sems.at[0],
            recv_sem=sems.at[1],
            device_id=peer,
            device_id_type=pl.DeviceIdType.MESH,
        )

    def region(xs, bs, zs, start=0, size=width):
        row = pl.multiple_of((xs * 4 + bs) * local, local)
        column = pl.multiple_of(zs * width + start, half)
        return out_ref.at[pl.ds(row, local), pl.ds(column, size)]

    def piece_of(xs, bs, zs, start=0, size=rank):
        row = pl.multiple_of(zs * width + (xs * 4 + bs) * piece, piece)
        return whole_ref.at[pl.ds(row, piece), pl.ds(start, size)]

    started = []

    def send(area, sems, peer):
        going = copy(area, area, sems, peer)
        going.start()
        started.append(going)

    def arrive(area, sems, peer):
        copy(area, area, sems, peer).wait_recv()

    def send_z(area, kind, turn):
        going = pltpu.make_async_remote_copy(
            src_ref=area,
            dst_ref=area,
            send_sem=z_sems.at[kind, sources[turn], 0],
            recv_sem=z_sems.at[kind, z, 1],
            device_id=z_peer(turn),
            device_id_type=pl.DeviceIdType.MESH,
        )
        going.start()
        started.append(going)

    def spread(kind, area, middle, turn):
        s = sources[turn]
        own = area(x, b, s)
        if turn:
            arrive(own, z_sems.at[kind, s], z_peer(turn))
        send(own, x_sems.at[kind, turn], x_peer)
        send(own, y_sems.at[kind, turn], y_peer)
        send(own, core_sems.at[kind, turn, 0], core_peer)

    def relay(kind, area, middle, turn):
        s = sources[turn]
        arrive(area(other_x, b, s), x_sems.at[kind, turn], x_peer)
        beyond = area(other_x, b, s, middle, middle) if middle else area(other_x, b, s)
        send(beyond, y_half_sems.at[kind, turn], y_peer)
        send(area(other_x, b, s), core_sems.at[kind, turn, 1], core_peer)
        arrive(area(x, other_y, s), y_sems.at[kind, turn], y_peer)
        if middle:
            send(area(x, other_y, s, 0, middle), x_half_sems.at[kind, turn], x_peer)
        send(area(x, other_y, s), core_sems.at[kind, turn, 2], core_peer)

    def finish(kind, area, middle, turn):
        s = sources[turn]
        if middle:
            arrive(area(other_x, other_y, s, 0, middle), x_half_sems.at[kind, turn], x_peer)
        beyond = area(other_x, other_y, s, middle, middle) if middle else area(other_x, other_y, s)
        arrive(beyond, y_half_sems.at[kind, turn], y_peer)
        send(area(other_x, other_y, s), core_sems.at[kind, turn, 3], core_peer)

    far = (partner + 2) % 4

    def gathered(kind, area, middle, turn):
        places = [(x, partner), (other_x, partner), (x, far), (other_x, far)]
        for place, (xs, bs) in enumerate(places):
            arrive(area(xs, bs, sources[turn]), core_sems.at[kind, turn, place], core_peer)

    joint = [(0, region, half, turn) for turn in range(heads)]
    pieces = [(1, piece_of, 0, turn) for turn in range(1, heads)]
    tokens, strip = out_ref.shape[0], 256

    def accumulate(turn):
        place = pl.multiple_of(sources[turn] * width, width)
        block = out_ref[:, pl.ds(place, width)]
        basis_high, basis_low = halves_of(whole_ref[pl.ds(place, width), :])
        for start in range(0, tokens, strip):
            area = slice(start, start + strip)
            part = out_ref[area, pl.ds(place, width)]
            product = dot_of(part, block, 1, 1)
            rows = dot_of(basis_high, part, 0, 1) + dot_of(basis_low, part, 0, 1)
            if turn:
                product = product + token_sums[area, :]
                rows = rows + rows_ref[:, area]
            rows_ref[:, area] = rows
            if turn < heads - 1:
                token_sums[area, :] = product
            else:
                high, low = halves_of(product * (1.0 / tokens))
                high_ref[area, :] = high
                low_ref[area, :] = low
            if turn == 0:
                own_ref[area, :] = part

    basis_load.wait()
    for turn in range(1, heads):
        send_z(piece_of(x, b, z), 1, turn)

    def prepare(area, c, total):
        widened = hidden_rows[area, span(c)].astype(jnp.float32)
        scaled = (widened * gain_row[:, span(c)]).astype(jnp.bfloat16)
        hidden_rows[area, span(c)] = scaled
        squared = widened * widened
        for start in range(0, chunk, LANES):
            total = total + squared[:, start : start + LANES]
        return scaled, total

    def across(total):
        ones = jnp.ones((SUBLANES, LANES), jnp.float32)
        return exact(ones, total, 1, 1)

    def swap(source_ref, target_ref, index):
        going = copy(source_ref, target_ref, swap_sems.at[index], x_peer)
        going.start()
        return going

    gain_load.wait()
    away_total = jnp.zeros((local, LANES), jnp.float32)
    sums = jnp.zeros((local, half), jnp.float32)
    for c in range(chunks):
        away_loads[c].wait()
        scaled, away_total = prepare(away, c, away_total)
        key_loads[c].wait()
        sums = sums + dot_of(scaled, key_rows[span(c), :], 1, 0)
    partial[:, :half] = sums
    squares[...] = across(away_total)
    swaps = [
        swap(squares, peer_squares, 0),
        swap(partial.at[:, pl.ds(0, half)], peer_partial.at[:, pl.ds(0, half)], 1),
    ]
    for item in pieces:
        spread(*item)
    sums = jnp.zeros((local, half), jnp.float32)
    for c in range(chunks):
        value_loads[c].wait()
        sums = sums + dot_of(hidden_rows[away, span(c)], value_rows[span(c), :], 1, 0)
    partial[:, half:] = sums
    swaps.append(swap(partial.at[:, pl.ds(half, half)], peer_partial.at[:, pl.ds(half, half)], 2))
    for item in pieces:
        relay(*item)
    mine_total = jnp.zeros((local, LANES), jnp.float32)
    key_sums = jnp.zeros((local, half), jnp.float32)
    value_sums = jnp.zeros((local, half), jnp.float32)
    for c in range(chunks):
        mine_loads[c].wait()
        scaled, mine_total = prepare(mine, c, mine_total)
        key_sums = key_sums + dot_of(scaled, key_rows[span(c), :], 1, 0)
        value_sums = value_sums + dot_of(scaled, value_rows[span(c), :], 1, 0)
    own_squares = across(mine_total)
    for item in pieces:
        finish(*item)

    swaps[0].wait()
    eighths = jnp.full((SUBLANES, LANES), 1.0 / SUBLANES, jnp.float32)
    inverse_scale = lax.rsqrt(exact(own_squares + peer_squares[...], eighths, 0, 0) / D + EPSILON)
    row = pl.multiple_of((x * 4 + b) * local, local)
    swaps[1].wait()
    for g in range(half // HEAD_DIM):
        spot = slice(g * HEAD_DIM, (g + 1) * HEAD_DIM)
        key = (key_sums[:, spot] + peer_partial[:, spot]) * inverse_scale
        turned = key * cosine_ref[...] + pltpu.roll(key, HEAD_DIM // 2, 1) * sine_ref[...]
        column = pl.multiple_of(z * width + 2 * g * HEAD_DIM, HEAD_DIM)
        out_ref[pl.ds(row, local), pl.ds(column, HEAD_DIM)] = turned.astype(jnp.bfloat16)
    swaps[2].wait()
    for g in range(half // HEAD_DIM):
        spot = slice(g * HEAD_DIM, (g + 1) * HEAD_DIM)
        there = slice(half + g * HEAD_DIM, half + (g + 1) * HEAD_DIM)
        value = (value_sums[:, spot] + peer_partial[:, there]) * inverse_scale
        column = pl.multiple_of(z * width + (2 * g + 1) * HEAD_DIM, HEAD_DIM)
        out_ref[pl.ds(row, local), pl.ds(column, HEAD_DIM)] = value.astype(jnp.bfloat16)

    for turn in range(1, heads):
        send_z(region(x, b, z), 0, turn)
    for turn in range(len(joint) + 3):
        if turn < len(joint):
            spread(*joint[turn])
        if 1 <= turn < len(joint) + 1:
            relay(*joint[turn - 1])
        if 2 <= turn < len(joint) + 2:
            finish(*joint[turn - 2])
        if turn == 2:
            for item in pieces:
                gathered(*item)
        if turn >= 3:
            gathered(*joint[turn - 3])
            accumulate(turn - 3)
    for going in started:
        going.wait_send()


def collect(hidden_rows, gain, key_weight, value_weight, positions, basis, heads, tokens):
    depth = hidden_rows.shape[1]
    local = positions.shape[0]
    half, width = key_weight.shape[1], key_weight.shape[1] + value_weight.shape[1]
    half_width = HEAD_DIM // 2
    chunks = 4
    frequency = jnp.exp(
        jnp.arange(half_width, dtype=jnp.float32) * (-math.log(ROTARY_BASE) / half_width)
    )
    angles = positions.astype(jnp.float32)[:, None] * frequency[None, :]
    cosine, sine = jnp.cos(angles), jnp.sin(angles)
    dma = pltpu.SemaphoreType.DMA
    anywhere = pl.BlockSpec(memory_space=pltpu.HBM)
    inside = pl.BlockSpec(memory_space=pltpu.VMEM)
    return pl.pallas_call(
        functools.partial(collect_kernel, heads),
        out_shape=(
            jax.ShapeDtypeStruct((tokens, tokens), jnp.bfloat16),
            jax.ShapeDtypeStruct((tokens, tokens), jnp.bfloat16),
            jax.ShapeDtypeStruct((basis.shape[1], tokens), jnp.float32),
            jax.ShapeDtypeStruct((tokens, width), jnp.bfloat16),
        ),
        in_specs=[anywhere] * 4 + [inside] * 2 + [anywhere],
        out_specs=(inside,) * 4,
        scratch_shapes=[
            pltpu.VMEM((tokens, heads * width), jnp.bfloat16),
            pltpu.VMEM((heads * width, basis.shape[1]), jnp.float32),
            pltpu.VMEM((tokens, tokens), jnp.float32),
            pltpu.VMEM(hidden_rows.shape, jnp.bfloat16),
            pltpu.VMEM((1, depth), jnp.float32),
            pltpu.VMEM(key_weight.shape, jnp.bfloat16),
            pltpu.VMEM(value_weight.shape, jnp.bfloat16),
            pltpu.VMEM((local, width), jnp.float32),
            pltpu.VMEM((local, width), jnp.float32),
            pltpu.VMEM((SUBLANES, local), jnp.float32),
            pltpu.VMEM((SUBLANES, local), jnp.float32),
            dma((2, chunks)),
            dma((3, chunks)),
            dma((3, 2)),
            dma((2, heads, 2)),
            dma((2, heads, 2)),
            dma((2, heads, 2)),
            dma((2, heads, 2)),
            dma((2, heads, 2)),
            dma((2, heads, 4, 2)),
        ],
        compiler_params=pltpu.CompilerParams(
            collective_id=0, has_side_effects=True, vmem_limit_bytes=45 * 2**20
        ),
    )(
        hidden_rows,
        gain[None, :],
        key_weight,
        value_weight,
        jnp.concatenate([cosine, cosine], axis=1),
        jnp.concatenate([-sine, sine], axis=1),
        basis,
    )


def body(hidden, gain, key_weight, value_weight, positions, initial_basis):
    hidden_rows = hidden[0]
    local_tokens = positions.shape[1]
    seqs, batches, heads = lax.axis_size("seq"), lax.axis_size("batch"), lax.axis_size("head")
    tokens = local_tokens * seqs * batches
    if seqs == 2 and batches == 4 and tokens <= initial_basis.shape[0] * heads:
        collected = collect(
            hidden_rows,
            gain,
            key_weight,
            value_weight,
            positions[0],
            initial_basis,
            heads,
            tokens,
        )
        return iterate(*collected, initial_basis.shape[0] * heads)
    widened = hidden_rows.astype(jnp.float32)
    scaled = (widened * gain).astype(jnp.bfloat16)
    local_squares = jnp.sum(widened * widened, axis=1)
    key_columns = key_weight.shape[1]
    weights = jnp.concatenate([key_weight, value_weight], axis=1)
    own_squares = total_squares(local_squares, local_tokens)
    projected = lax.psum_scatter(
        jnp.dot(scaled, weights, preferred_element_type=jnp.float32),
        "seq",
        scatter_dimension=0,
        tiled=True,
    )
    inverse_scale = lax.rsqrt(own_squares / D + EPSILON)
    projected = projected * inverse_scale[:, None]
    key_rows = rotary(projected[:, :key_columns].reshape(local_tokens, -1, HEAD_DIM), positions[0])
    value_rows = projected[:, key_columns:].reshape(local_tokens, -1, HEAD_DIM)
    joint_rows = (
        jnp.stack([key_rows, value_rows], axis=2).reshape(local_tokens, -1).astype(jnp.bfloat16)
    )
    partial_value = lax.dot_general(
        joint_rows,
        lax.all_gather(joint_rows, "head", axis=1, tiled=True),
        (((0,), (0,)), ((), ())),
        preferred_element_type=jnp.float32,
    )
    token_total = local_tokens * lax.axis_size("seq") * lax.axis_size("batch")
    basis_block = initial_basis
    covariance = lax.psum(partial_value, ("seq", "batch")) / token_total
    for iteration in range(ITERS):
        whole_basis = whole_of(basis_block)
        images = jnp.dot(
            covariance,
            whole_basis,
            precision=lax.Precision.HIGHEST,
            preferred_element_type=jnp.float32,
        )
        gram_matrix = lax.psum(gram_of(images), "head") / whole_basis.shape[0]
        basis_block = orthonormal(images, gram_matrix)
    return basis_block


def solution(mesh):
    return jax.shard_map(
        body,
        mesh=mesh,
        in_specs=(
            P("batch", None, "seq"),
            P("seq"),
            P("seq", "head"),
            P("seq", "head"),
            P("batch", "seq"),
            P("head", None),
        ),
        out_specs=P("head", None),
        check_vma=False,
    )
```

```python
import functools
import math

import jax
import jax.numpy as jnp
from jax import lax
from jax.experimental import pallas as pl
from jax.experimental.pallas import tpu as pltpu
from jax.sharding import PartitionSpec as P

D = 16384
HEAD_DIM = 128
ITERS = 4


EPSILON = 1e-05
ROTARY_BASE = 500000.0


def rotary(head_rows, position_row):
    half_width = head_rows.shape[-1] // 2
    index_row = jnp.arange(half_width, dtype=jnp.float32)
    frequency = jnp.exp(index_row * (-math.log(ROTARY_BASE) / half_width))
    angles = position_row.astype(jnp.float32)[:, None] * frequency[None, :]
    cosine = jnp.cos(angles)[:, None, :]
    sine_part = jnp.sin(angles)[:, None, :]
    first_half = head_rows[..., :half_width]
    second_half = head_rows[..., half_width:]
    return jnp.concatenate(
        [
            first_half * cosine - second_half * sine_part,
            second_half * cosine + first_half * sine_part,
        ],
        axis=-1,
    )


def whole_of(basis_block):
    return lax.all_gather(basis_block, "head", axis=0, tiled=True)


def total_squares(local_squares, local_tokens):
    all_squares = lax.psum(local_squares, "seq")
    return lax.dynamic_slice_in_dim(all_squares, lax.axis_index("seq") * local_tokens, local_tokens)


def gram_of(images):
    return lax.dot_general(
        images,
        images,
        (((0,), (0,)), ((), ())),
        precision=lax.Precision.HIGHEST,
        preferred_element_type=jnp.float32,
    )


def orthonormal(images, gram_matrix):
    factor = jnp.linalg.cholesky(gram_matrix)
    return lax.linalg.triangular_solve(
        factor, images, left_side=False, lower=True, transpose_a=True
    )


LANES = 128
SUBLANES = 8
AHEAD = True


def dot_of(left, right, left_axis, right_axis, precision=None):
    return lax.dot_general(
        left,
        right,
        (((left_axis,), (right_axis,)), ((), ())),
        precision=precision,
        preferred_element_type=jnp.float32,
    )


def exact(left, right, left_axis, right_axis):
    return dot_of(left, right, left_axis, right_axis, lax.Precision.HIGHEST)


def halves_of(value):
    high = value.astype(jnp.bfloat16)
    return high, (value - high.astype(jnp.float32)).astype(jnp.bfloat16)


def thrice(left, right, left_axis, right_axis):
    left_high, left_low = halves_of(left)
    right_high, right_low = halves_of(right)
    return (
        dot_of(left_high, right_high, left_axis, right_axis)
        + dot_of(left_high, right_low, left_axis, right_axis)
        + dot_of(left_low, right_high, left_axis, right_axis)
    )


def inverse_factor(matrix):
    size = matrix.shape[0]
    shape = (SUBLANES, size)
    rows = lax.broadcasted_iota(jnp.int32, shape, 0)
    lanes = lax.broadcasted_iota(jnp.int32, shape, 1)
    groups = size // SUBLANES
    tiles = [matrix[SUBLANES * g : SUBLANES * (g + 1)] for g in range(groups)]
    out = []

    def row_of(value, at):
        return jnp.broadcast_to(value[at : at + 1, :], shape)

    def lane_of(value, at):
        return jnp.broadcast_to(value[:, at : at + 1], shape)

    def total(terms):
        while len(terms) > 1:
            pairs = [terms[i] + terms[i + 1] for i in range(0, len(terms) - 1, 2)]
            terms = pairs + terms[2 * len(pairs) :]
        return terms[0]

    zero = jnp.zeros(shape, jnp.float32)
    for own in range(groups):
        pivot = own * SUBLANES
        block = [lane_of(tiles[own], pivot + j) for j in range(SUBLANES)]
        if AHEAD and own:
            block = following
        last_group = own + 1 == groups
        if not last_group:
            below = [lane_of(tiles[own + 1], pivot + j) for j in range(SUBLANES)]
            if AHEAD:
                after = [lane_of(tiles[own + 1], pivot + SUBLANES + j) for j in range(SUBLANES)]
        factor = [None] * SUBLANES
        turned, weighted = [], []
        for k in range(0, SUBLANES, 2):
            one, two = block[k], block[k + 1]
            if not AHEAD:
                one, two = one + zero, two + zero
            first, cross, last = row_of(one, k), row_of(two, k), row_of(two, k + 1)
            scale = 1.0 / (first * last - cross * cross)
            mixed = cross * scale
            here, next_ = rows == k, rows == k + 1
            pair = here | next_
            first_scaled, last_scaled = first * scale, last * scale
            top = one * last_scaled - two * mixed
            low = two * first_scaled - one * mixed
            top = jnp.where(here, -last_scaled, jnp.where(next_, mixed, top))
            low = jnp.where(here, mixed, jnp.where(next_, -first_scaled, low))
            heads = {}
            for j in range(SUBLANES):
                if j in (k, k + 1):
                    continue
                x, y = row_of(block[j], k), row_of(block[j], k + 1)
                heads[j] = (x, y)
                block[j] = jnp.where(pair, 0.0, block[j]) - (top * x + low * y)
            block[k], block[k + 1] = -top, -low
            ratio = cross / first
            top_scale, low_scale = lax.rsqrt(first), lax.rsqrt(last - ratio * cross)
            ratio_scale = ratio * low_scale
            for j in range(k):
                x, y = heads[j]
                lower = y * low_scale - x * ratio_scale
                factor[j] = jnp.where(here, x * top_scale, jnp.where(next_, lower, factor[j]))
            factor[k] = jnp.where(here, top_scale, jnp.where(next_, -ratio_scale, 0.0))
            factor[k + 1] = jnp.where(next_, low_scale, 0.0)
            if AHEAD and not last_group:
                t1 = total([below[k]] + [heads[j][0] * below[j] for j in range(k)])
                t2 = total([below[k + 1]] + [heads[j][1] * below[j] for j in range(k)])
                turned += [t1, t2]
                weighted += [t1 * last_scaled - t2 * mixed, t2 * first_scaled - t1 * mixed]
        inside = (lanes >= pivot) & (lanes < pivot + SUBLANES)
        held = jnp.where(inside, jnp.where(lanes == rows + pivot, 1.0, 0.0), tiles[own])
        spread = [row_of(held, j) for j in range(SUBLANES)]
        result = total([factor[j] * spread[j] for j in range(SUBLANES)])
        out.append(jnp.where(lanes < pivot + SUBLANES, result, 0.0))
        if last_group:
            break
        mixed = total([block[j] * spread[j] for j in range(SUBLANES)])
        mixes = [row_of(mixed, j) for j in range(SUBLANES)]
        if AHEAD:
            following = [
                after[j] - total([turned[m] * row_of(weighted[m], j) for m in range(SUBLANES)])
                for j in range(SUBLANES)
            ]
        columns = [
            [below[j]] + [lane_of(tiles[g], pivot + j) for g in range(own + 2, groups)]
            for j in range(SUBLANES)
        ]
        for g in range(own + 1, groups):
            changes = [columns[j][g - own - 1] * mixes[j] for j in range(SUBLANES)]
            tiles[g] = jnp.where(inside, 0.0, tiles[g]) - total(changes)
        yield
    yield jnp.concatenate(out, axis=0)


def factors_of(*matrices):
    running = [inverse_factor(matrix) for matrix in matrices]
    for _ in range(matrices[0].shape[0] // SUBLANES):
        results = [next(each) for each in running]
    return results


def iterate_kernel(
    high_ref, low_ref, start_ref, own_ref, out_ref, rows_ref, images_ref, gram_ref, factor_ref, joint
):
    rank, tokens = start_ref.shape
    scale = 1.0 / (tokens * joint)
    left, right = slice(0, rank // 2), slice(rank // 2, rank)

    def applied(rows):
        rows_high, rows_low = halves_of(rows)
        return (
            dot_of(rows_high, high_ref[...], 1, 0)
            + dot_of(rows_high, low_ref[...], 1, 0)
            + dot_of(rows_low, high_ref[...], 1, 0)
        )

    def gram_block(rows, images):
        return thrice(rows, images, 1, 1) * scale

    def reduced(factor):
        scaled = exact(factor, gram_ref[left, right], 1, 0)
        return scaled, gram_ref[right, right] - exact(scaled, scaled, 0, 0)

    images = applied(start_ref[...])
    images_ref[...] = images
    gram = gram_block(start_ref[...], images)
    gram_ref[...] = gram
    factor_ref[...] = factors_of(gram[left, left])[0]

    def step(iteration, carry):
        factor = factor_ref[...]
        scaled, rest = reduced(factor)
        first = thrice(factor, images_ref[left, :], 1, 0)
        first_images = applied(first)
        rest_factor, next_factor = factors_of(rest, gram_block(first, first_images))
        remaining = images_ref[right, :] - thrice(scaled, first, 0, 0)
        second = thrice(rest_factor, remaining, 1, 0)
        second_images = applied(second)
        rows_ref[left, :] = first
        rows_ref[right, :] = second
        gram_ref[left, right] = gram_block(first, second_images)
        gram_ref[right, right] = gram_block(second, second_images)
        images_ref[left, :] = first_images
        images_ref[right, :] = second_images
        factor_ref[...] = next_factor
        return carry

    lax.fori_loop(0, ITERS - 1, step, 0)
    rows_high, rows_low = halves_of(rows_ref[...])
    own = own_ref[...]
    loose = (dot_of(rows_high, own, 1, 0) + dot_of(rows_low, own, 1, 0)) * (1.0 / tokens)
    factor = factor_ref[...]
    scaled, rest = reduced(factor)
    first = thrice(factor, loose[left, :], 1, 0)
    out_ref[:, left] = thrice(loose[left, :], factor, 0, 1)
    second = loose[right, :] - thrice(scaled, first, 0, 0)
    out_ref[:, right] = thrice(second, factors_of(rest)[0], 0, 1)


def iterate(high, low, start, own, joint):
    rank, tokens = start.shape

    def kernel(*refs):
        iterate_kernel(*refs, joint)

    return pl.pallas_call(
        kernel,
        out_shape=jax.ShapeDtypeStruct((own.shape[1], rank), jnp.float32),
        in_specs=[pl.BlockSpec(memory_space=pltpu.VMEM)] * 4,
        out_specs=pl.BlockSpec(memory_space=pltpu.VMEM),
        scratch_shapes=[
            pltpu.VMEM((rank, tokens), jnp.float32),
            pltpu.VMEM((rank, tokens), jnp.float32),
            pltpu.VMEM((rank, rank), jnp.float32),
            pltpu.VMEM((rank // 2, rank // 2), jnp.float32),
        ],
        compiler_params=pltpu.CompilerParams(vmem_limit_bytes=40 * 2**20),
    )(high, low, start, own)


def collect_kernel(
    heads,
    hidden_ref,
    gain_ref,
    key_ref,
    value_ref,
    cosine_ref,
    sine_ref,
    basis_ref,
    high_ref,
    low_ref,
    rows_ref,
    own_ref,
    out_ref,
    whole_ref,
    token_sums,
    hidden_rows,
    gain_row,
    key_rows,
    value_rows,
    partial,
    peer_partial,
    squares,
    peer_squares,
    load_sems,
    half_sems,
    swap_sems,
    z_sems,
    x_sems,
    y_sems,
    x_half_sems,
    y_half_sems,
    core_sems,
):
    x, b, z = lax.axis_index("seq"), lax.axis_index("batch"), lax.axis_index("head")
    local, width = peer_partial.shape
    half = width // 2
    rank = whole_ref.shape[1]
    piece = width // 4
    depth = gain_row.shape[1]
    chunks = load_sems.shape[1]
    chunk = depth // chunks
    other_x, other_y = 1 - x, (b + 2) % 4
    partner = b + 1 - 2 * (b % 2)
    x_peer, y_peer, core_peer = (other_x, b, z), (x, other_y, z), (x, partner, z)
    away = pl.ds(pl.multiple_of(other_x * local, local), local)
    mine = pl.ds(pl.multiple_of(x * local, local), local)

    def nearest(turn):
        if turn == 0 or heads != 4:
            return (z + turn) % heads
        side = z // 2
        inner = z + side * (3 - 2 * z)
        place = (1 + inner, 2 - 2 * inner, 3)[turn - 1]
        return 3 * side + (1 - 2 * side) * place

    sources = [nearest(turn) for turn in range(heads)]

    def z_peer(turn):
        return (x, b, sources[turn])

    own_block = whole_ref.at[pl.ds(pl.multiple_of(z * width, width), width), :]
    basis_load = pltpu.make_async_copy(basis_ref, own_block, half_sems.at[2, 0])
    gain_load = pltpu.make_async_copy(gain_ref, gain_row, half_sems.at[2, 1])

    def span(c):
        return pl.ds(c * chunk, chunk)

    def token_load(kind, area, c):
        return pltpu.make_async_copy(
            hidden_ref.at[area, span(c)], hidden_rows.at[area, span(c)], half_sems.at[kind, c]
        )

    away_loads = [token_load(0, away, c) for c in range(chunks)]
    mine_loads = [token_load(1, mine, c) for c in range(chunks)]
    key_loads = [
        pltpu.make_async_copy(key_ref.at[span(c), :], key_rows.at[span(c), :], load_sems.at[0, c])
        for c in range(chunks)
    ]
    value_loads = [
        pltpu.make_async_copy(
            value_ref.at[span(c), :], value_rows.at[span(c), :], load_sems.at[1, c]
        )
        for c in range(chunks)
    ]
    basis_load.start()
    gain_load.start()
    for c in range(chunks):
        away_loads[c].start()
        key_loads[c].start()
    for load in mine_loads + value_loads:
        load.start()

    barrier = pltpu.get_barrier_semaphore()
    peers = [x_peer, y_peer, core_peer] + [z_peer(d) for d in range(1, heads)]
    for peer in peers:
        pl.semaphore_signal(barrier, inc=1, device_id=peer, device_id_type=pl.DeviceIdType.MESH)
    pl.semaphore_wait(barrier, len(peers))

    def copy(source, target, sems, peer):
        return pltpu.make_async_remote_copy(
            src_ref=source,
            dst_ref=target,
            send_sem=sems.at[0],
            recv_sem=sems.at[1],
            device_id=peer,
            device_id_type=pl.DeviceIdType.MESH,
        )

    def region(kind, xs, bs, zs, start=0, size=half):
        row = pl.multiple_of((xs * 4 + bs) * local, local)
        column = pl.multiple_of(zs * width + (half if kind else 0) + start, LANES)
        return out_ref.at[pl.ds(row, local), pl.ds(column, size)]

    def piece_of(bs, zs):
        row = pl.multiple_of(zs * width + bs * piece, piece)
        return whole_ref.at[pl.ds(row, piece), :]

    started = []

    def send(area, sems, peer):
        going = copy(area, area, sems, peer)
        going.start()
        started.append(going)

    def arrive(area, sems, peer):
        copy(area, area, sems, peer).wait_recv()

    def send_z(area, kind, turn):
        going = pltpu.make_async_remote_copy(
            src_ref=area,
            dst_ref=area,
            send_sem=z_sems.at[kind, sources[turn], 0],
            recv_sem=z_sems.at[kind, z, 1],
            device_id=z_peer(turn),
            device_id_type=pl.DeviceIdType.MESH,
        )
        going.start()
        started.append(going)

    cuts = (half // 2, 0, half)

    def spread(kind, turn):
        own = region(kind, x, b, sources[turn])
        if turn:
            arrive(own, z_sems.at[kind, sources[turn]], z_peer(turn))
        send(own, x_sems.at[kind, turn], x_peer)
        send(own, y_sems.at[kind, turn], y_peer)
        send(own, core_sems.at[kind, turn, 0], core_peer)

    def relay(kind, turn):
        s, cut = sources[turn], cuts[kind]
        arrive(region(kind, other_x, b, s), x_sems.at[kind, turn], x_peer)
        if cut < half:
            beyond = region(kind, other_x, b, s, cut, half - cut)
            send(beyond, y_half_sems.at[kind, turn], y_peer)
        send(region(kind, other_x, b, s), core_sems.at[kind, turn, 1], core_peer)
        arrive(region(kind, x, other_y, s), y_sems.at[kind, turn], y_peer)
        send(region(kind, x, other_y, s, 0, cut), x_half_sems.at[kind, turn], x_peer)
        send(region(kind, x, other_y, s), core_sems.at[kind, turn, 2], core_peer)

    def finish(kind, turn):
        s, cut = sources[turn], cuts[kind]
        arrive(region(kind, other_x, other_y, s, 0, cut), x_half_sems.at[kind, turn], x_peer)
        if cut < half:
            beyond = region(kind, other_x, other_y, s, cut, half - cut)
            arrive(beyond, y_half_sems.at[kind, turn], y_peer)
        send(region(kind, other_x, other_y, s), core_sems.at[kind, turn, 3], core_peer)

    far = (partner + 2) % 4

    def gathered(kind, turn):
        places = [(x, partner), (other_x, partner), (x, far), (other_x, far)]
        for place, (xs, bs) in enumerate(places):
            area = region(kind, xs, bs, sources[turn])
            arrive(area, core_sems.at[kind, turn, place], core_peer)

    def spread_basis(turn):
        own = piece_of(b, sources[turn])
        arrive(own, z_sems.at[1, sources[turn]], z_peer(turn))
        send(own, y_sems.at[1, turn], y_peer)
        send(own, core_sems.at[1, turn, 0], core_peer)

    def relay_basis(turn):
        other = piece_of(other_y, sources[turn])
        arrive(other, y_sems.at[1, turn], y_peer)
        send(other, core_sems.at[1, turn, 1], core_peer)

    def gathered_basis(turn):
        arrive(piece_of(partner, sources[turn]), core_sems.at[1, turn, 0], core_peer)
        arrive(piece_of(far, sources[turn]), core_sems.at[1, turn, 1], core_peer)

    tokens, strip = out_ref.shape[0], 256

    def accumulate(turn):
        place = pl.multiple_of(sources[turn] * width, width)
        block = out_ref[:, pl.ds(place, width)]
        basis_block = whole_ref[pl.ds(place, width), :]
        spots = [slice(at, at + HEAD_DIM) for at in range(0, width, HEAD_DIM)]
        spots = spots[0::2] + spots[1::2]
        basis_block = jnp.concatenate([basis_block[spot, :] for spot in spots], axis=0)
        basis_high, basis_low = halves_of(basis_block)
        for start in range(0, tokens, strip):
            area = slice(start, start + strip)
            part = out_ref[area, pl.ds(place, width)]
            product = dot_of(part, block, 1, 1)
            rows = dot_of(basis_high, part, 0, 1) + dot_of(basis_low, part, 0, 1)
            if turn:
                product = product + token_sums[area, :]
                rows = rows + rows_ref[:, area]
            rows_ref[:, area] = rows
            if turn < heads - 1:
                token_sums[area, :] = product
            else:
                high, low = halves_of(product * (1.0 / tokens))
                high_ref[area, :] = high
                low_ref[area, :] = low
            if turn == 0:
                for index, spot in enumerate(spots):
                    own_ref[area, spot] = part[:, index * HEAD_DIM : (index + 1) * HEAD_DIM]

    basis_load.wait()
    for turn in range(1, heads):
        send_z(piece_of(b, z), 1, turn)

    def prepare(area, c, total):
        widened = hidden_rows[area, span(c)].astype(jnp.float32)
        scaled = (widened * gain_row[:, span(c)]).astype(jnp.bfloat16)
        hidden_rows[area, span(c)] = scaled
        squared = widened * widened
        for start in range(0, chunk, LANES):
            total = total + squared[:, start : start + LANES]
        return scaled, total

    def across(total):
        ones = jnp.ones((SUBLANES, LANES), jnp.float32)
        return exact(ones, total, 1, 1)

    def swap(source_ref, target_ref, index):
        going = copy(source_ref, target_ref, swap_sems.at[index], x_peer)
        going.start()
        return going

    gain_load.wait()
    away_total = jnp.zeros((local, LANES), jnp.float32)
    sums = jnp.zeros((local, half), jnp.float32)
    for c in range(chunks):
        away_loads[c].wait()
        scaled, away_total = prepare(away, c, away_total)
        key_loads[c].wait()
        sums = sums + dot_of(scaled, key_rows[span(c), :], 1, 0)
    partial[:, :half] = sums
    squares[...] = across(away_total)
    swaps = [
        swap(squares, peer_squares, 0),
        swap(partial.at[:, pl.ds(0, half)], peer_partial.at[:, pl.ds(0, half)], 1),
    ]
    mine_total = jnp.zeros((local, LANES), jnp.float32)
    sums = jnp.zeros((local, half), jnp.float32)
    for c in range(chunks):
        mine_loads[c].wait()
        scaled, mine_total = prepare(mine, c, mine_total)
        sums = sums + dot_of(scaled, key_rows[span(c), :], 1, 0)
    own_squares = across(mine_total)

    swaps[0].wait()
    eighths = jnp.full((SUBLANES, LANES), 1.0 / SUBLANES, jnp.float32)
    inverse_scale = lax.rsqrt(exact(own_squares + peer_squares[...], eighths, 0, 0) / D + EPSILON)
    row = pl.multiple_of((x * 4 + b) * local, local)
    swaps[1].wait()
    for g in range(half // HEAD_DIM):
        spot = slice(g * HEAD_DIM, (g + 1) * HEAD_DIM)
        key = (sums[:, spot] + peer_partial[:, spot]) * inverse_scale
        turned = key * cosine_ref[...] + pltpu.roll(key, HEAD_DIM // 2, 1) * sine_ref[...]
        column = pl.multiple_of(z * width + g * HEAD_DIM, HEAD_DIM)
        out_ref[pl.ds(row, local), pl.ds(column, HEAD_DIM)] = turned.astype(jnp.bfloat16)
    for turn in range(1, heads):
        send_z(region(0, x, b, z), 0, turn)
    spread(0, 0)

    sums = jnp.zeros((local, half), jnp.float32)
    for c in range(chunks):
        value_loads[c].wait()
        sums = sums + dot_of(hidden_rows[away, span(c)], value_rows[span(c), :], 1, 0)
    partial[:, half:] = sums
    swaps.append(swap(partial.at[:, pl.ds(half, half)], peer_partial.at[:, pl.ds(half, half)], 2))
    sums = jnp.zeros((local, half), jnp.float32)
    for c in range(chunks):
        sums = sums + dot_of(hidden_rows[mine, span(c)], value_rows[span(c), :], 1, 0)

    def values():
        swaps[2].wait()
        for g in range(half // HEAD_DIM):
            spot = slice(g * HEAD_DIM, (g + 1) * HEAD_DIM)
            there = slice(half + g * HEAD_DIM, half + (g + 1) * HEAD_DIM)
            value = (sums[:, spot] + peer_partial[:, there]) * inverse_scale
            column = pl.multiple_of(z * width + half + g * HEAD_DIM, HEAD_DIM)
            out_ref[pl.ds(row, local), pl.ds(column, HEAD_DIM)] = value.astype(jnp.bfloat16)
        for turn in range(1, heads):
            send_z(region(2, x, b, z), 2, turn)

    keys_first = min(2, heads)
    items = [(0, turn) for turn in range(keys_first)] + [(2, 0)]
    items += [(0, turn) for turn in range(keys_first, heads)]
    items += [(2, turn) for turn in range(1, heads)]

    def complete(kind, turn):
        gathered(kind, turn)
        if kind:
            accumulate(turn)

    for step in range(1, len(items) + 3):
        if step < len(items):
            if items[step] == (2, 0):
                values()
            spread(*items[step])
            if items[step] == (2, 0):
                for turn in range(1, heads):
                    spread_basis(turn)
        if step < len(items) + 1:
            relay(*items[step - 1])
        if step == len(items) - 1:
            for turn in range(1, heads):
                relay_basis(turn)
            for turn in range(1, heads):
                gathered_basis(turn)
        if step >= 3:
            complete(*items[step - 3])
        if 2 <= step < len(items) + 2:
            finish(*items[step - 2])
    for going in started:
        going.wait_send()


def collect(hidden_rows, gain, key_weight, value_weight, positions, basis, heads, tokens):
    depth = hidden_rows.shape[1]
    local = positions.shape[0]
    half, width = key_weight.shape[1], key_weight.shape[1] + value_weight.shape[1]
    half_width = HEAD_DIM // 2
    chunks = 4
    frequency = jnp.exp(
        jnp.arange(half_width, dtype=jnp.float32) * (-math.log(ROTARY_BASE) / half_width)
    )
    angles = positions.astype(jnp.float32)[:, None] * frequency[None, :]
    cosine, sine = jnp.cos(angles), jnp.sin(angles)
    dma = pltpu.SemaphoreType.DMA
    anywhere = pl.BlockSpec(memory_space=pltpu.HBM)
    inside = pl.BlockSpec(memory_space=pltpu.VMEM)
    return pl.pallas_call(
        functools.partial(collect_kernel, heads),
        out_shape=(
            jax.ShapeDtypeStruct((tokens, tokens), jnp.bfloat16),
            jax.ShapeDtypeStruct((tokens, tokens), jnp.bfloat16),
            jax.ShapeDtypeStruct((basis.shape[1], tokens), jnp.float32),
            jax.ShapeDtypeStruct((tokens, width), jnp.bfloat16),
        ),
        in_specs=[anywhere] * 4 + [inside] * 2 + [anywhere],
        out_specs=(inside,) * 4,
        scratch_shapes=[
            pltpu.VMEM((tokens, heads * width), jnp.bfloat16),
            pltpu.VMEM((heads * width, basis.shape[1]), jnp.float32),
            pltpu.VMEM((tokens, tokens), jnp.float32),
            pltpu.VMEM(hidden_rows.shape, jnp.bfloat16),
            pltpu.VMEM((1, depth), jnp.float32),
            pltpu.VMEM(key_weight.shape, jnp.bfloat16),
            pltpu.VMEM(value_weight.shape, jnp.bfloat16),
            pltpu.VMEM((local, width), jnp.float32),
            pltpu.VMEM((local, width), jnp.float32),
            pltpu.VMEM((SUBLANES, local), jnp.float32),
            pltpu.VMEM((SUBLANES, local), jnp.float32),
            dma((2, chunks)),
            dma((3, chunks)),
            dma((3, 2)),
            dma((3, heads, 2)),
            dma((3, heads, 2)),
            dma((3, heads, 2)),
            dma((3, heads, 2)),
            dma((3, heads, 2)),
            dma((3, heads, 4, 2)),
        ],
        compiler_params=pltpu.CompilerParams(
            collective_id=0, has_side_effects=True, vmem_limit_bytes=45 * 2**20
        ),
    )(
        hidden_rows,
        pltpu.with_memory_space_constraint(gain[None, :], pltpu.HBM),
        key_weight,
        value_weight,
        jnp.concatenate([cosine, cosine], axis=1),
        jnp.concatenate([-sine, sine], axis=1),
        pltpu.with_memory_space_constraint(basis, pltpu.HBM),
    )


def body(hidden, gain, key_weight, value_weight, positions, initial_basis):
    hidden_rows = hidden[0]
    local_tokens = positions.shape[1]
    seqs, batches, heads = lax.axis_size("seq"), lax.axis_size("batch"), lax.axis_size("head")
    tokens = local_tokens * seqs * batches
    if seqs == 2 and batches == 4 and tokens <= initial_basis.shape[0] * heads:
        collected = collect(
            hidden_rows,
            gain,
            key_weight,
            value_weight,
            positions[0],
            initial_basis,
            heads,
            tokens,
        )
        return iterate(*collected, initial_basis.shape[0] * heads)
    widened = hidden_rows.astype(jnp.float32)
    scaled = (widened * gain).astype(jnp.bfloat16)
    local_squares = jnp.sum(widened * widened, axis=1)
    key_columns = key_weight.shape[1]
    weights = jnp.concatenate([key_weight, value_weight], axis=1)
    own_squares = total_squares(local_squares, local_tokens)
    projected = lax.psum_scatter(
        jnp.dot(scaled, weights, preferred_element_type=jnp.float32),
        "seq",
        scatter_dimension=0,
        tiled=True,
    )
    inverse_scale = lax.rsqrt(own_squares / D + EPSILON)
    projected = projected * inverse_scale[:, None]
    key_rows = rotary(projected[:, :key_columns].reshape(local_tokens, -1, HEAD_DIM), positions[0])
    value_rows = projected[:, key_columns:].reshape(local_tokens, -1, HEAD_DIM)
    joint_rows = (
        jnp.stack([key_rows, value_rows], axis=2).reshape(local_tokens, -1).astype(jnp.bfloat16)
    )
    partial_value = lax.dot_general(
        joint_rows,
        lax.all_gather(joint_rows, "head", axis=1, tiled=True),
        (((0,), (0,)), ((), ())),
        preferred_element_type=jnp.float32,
    )
    token_total = local_tokens * lax.axis_size("seq") * lax.axis_size("batch")
    basis_block = initial_basis
    covariance = lax.psum(partial_value, ("seq", "batch")) / token_total
    for iteration in range(ITERS):
        whole_basis = whole_of(basis_block)
        images = jnp.dot(
            covariance,
            whole_basis,
            precision=lax.Precision.HIGHEST,
            preferred_element_type=jnp.float32,
        )
        gram_matrix = lax.psum(gram_of(images), "head") / whole_basis.shape[0]
        basis_block = orthonormal(images, gram_matrix)
    return basis_block


def solution(mesh):
    return jax.shard_map(
        body,
        mesh=mesh,
        in_specs=(
            P("batch", None, "seq"),
            P("seq"),
            P("seq", "head"),
            P("seq", "head"),
            P("batch", "seq"),
            P("head", None),
        ),
        out_specs=P("head", None),
        check_vma=False,
    )
```

```python
import functools
import math

import jax
import jax.numpy as jnp
from jax import lax
from jax.experimental import pallas as pl
from jax.experimental.pallas import tpu as pltpu
from jax.sharding import PartitionSpec as P

D = 16384
HEAD_DIM = 128
ITERS = 4


EPSILON = 1e-05
ROTARY_BASE = 500000.0


def rotary(head_rows, position_row):
    half_width = head_rows.shape[-1] // 2
    index_row = jnp.arange(half_width, dtype=jnp.float32)
    frequency = jnp.exp(index_row * (-math.log(ROTARY_BASE) / half_width))
    angles = position_row.astype(jnp.float32)[:, None] * frequency[None, :]
    cosine = jnp.cos(angles)[:, None, :]
    sine_part = jnp.sin(angles)[:, None, :]
    first_half = head_rows[..., :half_width]
    second_half = head_rows[..., half_width:]
    return jnp.concatenate(
        [
            first_half * cosine - second_half * sine_part,
            second_half * cosine + first_half * sine_part,
        ],
        axis=-1,
    )


def whole_of(basis_block):
    return lax.all_gather(basis_block, "head", axis=0, tiled=True)


def total_squares(local_squares, local_tokens):
    all_squares = lax.psum(local_squares, "seq")
    return lax.dynamic_slice_in_dim(all_squares, lax.axis_index("seq") * local_tokens, local_tokens)


def gram_of(images):
    return lax.dot_general(
        images,
        images,
        (((0,), (0,)), ((), ())),
        precision=lax.Precision.HIGHEST,
        preferred_element_type=jnp.float32,
    )


def orthonormal(images, gram_matrix):
    factor = jnp.linalg.cholesky(gram_matrix)
    return lax.linalg.triangular_solve(
        factor, images, left_side=False, lower=True, transpose_a=True
    )


LANES = 128
SUBLANES = 8
AHEAD = True


def dot_of(left, right, left_axis, right_axis, precision=None):
    return lax.dot_general(
        left,
        right,
        (((left_axis,), (right_axis,)), ((), ())),
        precision=precision,
        preferred_element_type=jnp.float32,
    )


def exact(left, right, left_axis, right_axis):
    return dot_of(left, right, left_axis, right_axis, lax.Precision.HIGHEST)


def halves_of(value):
    high = value.astype(jnp.bfloat16)
    return high, (value - high.astype(jnp.float32)).astype(jnp.bfloat16)


def thrice(left, right, left_axis, right_axis):
    left_high, left_low = halves_of(left)
    right_high, right_low = halves_of(right)
    return (
        dot_of(left_high, right_high, left_axis, right_axis)
        + dot_of(left_high, right_low, left_axis, right_axis)
        + dot_of(left_low, right_high, left_axis, right_axis)
    )


def inverse_factor(matrix):
    size = matrix.shape[0]
    shape = (SUBLANES, size)
    rows = lax.broadcasted_iota(jnp.int32, shape, 0)
    lanes = lax.broadcasted_iota(jnp.int32, shape, 1)
    groups = size // SUBLANES
    tiles = [matrix[SUBLANES * g : SUBLANES * (g + 1)] for g in range(groups)]
    out = []

    def row_of(value, at):
        return jnp.broadcast_to(value[at : at + 1, :], shape)

    def lane_of(value, at):
        return jnp.broadcast_to(value[:, at : at + 1], shape)

    def total(terms):
        while len(terms) > 1:
            pairs = [terms[i] + terms[i + 1] for i in range(0, len(terms) - 1, 2)]
            terms = pairs + terms[2 * len(pairs) :]
        return terms[0]

    zero = jnp.zeros(shape, jnp.float32)
    for own in range(groups):
        pivot = own * SUBLANES
        block = [lane_of(tiles[own], pivot + j) for j in range(SUBLANES)]
        if AHEAD and own:
            block = following
        last_group = own + 1 == groups
        if not last_group:
            below = [lane_of(tiles[own + 1], pivot + j) for j in range(SUBLANES)]
            if AHEAD:
                after = [lane_of(tiles[own + 1], pivot + SUBLANES + j) for j in range(SUBLANES)]
        factor = [None] * SUBLANES
        turned, weighted = [], []
        for k in range(0, SUBLANES, 2):
            one, two = block[k], block[k + 1]
            if not AHEAD:
                one, two = one + zero, two + zero
            first, cross, last = row_of(one, k), row_of(two, k), row_of(two, k + 1)
            scale = 1.0 / (first * last - cross * cross)
            mixed = cross * scale
            here, next_ = rows == k, rows == k + 1
            pair = here | next_
            first_scaled, last_scaled = first * scale, last * scale
            top = one * last_scaled - two * mixed
            low = two * first_scaled - one * mixed
            top = jnp.where(here, -last_scaled, jnp.where(next_, mixed, top))
            low = jnp.where(here, mixed, jnp.where(next_, -first_scaled, low))
            heads = {}
            for j in range(SUBLANES):
                if j in (k, k + 1):
                    continue
                x, y = row_of(block[j], k), row_of(block[j], k + 1)
                heads[j] = (x, y)
                block[j] = jnp.where(pair, 0.0, block[j]) - (top * x + low * y)
            block[k], block[k + 1] = -top, -low
            ratio = cross / first
            top_scale, low_scale = lax.rsqrt(first), lax.rsqrt(last - ratio * cross)
            ratio_scale = ratio * low_scale
            for j in range(k):
                x, y = heads[j]
                lower = y * low_scale - x * ratio_scale
                factor[j] = jnp.where(here, x * top_scale, jnp.where(next_, lower, factor[j]))
            factor[k] = jnp.where(here, top_scale, jnp.where(next_, -ratio_scale, 0.0))
            factor[k + 1] = jnp.where(next_, low_scale, 0.0)
            if AHEAD and not last_group:
                t1 = total([below[k]] + [heads[j][0] * below[j] for j in range(k)])
                t2 = total([below[k + 1]] + [heads[j][1] * below[j] for j in range(k)])
                turned += [t1, t2]
                weighted += [t1 * last_scaled - t2 * mixed, t2 * first_scaled - t1 * mixed]
        inside = (lanes >= pivot) & (lanes < pivot + SUBLANES)
        held = jnp.where(inside, jnp.where(lanes == rows + pivot, 1.0, 0.0), tiles[own])
        spread = [row_of(held, j) for j in range(SUBLANES)]
        result = total([factor[j] * spread[j] for j in range(SUBLANES)])
        out.append(jnp.where(lanes < pivot + SUBLANES, result, 0.0))
        if last_group:
            break
        mixed = total([block[j] * spread[j] for j in range(SUBLANES)])
        mixes = [row_of(mixed, j) for j in range(SUBLANES)]
        if AHEAD:
            following = [
                after[j] - total([turned[m] * row_of(weighted[m], j) for m in range(SUBLANES)])
                for j in range(SUBLANES)
            ]
        columns = [
            [below[j]] + [lane_of(tiles[g], pivot + j) for g in range(own + 2, groups)]
            for j in range(SUBLANES)
        ]
        for g in range(own + 1, groups):
            changes = [columns[j][g - own - 1] * mixes[j] for j in range(SUBLANES)]
            tiles[g] = jnp.where(inside, 0.0, tiles[g]) - total(changes)
        yield
    yield jnp.concatenate(out, axis=0)


def factors_of(*matrices):
    running = [inverse_factor(matrix) for matrix in matrices]
    for _ in range(matrices[0].shape[0] // SUBLANES):
        results = [next(each) for each in running]
    return results


def iterate_kernel(
    high_ref, low_ref, start_ref, own_ref, out_ref, rows_ref, images_ref, gram_ref, factor_ref, joint
):
    rank, tokens = start_ref.shape
    scale = 1.0 / (tokens * joint)
    left, right = slice(0, rank // 2), slice(rank // 2, rank)

    def applied(rows):
        rows_high, rows_low = halves_of(rows)
        return (
            dot_of(rows_high, high_ref[...], 1, 0)
            + dot_of(rows_high, low_ref[...], 1, 0)
            + dot_of(rows_low, high_ref[...], 1, 0)
        )

    def gram_block(rows, images):
        return thrice(rows, images, 1, 1) * scale

    def reduced(factor):
        scaled = exact(factor, gram_ref[left, right], 1, 0)
        return scaled, gram_ref[right, right] - exact(scaled, scaled, 0, 0)

    images = applied(start_ref[...])
    images_ref[...] = images
    gram = gram_block(start_ref[...], images)
    gram_ref[...] = gram
    factor_ref[...] = factors_of(gram[left, left])[0]

    def step(iteration, carry):
        factor = factor_ref[...]
        scaled, rest = reduced(factor)
        first = thrice(factor, images_ref[left, :], 1, 0)
        first_images = applied(first)
        rest_factor, next_factor = factors_of(rest, gram_block(first, first_images))
        remaining = images_ref[right, :] - thrice(scaled, first, 0, 0)
        second = thrice(rest_factor, remaining, 1, 0)
        second_images = applied(second)
        rows_ref[left, :] = first
        rows_ref[right, :] = second
        gram_ref[left, right] = gram_block(first, second_images)
        gram_ref[right, right] = gram_block(second, second_images)
        images_ref[left, :] = first_images
        images_ref[right, :] = second_images
        factor_ref[...] = next_factor
        return carry

    lax.fori_loop(0, ITERS - 1, step, 0)
    rows_high, rows_low = halves_of(rows_ref[...])
    own = own_ref[...]
    loose = (dot_of(rows_high, own, 1, 0) + dot_of(rows_low, own, 1, 0)) * (1.0 / tokens)
    factor = factor_ref[...]
    scaled, rest = reduced(factor)
    first = thrice(factor, loose[left, :], 1, 0)
    out_ref[:, left] = thrice(loose[left, :], factor, 0, 1)
    second = loose[right, :] - thrice(scaled, first, 0, 0)
    out_ref[:, right] = thrice(second, factors_of(rest)[0], 0, 1)


def iterate(high, low, start, own, joint):
    rank, tokens = start.shape

    def kernel(*refs):
        iterate_kernel(*refs, joint)

    return pl.pallas_call(
        kernel,
        out_shape=jax.ShapeDtypeStruct((own.shape[1], rank), jnp.float32),
        in_specs=[pl.BlockSpec(memory_space=pltpu.VMEM)] * 4,
        out_specs=pl.BlockSpec(memory_space=pltpu.VMEM),
        scratch_shapes=[
            pltpu.VMEM((rank, tokens), jnp.float32),
            pltpu.VMEM((rank, tokens), jnp.float32),
            pltpu.VMEM((rank, rank), jnp.float32),
            pltpu.VMEM((rank // 2, rank // 2), jnp.float32),
        ],
        compiler_params=pltpu.CompilerParams(vmem_limit_bytes=40 * 2**20),
    )(high, low, start, own)


def collect_kernel(
    heads,
    hidden_ref,
    gain_ref,
    key_ref,
    value_ref,
    cosine_ref,
    sine_ref,
    basis_ref,
    high_ref,
    low_ref,
    rows_ref,
    own_ref,
    out_ref,
    whole_ref,
    token_sums,
    hidden_rows,
    gain_row,
    key_rows,
    value_rows,
    partial,
    peer_partial,
    squares,
    peer_squares,
    load_sems,
    half_sems,
    swap_sems,
    z_sems,
    x_sems,
    y_sems,
    x_half_sems,
    y_half_sems,
    core_sems,
):
    x, b, z = lax.axis_index("seq"), lax.axis_index("batch"), lax.axis_index("head")
    local, width = peer_partial.shape
    half = width // 2
    rank = whole_ref.shape[1]
    piece = width // 8
    depth = gain_row.shape[1]
    chunks = load_sems.shape[1]
    chunk = depth // chunks
    other_x, other_y = 1 - x, (b + 2) % 4
    partner = b + 1 - 2 * (b % 2)
    x_peer, y_peer, core_peer = (other_x, b, z), (x, other_y, z), (x, partner, z)
    away = pl.ds(pl.multiple_of(other_x * local, local), local)
    mine = pl.ds(pl.multiple_of(x * local, local), local)

    def nearest(turn):
        if turn == 0 or heads != 4:
            return (z + turn) % heads
        side = z // 2
        inner = z + side * (3 - 2 * z)
        place = (1 + inner, 2 - 2 * inner, 3)[turn - 1]
        return 3 * side + (1 - 2 * side) * place

    sources = [nearest(turn) for turn in range(heads)]

    def z_peer(turn):
        return (x, b, sources[turn])

    own_block = whole_ref.at[pl.ds(pl.multiple_of(z * width, width), width), :]
    basis_load = pltpu.make_async_copy(basis_ref, own_block, half_sems.at[2, 0])
    gain_load = pltpu.make_async_copy(gain_ref, gain_row, half_sems.at[2, 1])

    def span(c):
        return pl.ds(c * chunk, chunk)

    def token_load(kind, area, c):
        return pltpu.make_async_copy(
            hidden_ref.at[area, span(c)], hidden_rows.at[area, span(c)], half_sems.at[kind, c]
        )

    away_loads = [token_load(0, away, c) for c in range(chunks)]
    mine_loads = [token_load(1, mine, c) for c in range(chunks)]
    key_loads = [
        pltpu.make_async_copy(key_ref.at[span(c), :], key_rows.at[span(c), :], load_sems.at[0, c])
        for c in range(chunks)
    ]
    value_loads = [
        pltpu.make_async_copy(
            value_ref.at[span(c), :], value_rows.at[span(c), :], load_sems.at[1, c]
        )
        for c in range(chunks)
    ]
    basis_load.start()
    gain_load.start()
    loads = [load for pair in zip(away_loads, key_loads) for load in pair]
    loads += value_loads + mine_loads
    waiting = list(loads)

    def issue():
        if waiting:
            waiting.pop(0).start()

    def ready(load):
        load.wait()
        issue()

    for _ in range(4):
        issue()

    barrier = pltpu.get_barrier_semaphore()
    peers = [x_peer, y_peer, core_peer] + [z_peer(d) for d in range(1, heads)]
    for peer in peers:
        pl.semaphore_signal(barrier, inc=1, device_id=peer, device_id_type=pl.DeviceIdType.MESH)
    pl.semaphore_wait(barrier, len(peers))

    def copy(source, target, sems, peer):
        return pltpu.make_async_remote_copy(
            src_ref=source,
            dst_ref=target,
            send_sem=sems.at[0],
            recv_sem=sems.at[1],
            device_id=peer,
            device_id_type=pl.DeviceIdType.MESH,
        )

    def region(xs, bs, zs, start=0, size=width):
        row = pl.multiple_of((xs * 4 + bs) * local, local)
        column = pl.multiple_of(zs * width + start, half)
        return out_ref.at[pl.ds(row, local), pl.ds(column, size)]

    def piece_of(xs, bs, zs, start=0, size=rank):
        row = pl.multiple_of(zs * width + (xs * 4 + bs) * piece, piece)
        return whole_ref.at[pl.ds(row, piece), pl.ds(start, size)]

    started = []

    def send(area, sems, peer):
        going = copy(area, area, sems, peer)
        going.start()
        started.append(going)

    def arrive(area, sems, peer):
        copy(area, area, sems, peer).wait_recv()

    def send_z(area, kind, turn):
        going = pltpu.make_async_remote_copy(
            src_ref=area,
            dst_ref=area,
            send_sem=z_sems.at[kind, sources[turn], 0],
            recv_sem=z_sems.at[kind, z, 1],
            device_id=z_peer(turn),
            device_id_type=pl.DeviceIdType.MESH,
        )
        going.start()
        started.append(going)

    def spread(kind, area, middle, turn):
        s = sources[turn]
        own = area(x, b, s)
        if turn:
            arrive(own, z_sems.at[kind, s], z_peer(turn))
        send(own, x_sems.at[kind, turn], x_peer)
        send(own, y_sems.at[kind, turn], y_peer)
        send(own, core_sems.at[kind, turn, 0], core_peer)

    def relay(kind, area, middle, turn):
        s = sources[turn]
        arrive(area(other_x, b, s), x_sems.at[kind, turn], x_peer)
        beyond = area(other_x, b, s, middle, middle) if middle else area(other_x, b, s)
        send(beyond, y_half_sems.at[kind, turn], y_peer)
        send(area(other_x, b, s), core_sems.at[kind, turn, 1], core_peer)
        arrive(area(x, other_y, s), y_sems.at[kind, turn], y_peer)
        if middle:
            send(area(x, other_y, s, 0, middle), x_half_sems.at[kind, turn], x_peer)
        send(area(x, other_y, s), core_sems.at[kind, turn, 2], core_peer)

    def finish(kind, area, middle, turn):
        s = sources[turn]
        if middle:
            arrive(area(other_x, other_y, s, 0, middle), x_half_sems.at[kind, turn], x_peer)
        beyond = area(other_x, other_y, s, middle, middle) if middle else area(other_x, other_y, s)
        arrive(beyond, y_half_sems.at[kind, turn], y_peer)
        send(area(other_x, other_y, s), core_sems.at[kind, turn, 3], core_peer)

    far = (partner + 2) % 4

    def gathered(kind, area, middle, turn):
        places = [(x, partner), (other_x, partner), (x, far), (other_x, far)]
        for place, (xs, bs) in enumerate(places):
            arrive(area(xs, bs, sources[turn]), core_sems.at[kind, turn, place], core_peer)

    joint = [(0, region, half, turn) for turn in range(heads)]
    pieces = [(1, piece_of, 0, turn) for turn in range(1, heads)]
    tokens, strip = out_ref.shape[0], 256

    def accumulate(turn):
        place = pl.multiple_of(sources[turn] * width, width)
        block = out_ref[:, pl.ds(place, width)]
        basis_high, basis_low = halves_of(whole_ref[pl.ds(place, width), :])
        for start in range(0, tokens, strip):
            area = slice(start, start + strip)
            part = out_ref[area, pl.ds(place, width)]
            product = dot_of(block, part, 1, 1)
            rows = dot_of(basis_high, part, 0, 1) + dot_of(basis_low, part, 0, 1)
            if turn:
                product = product + token_sums[:, area]
                rows = rows + rows_ref[:, area]
            rows_ref[:, area] = rows
            if turn < heads - 1:
                token_sums[:, area] = product
            else:
                high, low = halves_of(product * (1.0 / tokens))
                high_ref[:, area] = high
                low_ref[:, area] = low
            if turn == 0:
                own_ref[area, :] = part

    basis_load.wait()
    for turn in range(1, heads):
        send_z(piece_of(x, b, z), 1, turn)

    def prepare(area, c, total):
        widened = hidden_rows[area, span(c)].astype(jnp.float32)
        scaled = (widened * gain_row[:, span(c)]).astype(jnp.bfloat16)
        hidden_rows[area, span(c)] = scaled
        squared = widened * widened
        for start in range(0, chunk, LANES):
            total = total + squared[:, start : start + LANES]
        return scaled, total

    def across(total):
        ones = jnp.ones((SUBLANES, LANES), jnp.float32)
        return exact(ones, total, 1, 1)

    def swap(source_ref, target_ref, index):
        going = copy(source_ref, target_ref, swap_sems.at[index], x_peer)
        going.start()
        return going

    gain_load.wait()
    away_total = jnp.zeros((local, LANES), jnp.float32)
    sums = jnp.zeros((local, half), jnp.float32)
    for c in range(chunks):
        ready(away_loads[c])
        scaled, away_total = prepare(away, c, away_total)
        ready(key_loads[c])
        sums = sums + dot_of(scaled, key_rows[span(c), :], 1, 0)
    partial[:, :half] = sums
    squares[...] = across(away_total)
    swaps = [
        swap(squares, peer_squares, 0),
        swap(partial.at[:, pl.ds(0, half)], peer_partial.at[:, pl.ds(0, half)], 1),
    ]
    sums = jnp.zeros((local, half), jnp.float32)
    for c in range(chunks):
        ready(value_loads[c])
        sums = sums + dot_of(hidden_rows[away, span(c)], value_rows[span(c), :], 1, 0)
    partial[:, half:] = sums
    swaps.append(swap(partial.at[:, pl.ds(half, half)], peer_partial.at[:, pl.ds(half, half)], 2))
    mine_total = jnp.zeros((local, LANES), jnp.float32)
    key_sums = jnp.zeros((local, half), jnp.float32)
    value_sums = jnp.zeros((local, half), jnp.float32)
    for c in range(chunks):
        ready(mine_loads[c])
        scaled, mine_total = prepare(mine, c, mine_total)
        key_sums = key_sums + dot_of(scaled, key_rows[span(c), :], 1, 0)
        value_sums = value_sums + dot_of(scaled, value_rows[span(c), :], 1, 0)
    own_squares = across(mine_total)
    for item in pieces:
        spread(*item)

    swaps[0].wait()
    eighths = jnp.full((SUBLANES, LANES), 1.0 / SUBLANES, jnp.float32)
    inverse_scale = lax.rsqrt(exact(own_squares + peer_squares[...], eighths, 0, 0) / D + EPSILON)
    row = pl.multiple_of((x * 4 + b) * local, local)
    swaps[1].wait()
    for g in range(half // HEAD_DIM):
        spot = slice(g * HEAD_DIM, (g + 1) * HEAD_DIM)
        key = (key_sums[:, spot] + peer_partial[:, spot]) * inverse_scale
        turned = key * cosine_ref[...] + pltpu.roll(key, HEAD_DIM // 2, 1) * sine_ref[...]
        column = pl.multiple_of(z * width + 2 * g * HEAD_DIM, HEAD_DIM)
        out_ref[pl.ds(row, local), pl.ds(column, HEAD_DIM)] = turned.astype(jnp.bfloat16)
    swaps[2].wait()
    for g in range(half // HEAD_DIM):
        spot = slice(g * HEAD_DIM, (g + 1) * HEAD_DIM)
        there = slice(half + g * HEAD_DIM, half + (g + 1) * HEAD_DIM)
        value = (value_sums[:, spot] + peer_partial[:, there]) * inverse_scale
        column = pl.multiple_of(z * width + (2 * g + 1) * HEAD_DIM, HEAD_DIM)
        out_ref[pl.ds(row, local), pl.ds(column, HEAD_DIM)] = value.astype(jnp.bfloat16)

    for turn in range(1, heads):
        send_z(region(x, b, z), 0, turn)
    for turn in range(len(joint) + 2):
        if turn < len(joint):
            spread(*joint[turn])
        if 1 <= turn < len(joint) + 1:
            relay(*joint[turn - 1])
        if turn == len(joint) + 1:
            for item in pieces:
                gathered(*item)
            for early in range(1, len(joint) - 2):
                gathered(*joint[early])
                accumulate(early)
        if turn >= 2:
            finish(*joint[turn - 2])
        if turn == 1:
            for item in pieces:
                relay(*item)
        if turn == 2:
            for item in pieces:
                finish(*item)
        if turn == 3:
            gathered(*joint[0])
            accumulate(0)
    for turn in range(max(1, len(joint) - 2), len(joint)):
        gathered(*joint[turn])
        accumulate(turn)
    for going in started:
        going.wait_send()


def collect(hidden_rows, gain, key_weight, value_weight, positions, basis, heads, tokens):
    depth = hidden_rows.shape[1]
    local = positions.shape[0]
    half, width = key_weight.shape[1], key_weight.shape[1] + value_weight.shape[1]
    half_width = HEAD_DIM // 2
    chunks = 4
    frequency = jnp.exp(
        jnp.arange(half_width, dtype=jnp.float32) * (-math.log(ROTARY_BASE) / half_width)
    )
    angles = positions.astype(jnp.float32)[:, None] * frequency[None, :]
    cosine, sine = jnp.cos(angles), jnp.sin(angles)
    dma = pltpu.SemaphoreType.DMA
    anywhere = pl.BlockSpec(memory_space=pltpu.HBM)
    inside = pl.BlockSpec(memory_space=pltpu.VMEM)
    return pl.pallas_call(
        functools.partial(collect_kernel, heads),
        out_shape=(
            jax.ShapeDtypeStruct((tokens, tokens), jnp.bfloat16),
            jax.ShapeDtypeStruct((tokens, tokens), jnp.bfloat16),
            jax.ShapeDtypeStruct((basis.shape[1], tokens), jnp.float32),
            jax.ShapeDtypeStruct((tokens, width), jnp.bfloat16),
        ),
        in_specs=[anywhere] * 4 + [inside] * 2 + [anywhere],
        out_specs=(inside,) * 4,
        scratch_shapes=[
            pltpu.VMEM((tokens, heads * width), jnp.bfloat16),
            pltpu.VMEM((heads * width, basis.shape[1]), jnp.float32),
            pltpu.VMEM((tokens, tokens), jnp.float32),
            pltpu.VMEM(hidden_rows.shape, jnp.bfloat16),
            pltpu.VMEM((1, depth), jnp.float32),
            pltpu.VMEM(key_weight.shape, jnp.bfloat16),
            pltpu.VMEM(value_weight.shape, jnp.bfloat16),
            pltpu.VMEM((local, width), jnp.float32),
            pltpu.VMEM((local, width), jnp.float32),
            pltpu.VMEM((SUBLANES, local), jnp.float32),
            pltpu.VMEM((SUBLANES, local), jnp.float32),
            dma((2, chunks)),
            dma((3, chunks)),
            dma((3, 2)),
            dma((2, heads, 2)),
            dma((2, heads, 2)),
            dma((2, heads, 2)),
            dma((2, heads, 2)),
            dma((2, heads, 2)),
            dma((2, heads, 4, 2)),
        ],
        compiler_params=pltpu.CompilerParams(
            collective_id=0, has_side_effects=True, vmem_limit_bytes=45 * 2**20
        ),
    )(
        hidden_rows,
        pltpu.with_memory_space_constraint(gain[None, :], pltpu.HBM),
        key_weight,
        value_weight,
        jnp.concatenate([cosine, cosine], axis=1),
        jnp.concatenate([-sine, sine], axis=1),
        pltpu.with_memory_space_constraint(basis, pltpu.HBM),
    )


def body(hidden, gain, key_weight, value_weight, positions, initial_basis):
    hidden_rows = hidden[0]
    local_tokens = positions.shape[1]
    seqs, batches, heads = lax.axis_size("seq"), lax.axis_size("batch"), lax.axis_size("head")
    tokens = local_tokens * seqs * batches
    if seqs == 2 and batches == 4 and tokens <= initial_basis.shape[0] * heads:
        collected = collect(
            hidden_rows,
            gain,
            key_weight,
            value_weight,
            positions[0],
            initial_basis,
            heads,
            tokens,
        )
        return iterate(*collected, initial_basis.shape[0] * heads)
    widened = hidden_rows.astype(jnp.float32)
    scaled = (widened * gain).astype(jnp.bfloat16)
    local_squares = jnp.sum(widened * widened, axis=1)
    key_columns = key_weight.shape[1]
    weights = jnp.concatenate([key_weight, value_weight], axis=1)
    own_squares = total_squares(local_squares, local_tokens)
    projected = lax.psum_scatter(
        jnp.dot(scaled, weights, preferred_element_type=jnp.float32),
        "seq",
        scatter_dimension=0,
        tiled=True,
    )
    inverse_scale = lax.rsqrt(own_squares / D + EPSILON)
    projected = projected * inverse_scale[:, None]
    key_rows = rotary(projected[:, :key_columns].reshape(local_tokens, -1, HEAD_DIM), positions[0])
    value_rows = projected[:, key_columns:].reshape(local_tokens, -1, HEAD_DIM)
    joint_rows = (
        jnp.stack([key_rows, value_rows], axis=2).reshape(local_tokens, -1).astype(jnp.bfloat16)
    )
    partial_value = lax.dot_general(
        joint_rows,
        lax.all_gather(joint_rows, "head", axis=1, tiled=True),
        (((0,), (0,)), ((), ())),
        preferred_element_type=jnp.float32,
    )
    token_total = local_tokens * lax.axis_size("seq") * lax.axis_size("batch")
    basis_block = initial_basis
    covariance = lax.psum(partial_value, ("seq", "batch")) / token_total
    for iteration in range(ITERS):
        whole_basis = whole_of(basis_block)
        images = jnp.dot(
            covariance,
            whole_basis,
            precision=lax.Precision.HIGHEST,
            preferred_element_type=jnp.float32,
        )
        gram_matrix = lax.psum(gram_of(images), "head") / whole_basis.shape[0]
        basis_block = orthonormal(images, gram_matrix)
    return basis_block


def solution(mesh):
    return jax.shard_map(
        body,
        mesh=mesh,
        in_specs=(
            P("batch", None, "seq"),
            P("seq"),
            P("seq", "head"),
            P("seq", "head"),
            P("batch", "seq"),
            P("head", None),
        ),
        out_specs=P("head", None),
        check_vma=False,
    )
```

```python
import functools
import math

import jax
import jax.numpy as jnp
from jax import lax
from jax.experimental import pallas as pl
from jax.experimental.pallas import tpu as pltpu
from jax.sharding import PartitionSpec as P

D = 16384
HEAD_DIM = 128
ITERS = 4


EPSILON = 1e-05
ROTARY_BASE = 500000.0


def rotary(head_rows, position_row):
    half_width = head_rows.shape[-1] // 2
    index_row = jnp.arange(half_width, dtype=jnp.float32)
    frequency = jnp.exp(index_row * (-math.log(ROTARY_BASE) / half_width))
    angles = position_row.astype(jnp.float32)[:, None] * frequency[None, :]
    cosine = jnp.cos(angles)[:, None, :]
    sine_part = jnp.sin(angles)[:, None, :]
    first_half = head_rows[..., :half_width]
    second_half = head_rows[..., half_width:]
    return jnp.concatenate(
        [
            first_half * cosine - second_half * sine_part,
            second_half * cosine + first_half * sine_part,
        ],
        axis=-1,
    )


def whole_of(basis_block):
    return lax.all_gather(basis_block, "head", axis=0, tiled=True)


def total_squares(local_squares, local_tokens):
    all_squares = lax.psum(local_squares, "seq")
    return lax.dynamic_slice_in_dim(all_squares, lax.axis_index("seq") * local_tokens, local_tokens)


def gram_of(images):
    return lax.dot_general(
        images,
        images,
        (((0,), (0,)), ((), ())),
        precision=lax.Precision.HIGHEST,
        preferred_element_type=jnp.float32,
    )


def orthonormal(images, gram_matrix):
    factor = jnp.linalg.cholesky(gram_matrix)
    return lax.linalg.triangular_solve(
        factor, images, left_side=False, lower=True, transpose_a=True
    )


LANES = 128
SUBLANES = 8
AHEAD = True


def dot_of(left, right, left_axis, right_axis, precision=None):
    return lax.dot_general(
        left,
        right,
        (((left_axis,), (right_axis,)), ((), ())),
        precision=precision,
        preferred_element_type=jnp.float32,
    )


def exact(left, right, left_axis, right_axis):
    return dot_of(left, right, left_axis, right_axis, lax.Precision.HIGHEST)


def halves_of(value):
    high = value.astype(jnp.bfloat16)
    return high, (value - high.astype(jnp.float32)).astype(jnp.bfloat16)


def thrice(left, right, left_axis, right_axis):
    left_high, left_low = halves_of(left)
    right_high, right_low = halves_of(right)
    return (
        dot_of(left_high, right_high, left_axis, right_axis)
        + dot_of(left_high, right_low, left_axis, right_axis)
        + dot_of(left_low, right_high, left_axis, right_axis)
    )


def inverse_factor(matrix):
    size = matrix.shape[0]
    shape = (SUBLANES, size)
    rows = lax.broadcasted_iota(jnp.int32, shape, 0)
    lanes = lax.broadcasted_iota(jnp.int32, shape, 1)
    groups = size // SUBLANES
    tiles = [matrix[SUBLANES * g : SUBLANES * (g + 1)] for g in range(groups)]
    out = []

    def row_of(value, at):
        return jnp.broadcast_to(value[at : at + 1, :], shape)

    def lane_of(value, at):
        return jnp.broadcast_to(value[:, at : at + 1], shape)

    def total(terms):
        while len(terms) > 1:
            pairs = [terms[i] + terms[i + 1] for i in range(0, len(terms) - 1, 2)]
            terms = pairs + terms[2 * len(pairs) :]
        return terms[0]

    zero = jnp.zeros(shape, jnp.float32)
    for own in range(groups):
        pivot = own * SUBLANES
        block = [lane_of(tiles[own], pivot + j) for j in range(SUBLANES)]
        if AHEAD and own:
            block = following
        last_group = own + 1 == groups
        if not last_group:
            below = [lane_of(tiles[own + 1], pivot + j) for j in range(SUBLANES)]
            if AHEAD:
                after = [lane_of(tiles[own + 1], pivot + SUBLANES + j) for j in range(SUBLANES)]
        factor = [None] * SUBLANES
        turned, weighted = [], []
        for k in range(0, SUBLANES, 2):
            one, two = block[k], block[k + 1]
            if not AHEAD:
                one, two = one + zero, two + zero
            first, cross, last = row_of(one, k), row_of(two, k), row_of(two, k + 1)
            scale = 1.0 / (first * last - cross * cross)
            mixed = cross * scale
            here, next_ = rows == k, rows == k + 1
            pair = here | next_
            first_scaled, last_scaled = first * scale, last * scale
            top = one * last_scaled - two * mixed
            low = two * first_scaled - one * mixed
            top = jnp.where(here, -last_scaled, jnp.where(next_, mixed, top))
            low = jnp.where(here, mixed, jnp.where(next_, -first_scaled, low))
            heads = {}
            for j in range(SUBLANES):
                if j in (k, k + 1):
                    continue
                x, y = row_of(block[j], k), row_of(block[j], k + 1)
                heads[j] = (x, y)
                block[j] = jnp.where(pair, 0.0, block[j]) - (top * x + low * y)
            block[k], block[k + 1] = -top, -low
            ratio = cross / first
            top_scale, low_scale = lax.rsqrt(first), lax.rsqrt(last - ratio * cross)
            ratio_scale = ratio * low_scale
            for j in range(k):
                x, y = heads[j]
                lower = y * low_scale - x * ratio_scale
                factor[j] = jnp.where(here, x * top_scale, jnp.where(next_, lower, factor[j]))
            factor[k] = jnp.where(here, top_scale, jnp.where(next_, -ratio_scale, 0.0))
            factor[k + 1] = jnp.where(next_, low_scale, 0.0)
            if AHEAD and not last_group:
                t1 = total([below[k]] + [heads[j][0] * below[j] for j in range(k)])
                t2 = total([below[k + 1]] + [heads[j][1] * below[j] for j in range(k)])
                turned += [t1, t2]
                weighted += [t1 * last_scaled - t2 * mixed, t2 * first_scaled - t1 * mixed]
        inside = (lanes >= pivot) & (lanes < pivot + SUBLANES)
        held = jnp.where(inside, jnp.where(lanes == rows + pivot, 1.0, 0.0), tiles[own])
        spread = [row_of(held, j) for j in range(SUBLANES)]
        result = total([factor[j] * spread[j] for j in range(SUBLANES)])
        out.append(jnp.where(lanes < pivot + SUBLANES, result, 0.0))
        if last_group:
            break
        mixed = total([block[j] * spread[j] for j in range(SUBLANES)])
        mixes = [row_of(mixed, j) for j in range(SUBLANES)]
        if AHEAD:
            following = [
                after[j] - total([turned[m] * row_of(weighted[m], j) for m in range(SUBLANES)])
                for j in range(SUBLANES)
            ]
        columns = [
            [below[j]] + [lane_of(tiles[g], pivot + j) for g in range(own + 2, groups)]
            for j in range(SUBLANES)
        ]
        for g in range(own + 1, groups):
            changes = [columns[j][g - own - 1] * mixes[j] for j in range(SUBLANES)]
            tiles[g] = jnp.where(inside, 0.0, tiles[g]) - total(changes)
        yield
    yield jnp.concatenate(out, axis=0)


def factors_of(*matrices):
    running = [inverse_factor(matrix) for matrix in matrices]
    for _ in range(matrices[0].shape[0] // SUBLANES):
        results = [next(each) for each in running]
    return results


def iterate_kernel(
    high_ref, low_ref, start_ref, own_ref, out_ref, rows_ref, images_ref, gram_ref, factor_ref, joint
):
    rank, tokens = start_ref.shape
    scale = 1.0 / (tokens * joint)
    left, right = slice(0, rank // 2), slice(rank // 2, rank)

    def applied(rows):
        rows_high, rows_low = halves_of(rows)
        return (
            dot_of(rows_high, high_ref[...], 1, 0)
            + dot_of(rows_high, low_ref[...], 1, 0)
            + dot_of(rows_low, high_ref[...], 1, 0)
        )

    def gram_block(rows, images):
        return thrice(rows, images, 1, 1) * scale

    def reduced(factor):
        scaled = exact(factor, gram_ref[left, right], 1, 0)
        return scaled, gram_ref[right, right] - exact(scaled, scaled, 0, 0)

    images = applied(start_ref[...])
    images_ref[...] = images
    gram = gram_block(start_ref[...], images)
    gram_ref[...] = gram
    factor_ref[...] = factors_of(gram[left, left])[0]

    def step(iteration, carry):
        factor = factor_ref[...]
        scaled, rest = reduced(factor)
        first = thrice(factor, images_ref[left, :], 1, 0)
        first_images = applied(first)
        rest_factor, next_factor = factors_of(rest, gram_block(first, first_images))
        remaining = images_ref[right, :] - thrice(scaled, first, 0, 0)
        second = thrice(rest_factor, remaining, 1, 0)
        second_images = applied(second)
        rows_ref[left, :] = first
        rows_ref[right, :] = second
        gram_ref[left, right] = gram_block(first, second_images)
        gram_ref[right, right] = gram_block(second, second_images)
        images_ref[left, :] = first_images
        images_ref[right, :] = second_images
        factor_ref[...] = next_factor
        return carry

    lax.fori_loop(0, ITERS - 1, step, 0)
    rows_high, rows_low = halves_of(rows_ref[...])
    own = own_ref[...]
    loose = (dot_of(rows_high, own, 1, 0) + dot_of(rows_low, own, 1, 0)) * (1.0 / tokens)
    factor = factor_ref[...]
    scaled, rest = reduced(factor)
    first = thrice(factor, loose[left, :], 1, 0)
    out_ref[:, left] = thrice(loose[left, :], factor, 0, 1)
    second = loose[right, :] - thrice(scaled, first, 0, 0)
    out_ref[:, right] = thrice(second, factors_of(rest)[0], 0, 1)


def iterate(high, low, start, own, joint):
    rank, tokens = start.shape

    def kernel(*refs):
        iterate_kernel(*refs, joint)

    return pl.pallas_call(
        kernel,
        out_shape=jax.ShapeDtypeStruct((own.shape[1], rank), jnp.float32),
        in_specs=[pl.BlockSpec(memory_space=pltpu.VMEM)] * 4,
        out_specs=pl.BlockSpec(memory_space=pltpu.VMEM),
        scratch_shapes=[
            pltpu.VMEM((rank, tokens), jnp.float32),
            pltpu.VMEM((rank, tokens), jnp.float32),
            pltpu.VMEM((rank, rank), jnp.float32),
            pltpu.VMEM((rank // 2, rank // 2), jnp.float32),
        ],
        compiler_params=pltpu.CompilerParams(vmem_limit_bytes=40 * 2**20),
    )(high, low, start, own)


def collect_kernel(
    heads,
    hidden_ref,
    gain_ref,
    key_ref,
    value_ref,
    cosine_ref,
    sine_ref,
    basis_ref,
    high_ref,
    low_ref,
    rows_ref,
    own_ref,
    out_ref,
    whole_ref,
    token_sums,
    hidden_rows,
    gain_row,
    key_rows,
    value_rows,
    partial,
    peer_partial,
    squares,
    peer_squares,
    load_sems,
    half_sems,
    swap_sems,
    z_sems,
    x_sems,
    y_sems,
    x_half_sems,
    y_half_sems,
    core_sems,
):
    x, b, z = lax.axis_index("seq"), lax.axis_index("batch"), lax.axis_index("head")
    local, width = peer_partial.shape
    half = width // 2
    rank = whole_ref.shape[1]
    piece = width // 8
    depth = gain_row.shape[1]
    chunks = load_sems.shape[1]
    chunk = depth // chunks
    other_x, other_y = 1 - x, (b + 2) % 4
    partner = b + 1 - 2 * (b % 2)
    x_peer, y_peer, core_peer = (other_x, b, z), (x, other_y, z), (x, partner, z)
    away = pl.ds(pl.multiple_of(other_x * local, local), local)
    mine = pl.ds(pl.multiple_of(x * local, local), local)

    def nearest(turn):
        if turn == 0 or heads != 4:
            return (z + turn) % heads
        side = z // 2
        inner = z + side * (3 - 2 * z)
        place = (1 + inner, 2 - 2 * inner, 3)[turn - 1]
        return 3 * side + (1 - 2 * side) * place

    sources = [nearest(turn) for turn in range(heads)]

    def z_peer(turn):
        return (x, b, sources[turn])

    own_block = whole_ref.at[pl.ds(pl.multiple_of(z * width, width), width), :]
    basis_load = pltpu.make_async_copy(basis_ref, own_block, half_sems.at[2, 0])
    gain_load = pltpu.make_async_copy(gain_ref, gain_row, half_sems.at[2, 1])

    def span(c):
        return pl.ds(c * chunk, chunk)

    def token_load(kind, area, c):
        return pltpu.make_async_copy(
            hidden_ref.at[area, span(c)], hidden_rows.at[area, span(c)], half_sems.at[kind, c]
        )

    away_loads = [token_load(0, away, c) for c in range(chunks)]
    mine_loads = [token_load(1, mine, c) for c in range(chunks)]
    key_loads = [
        pltpu.make_async_copy(key_ref.at[span(c), :], key_rows.at[span(c), :], load_sems.at[0, c])
        for c in range(chunks)
    ]
    value_loads = [
        pltpu.make_async_copy(
            value_ref.at[span(c), :], value_rows.at[span(c), :], load_sems.at[1, c]
        )
        for c in range(chunks)
    ]
    basis_load.start()
    gain_load.start()
    loads = [load for pair in zip(away_loads, key_loads) for load in pair]
    loads += value_loads + mine_loads
    waiting = list(loads)

    def issue():
        if waiting:
            waiting.pop(0).start()

    def ready(load):
        load.wait()
        issue()

    for _ in range(6):
        issue()

    barrier = pltpu.get_barrier_semaphore()
    peers = [x_peer, y_peer, core_peer] + [z_peer(d) for d in range(1, heads)]
    for peer in peers:
        pl.semaphore_signal(barrier, inc=1, device_id=peer, device_id_type=pl.DeviceIdType.MESH)
    pl.semaphore_wait(barrier, len(peers))

    def copy(source, target, sems, peer):
        return pltpu.make_async_remote_copy(
            src_ref=source,
            dst_ref=target,
            send_sem=sems.at[0],
            recv_sem=sems.at[1],
            device_id=peer,
            device_id_type=pl.DeviceIdType.MESH,
        )

    def region(xs, bs, zs, start=0, size=width):
        row = pl.multiple_of((xs * 4 + bs) * local, local)
        column = pl.multiple_of(zs * width + start, half)
        return out_ref.at[pl.ds(row, local), pl.ds(column, size)]

    def piece_of(xs, bs, zs, start=0, size=rank):
        row = pl.multiple_of(zs * width + (xs * 4 + bs) * piece, piece)
        return whole_ref.at[pl.ds(row, piece), pl.ds(start, size)]

    started = []

    def send(area, sems, peer):
        going = copy(area, area, sems, peer)
        going.start()
        started.append(going)

    def arrive(area, sems, peer):
        copy(area, area, sems, peer).wait_recv()

    def send_z(area, kind, turn):
        going = pltpu.make_async_remote_copy(
            src_ref=area,
            dst_ref=area,
            send_sem=z_sems.at[kind, sources[turn], 0],
            recv_sem=z_sems.at[kind, z, 1],
            device_id=z_peer(turn),
            device_id_type=pl.DeviceIdType.MESH,
        )
        going.start()
        started.append(going)

    def spread(kind, area, middle, turn):
        s = sources[turn]
        own = area(x, b, s)
        if turn:
            arrive(own, z_sems.at[kind, s], z_peer(turn))
        send(own, x_sems.at[kind, turn], x_peer)
        send(own, y_sems.at[kind, turn], y_peer)
        send(own, core_sems.at[kind, turn, 0], core_peer)

    def relay(kind, area, middle, turn):
        s = sources[turn]
        arrive(area(other_x, b, s), x_sems.at[kind, turn], x_peer)
        beyond = area(other_x, b, s, middle, middle) if middle else area(other_x, b, s)
        send(beyond, y_half_sems.at[kind, turn], y_peer)
        send(area(other_x, b, s), core_sems.at[kind, turn, 1], core_peer)
        arrive(area(x, other_y, s), y_sems.at[kind, turn], y_peer)
        if middle:
            send(area(x, other_y, s, 0, middle), x_half_sems.at[kind, turn], x_peer)
        send(area(x, other_y, s), core_sems.at[kind, turn, 2], core_peer)

    def finish(kind, area, middle, turn):
        s = sources[turn]
        if middle:
            arrive(area(other_x, other_y, s, 0, middle), x_half_sems.at[kind, turn], x_peer)
        beyond = area(other_x, other_y, s, middle, middle) if middle else area(other_x, other_y, s)
        arrive(beyond, y_half_sems.at[kind, turn], y_peer)
        send(area(other_x, other_y, s), core_sems.at[kind, turn, 3], core_peer)

    far = (partner + 2) % 4

    def gathered(kind, area, middle, turn):
        places = [(x, partner), (other_x, partner), (x, far), (other_x, far)]
        for place, (xs, bs) in enumerate(places):
            arrive(area(xs, bs, sources[turn]), core_sems.at[kind, turn, place], core_peer)

    joint = [(0, region, half, turn) for turn in range(heads)]
    pieces = [(1, piece_of, 0, turn) for turn in range(1, heads)]
    tokens, strip = out_ref.shape[0], 256

    def accumulate(turn):
        place = pl.multiple_of(sources[turn] * width, width)
        block = out_ref[:, pl.ds(place, width)]
        basis_high, basis_low = halves_of(whole_ref[pl.ds(place, width), :])
        for start in range(0, tokens, strip):
            area = slice(start, start + strip)
            part = out_ref[area, pl.ds(place, width)]
            product = dot_of(block, part, 1, 1)
            rows = dot_of(basis_high, part, 0, 1) + dot_of(basis_low, part, 0, 1)
            if turn:
                product = product + token_sums[:, area]
                rows = rows + rows_ref[:, area]
            rows_ref[:, area] = rows
            if turn < heads - 1:
                token_sums[:, area] = product
            else:
                high, low = halves_of(product * (1.0 / tokens))
                high_ref[:, area] = high
                low_ref[:, area] = low
            if turn == 0:
                own_ref[area, :] = part

    basis_load.wait()
    for turn in range(1, heads):
        send_z(piece_of(x, b, z), 1, turn)

    def prepare(area, c, total):
        widened = hidden_rows[area, span(c)].astype(jnp.float32)
        scaled = (widened * gain_row[:, span(c)]).astype(jnp.bfloat16)
        hidden_rows[area, span(c)] = scaled
        squared = widened * widened
        for start in range(0, chunk, LANES):
            total = total + squared[:, start : start + LANES]
        return scaled, total

    def across(total):
        ones = jnp.ones((SUBLANES, LANES), jnp.float32)
        return exact(ones, total, 1, 1)

    def swap(source_ref, target_ref, index):
        going = copy(source_ref, target_ref, swap_sems.at[index], x_peer)
        going.start()
        return going

    gain_load.wait()
    away_total = jnp.zeros((local, LANES), jnp.float32)
    sums = jnp.zeros((local, half), jnp.float32)
    for c in range(chunks):
        ready(away_loads[c])
        scaled, away_total = prepare(away, c, away_total)
        ready(key_loads[c])
        sums = sums + dot_of(scaled, key_rows[span(c), :], 1, 0)
    partial[:, :half] = sums
    squares[...] = across(away_total)
    swaps = [
        swap(squares, peer_squares, 0),
        swap(partial.at[:, pl.ds(0, half)], peer_partial.at[:, pl.ds(0, half)], 1),
    ]
    sums = jnp.zeros((local, half), jnp.float32)
    for c in range(chunks):
        ready(value_loads[c])
        sums = sums + dot_of(hidden_rows[away, span(c)], value_rows[span(c), :], 1, 0)
    partial[:, half:] = sums
    swaps.append(swap(partial.at[:, pl.ds(half, half)], peer_partial.at[:, pl.ds(half, half)], 2))
    mine_total = jnp.zeros((local, LANES), jnp.float32)
    key_sums = jnp.zeros((local, half), jnp.float32)
    value_sums = jnp.zeros((local, half), jnp.float32)
    for c in range(chunks):
        ready(mine_loads[c])
        scaled, mine_total = prepare(mine, c, mine_total)
        key_sums = key_sums + dot_of(scaled, key_rows[span(c), :], 1, 0)
        value_sums = value_sums + dot_of(scaled, value_rows[span(c), :], 1, 0)
    own_squares = across(mine_total)

    swaps[0].wait()
    eighths = jnp.full((SUBLANES, LANES), 1.0 / SUBLANES, jnp.float32)
    inverse_scale = lax.rsqrt(exact(own_squares + peer_squares[...], eighths, 0, 0) / D + EPSILON)
    row = pl.multiple_of((x * 4 + b) * local, local)
    swaps[1].wait()
    for g in range(half // HEAD_DIM):
        spot = slice(g * HEAD_DIM, (g + 1) * HEAD_DIM)
        key = (key_sums[:, spot] + peer_partial[:, spot]) * inverse_scale
        turned = key * cosine_ref[...] + pltpu.roll(key, HEAD_DIM // 2, 1) * sine_ref[...]
        column = pl.multiple_of(z * width + 2 * g * HEAD_DIM, HEAD_DIM)
        out_ref[pl.ds(row, local), pl.ds(column, HEAD_DIM)] = turned.astype(jnp.bfloat16)
    swaps[2].wait()
    for g in range(half // HEAD_DIM):
        spot = slice(g * HEAD_DIM, (g + 1) * HEAD_DIM)
        there = slice(half + g * HEAD_DIM, half + (g + 1) * HEAD_DIM)
        value = (value_sums[:, spot] + peer_partial[:, there]) * inverse_scale
        column = pl.multiple_of(z * width + (2 * g + 1) * HEAD_DIM, HEAD_DIM)
        out_ref[pl.ds(row, local), pl.ds(column, HEAD_DIM)] = value.astype(jnp.bfloat16)

    for turn in range(1, heads):
        send_z(region(x, b, z), 0, turn)
    for turn in range(len(joint) + 2):
        if turn < len(joint):
            spread(*joint[turn])
        if turn == 0:
            for item in pieces:
                spread(*item)
        if 1 <= turn < len(joint) + 1:
            relay(*joint[turn - 1])
        if turn == len(joint) + 1:
            for item in pieces:
                gathered(*item)
            for early in range(1, len(joint) - 1):
                gathered(*joint[early])
                accumulate(early)
        if turn >= 2:
            finish(*joint[turn - 2])
        if turn == 2:
            for item in pieces:
                relay(*item)
        if turn == 3:
            for item in pieces:
                finish(*item)
            gathered(*joint[0])
            accumulate(0)
    gathered(*joint[-1])
    accumulate(len(joint) - 1)
    for going in started:
        going.wait_send()


def collect(hidden_rows, gain, key_weight, value_weight, positions, basis, heads, tokens):
    depth = hidden_rows.shape[1]
    local = positions.shape[0]
    half, width = key_weight.shape[1], key_weight.shape[1] + value_weight.shape[1]
    half_width = HEAD_DIM // 2
    chunks = 4
    frequency = jnp.exp(
        jnp.arange(half_width, dtype=jnp.float32) * (-math.log(ROTARY_BASE) / half_width)
    )
    angles = positions.astype(jnp.float32)[:, None] * frequency[None, :]
    cosine, sine = jnp.cos(angles), jnp.sin(angles)
    dma = pltpu.SemaphoreType.DMA
    anywhere = pl.BlockSpec(memory_space=pltpu.HBM)
    inside = pl.BlockSpec(memory_space=pltpu.VMEM)
    return pl.pallas_call(
        functools.partial(collect_kernel, heads),
        out_shape=(
            jax.ShapeDtypeStruct((tokens, tokens), jnp.bfloat16),
            jax.ShapeDtypeStruct((tokens, tokens), jnp.bfloat16),
            jax.ShapeDtypeStruct((basis.shape[1], tokens), jnp.float32),
            jax.ShapeDtypeStruct((tokens, width), jnp.bfloat16),
        ),
        in_specs=[anywhere] * 4 + [inside] * 2 + [anywhere],
        out_specs=(inside,) * 4,
        scratch_shapes=[
            pltpu.VMEM((tokens, heads * width), jnp.bfloat16),
            pltpu.VMEM((heads * width, basis.shape[1]), jnp.float32),
            pltpu.VMEM((tokens, tokens), jnp.float32),
            pltpu.VMEM(hidden_rows.shape, jnp.bfloat16),
            pltpu.VMEM((1, depth), jnp.float32),
            pltpu.VMEM(key_weight.shape, jnp.bfloat16),
            pltpu.VMEM(value_weight.shape, jnp.bfloat16),
            pltpu.VMEM((local, width), jnp.float32),
            pltpu.VMEM((local, width), jnp.float32),
            pltpu.VMEM((SUBLANES, local), jnp.float32),
            pltpu.VMEM((SUBLANES, local), jnp.float32),
            dma((2, chunks)),
            dma((3, chunks)),
            dma((3, 2)),
            dma((2, heads, 2)),
            dma((2, heads, 2)),
            dma((2, heads, 2)),
            dma((2, heads, 2)),
            dma((2, heads, 2)),
            dma((2, heads, 4, 2)),
        ],
        compiler_params=pltpu.CompilerParams(
            collective_id=0, has_side_effects=True, vmem_limit_bytes=45 * 2**20
        ),
    )(
        hidden_rows,
        pltpu.with_memory_space_constraint(gain[None, :], pltpu.HBM),
        key_weight,
        value_weight,
        jnp.concatenate([cosine, cosine], axis=1),
        jnp.concatenate([-sine, sine], axis=1),
        pltpu.with_memory_space_constraint(basis, pltpu.HBM),
    )


def body(hidden, gain, key_weight, value_weight, positions, initial_basis):
    hidden_rows = hidden[0]
    local_tokens = positions.shape[1]
    seqs, batches, heads = lax.axis_size("seq"), lax.axis_size("batch"), lax.axis_size("head")
    tokens = local_tokens * seqs * batches
    if seqs == 2 and batches == 4 and tokens <= initial_basis.shape[0] * heads:
        collected = collect(
            hidden_rows,
            gain,
            key_weight,
            value_weight,
            positions[0],
            initial_basis,
            heads,
            tokens,
        )
        return iterate(*collected, initial_basis.shape[0] * heads)
    widened = hidden_rows.astype(jnp.float32)
    scaled = (widened * gain).astype(jnp.bfloat16)
    local_squares = jnp.sum(widened * widened, axis=1)
    key_columns = key_weight.shape[1]
    weights = jnp.concatenate([key_weight, value_weight], axis=1)
    own_squares = total_squares(local_squares, local_tokens)
    projected = lax.psum_scatter(
        jnp.dot(scaled, weights, preferred_element_type=jnp.float32),
        "seq",
        scatter_dimension=0,
        tiled=True,
    )
    inverse_scale = lax.rsqrt(own_squares / D + EPSILON)
    projected = projected * inverse_scale[:, None]
    key_rows = rotary(projected[:, :key_columns].reshape(local_tokens, -1, HEAD_DIM), positions[0])
    value_rows = projected[:, key_columns:].reshape(local_tokens, -1, HEAD_DIM)
    joint_rows = (
        jnp.stack([key_rows, value_rows], axis=2).reshape(local_tokens, -1).astype(jnp.bfloat16)
    )
    partial_value = lax.dot_general(
        joint_rows,
        lax.all_gather(joint_rows, "head", axis=1, tiled=True),
        (((0,), (0,)), ((), ())),
        preferred_element_type=jnp.float32,
    )
    token_total = local_tokens * lax.axis_size("seq") * lax.axis_size("batch")
    basis_block = initial_basis
    covariance = lax.psum(partial_value, ("seq", "batch")) / token_total
    for iteration in range(ITERS):
        whole_basis = whole_of(basis_block)
        images = jnp.dot(
            covariance,
            whole_basis,
            precision=lax.Precision.HIGHEST,
            preferred_element_type=jnp.float32,
        )
        gram_matrix = lax.psum(gram_of(images), "head") / whole_basis.shape[0]
        basis_block = orthonormal(images, gram_matrix)
    return basis_block


def solution(mesh):
    return jax.shard_map(
        body,
        mesh=mesh,
        in_specs=(
            P("batch", None, "seq"),
            P("seq"),
            P("seq", "head"),
            P("seq", "head"),
            P("batch", "seq"),
            P("head", None),
        ),
        out_specs=P("head", None),
        check_vma=False,
    )
```

```python
import functools
import math

import jax
import jax.numpy as jnp
from jax import lax
from jax.experimental import pallas as pl
from jax.experimental.pallas import tpu as pltpu
from jax.sharding import PartitionSpec as P

D = 16384
HEAD_DIM = 128
ITERS = 4


EPSILON = 1e-05
ROTARY_BASE = 500000.0


def rotary(head_rows, position_row):
    half_width = head_rows.shape[-1] // 2
    index_row = jnp.arange(half_width, dtype=jnp.float32)
    frequency = jnp.exp(index_row * (-math.log(ROTARY_BASE) / half_width))
    angles = position_row.astype(jnp.float32)[:, None] * frequency[None, :]
    cosine = jnp.cos(angles)[:, None, :]
    sine_part = jnp.sin(angles)[:, None, :]
    first_half = head_rows[..., :half_width]
    second_half = head_rows[..., half_width:]
    return jnp.concatenate(
        [
            first_half * cosine - second_half * sine_part,
            second_half * cosine + first_half * sine_part,
        ],
        axis=-1,
    )


def whole_of(basis_block):
    return lax.all_gather(basis_block, "head", axis=0, tiled=True)


def total_squares(local_squares, local_tokens):
    all_squares = lax.psum(local_squares, "seq")
    return lax.dynamic_slice_in_dim(all_squares, lax.axis_index("seq") * local_tokens, local_tokens)


def gram_of(images):
    return lax.dot_general(
        images,
        images,
        (((0,), (0,)), ((), ())),
        precision=lax.Precision.HIGHEST,
        preferred_element_type=jnp.float32,
    )


def orthonormal(images, gram_matrix):
    factor = jnp.linalg.cholesky(gram_matrix)
    return lax.linalg.triangular_solve(
        factor, images, left_side=False, lower=True, transpose_a=True
    )


LANES = 128
SUBLANES = 8
AHEAD = True


def dot_of(left, right, left_axis, right_axis, precision=None):
    return lax.dot_general(
        left,
        right,
        (((left_axis,), (right_axis,)), ((), ())),
        precision=precision,
        preferred_element_type=jnp.float32,
    )


def exact(left, right, left_axis, right_axis):
    return dot_of(left, right, left_axis, right_axis, lax.Precision.HIGHEST)


def halves_of(value):
    high = value.astype(jnp.bfloat16)
    return high, (value - high.astype(jnp.float32)).astype(jnp.bfloat16)


def thrice(left, right, left_axis, right_axis):
    left_high, left_low = halves_of(left)
    right_high, right_low = halves_of(right)
    return (
        dot_of(left_high, right_high, left_axis, right_axis)
        + dot_of(left_high, right_low, left_axis, right_axis)
        + dot_of(left_low, right_high, left_axis, right_axis)
    )


def inverse_factor(matrix):
    size = matrix.shape[0]
    shape = (SUBLANES, size)
    rows = lax.broadcasted_iota(jnp.int32, shape, 0)
    lanes = lax.broadcasted_iota(jnp.int32, shape, 1)
    groups = size // SUBLANES
    tiles = [matrix[SUBLANES * g : SUBLANES * (g + 1)] for g in range(groups)]
    out = []

    def row_of(value, at):
        return jnp.broadcast_to(value[at : at + 1, :], shape)

    def lane_of(value, at):
        return jnp.broadcast_to(value[:, at : at + 1], shape)

    def total(terms):
        while len(terms) > 1:
            pairs = [terms[i] + terms[i + 1] for i in range(0, len(terms) - 1, 2)]
            terms = pairs + terms[2 * len(pairs) :]
        return terms[0]

    zero = jnp.zeros(shape, jnp.float32)
    for own in range(groups):
        pivot = own * SUBLANES
        block = [lane_of(tiles[own], pivot + j) for j in range(SUBLANES)]
        if AHEAD and own:
            block = following
        last_group = own + 1 == groups
        if not last_group:
            below = [lane_of(tiles[own + 1], pivot + j) for j in range(SUBLANES)]
            if AHEAD:
                after = [lane_of(tiles[own + 1], pivot + SUBLANES + j) for j in range(SUBLANES)]
        factor = [None] * SUBLANES
        turned, weighted = [], []
        for k in range(0, SUBLANES, 2):
            one, two = block[k], block[k + 1]
            if not AHEAD:
                one, two = one + zero, two + zero
            first, cross, last = row_of(one, k), row_of(two, k), row_of(two, k + 1)
            scale = 1.0 / (first * last - cross * cross)
            mixed = cross * scale
            here, next_ = rows == k, rows == k + 1
            pair = here | next_
            first_scaled, last_scaled = first * scale, last * scale
            top = one * last_scaled - two * mixed
            low = two * first_scaled - one * mixed
            top = jnp.where(here, -last_scaled, jnp.where(next_, mixed, top))
            low = jnp.where(here, mixed, jnp.where(next_, -first_scaled, low))
            heads = {}
            for j in range(SUBLANES):
                if j in (k, k + 1):
                    continue
                x, y = row_of(block[j], k), row_of(block[j], k + 1)
                heads[j] = (x, y)
                block[j] = jnp.where(pair, 0.0, block[j]) - (top * x + low * y)
            block[k], block[k + 1] = -top, -low
            ratio = cross / first
            top_scale, low_scale = lax.rsqrt(first), lax.rsqrt(last - ratio * cross)
            ratio_scale = ratio * low_scale
            for j in range(k):
                x, y = heads[j]
                lower = y * low_scale - x * ratio_scale
                factor[j] = jnp.where(here, x * top_scale, jnp.where(next_, lower, factor[j]))
            factor[k] = jnp.where(here, top_scale, jnp.where(next_, -ratio_scale, 0.0))
            factor[k + 1] = jnp.where(next_, low_scale, 0.0)
            if AHEAD and not last_group:
                t1 = total([below[k]] + [heads[j][0] * below[j] for j in range(k)])
                t2 = total([below[k + 1]] + [heads[j][1] * below[j] for j in range(k)])
                turned += [t1, t2]
                weighted += [t1 * last_scaled - t2 * mixed, t2 * first_scaled - t1 * mixed]
        inside = (lanes >= pivot) & (lanes < pivot + SUBLANES)
        held = jnp.where(inside, jnp.where(lanes == rows + pivot, 1.0, 0.0), tiles[own])
        spread = [row_of(held, j) for j in range(SUBLANES)]
        result = total([factor[j] * spread[j] for j in range(SUBLANES)])
        out.append(jnp.where(lanes < pivot + SUBLANES, result, 0.0))
        if last_group:
            break
        mixed = total([block[j] * spread[j] for j in range(SUBLANES)])
        mixes = [row_of(mixed, j) for j in range(SUBLANES)]
        if AHEAD:
            following = [
                after[j] - total([turned[m] * row_of(weighted[m], j) for m in range(SUBLANES)])
                for j in range(SUBLANES)
            ]
        columns = [
            [below[j]] + [lane_of(tiles[g], pivot + j) for g in range(own + 2, groups)]
            for j in range(SUBLANES)
        ]
        for g in range(own + 1, groups):
            changes = [columns[j][g - own - 1] * mixes[j] for j in range(SUBLANES)]
            tiles[g] = jnp.where(inside, 0.0, tiles[g]) - total(changes)
        yield
    yield jnp.concatenate(out, axis=0)


def factors_of(*matrices):
    running = [inverse_factor(matrix) for matrix in matrices]
    for _ in range(matrices[0].shape[0] // SUBLANES):
        results = [next(each) for each in running]
    return results


def iterate_kernel(
    high_ref, low_ref, start_ref, own_ref, out_ref, rows_ref, images_ref, gram_ref, factor_ref, joint
):
    rank, tokens = start_ref.shape
    scale = 1.0 / (tokens * joint)
    left, right = slice(0, rank // 2), slice(rank // 2, rank)

    def applied(rows):
        rows_high, rows_low = halves_of(rows)
        return (
            dot_of(rows_high, high_ref[...], 1, 0)
            + dot_of(rows_high, low_ref[...], 1, 0)
            + dot_of(rows_low, high_ref[...], 1, 0)
        )

    def gram_block(rows, images):
        return thrice(rows, images, 1, 1) * scale

    def reduced(factor):
        scaled = exact(factor, gram_ref[left, right], 1, 0)
        return scaled, gram_ref[right, right] - exact(scaled, scaled, 0, 0)

    images = applied(start_ref[...])
    images_ref[...] = images
    gram = gram_block(start_ref[...], images)
    gram_ref[...] = gram
    factor_ref[...] = factors_of(gram[left, left])[0]

    def step(iteration, carry):
        factor = factor_ref[...]
        scaled, rest = reduced(factor)
        first = thrice(factor, images_ref[left, :], 1, 0)
        first_images = applied(first)
        rest_factor, next_factor = factors_of(rest, gram_block(first, first_images))
        remaining = images_ref[right, :] - thrice(scaled, first, 0, 0)
        second = thrice(rest_factor, remaining, 1, 0)
        second_images = applied(second)
        rows_ref[left, :] = first
        rows_ref[right, :] = second
        gram_ref[left, right] = gram_block(first, second_images)
        gram_ref[right, right] = gram_block(second, second_images)
        images_ref[left, :] = first_images
        images_ref[right, :] = second_images
        factor_ref[...] = next_factor
        return carry

    lax.fori_loop(0, ITERS - 1, step, 0)
    rows_high, rows_low = halves_of(rows_ref[...])
    own = own_ref[...]
    loose = (dot_of(rows_high, own, 1, 0) + dot_of(rows_low, own, 1, 0)) * (1.0 / tokens)
    factor = factor_ref[...]
    scaled, rest = reduced(factor)
    first = thrice(factor, loose[left, :], 1, 0)
    out_ref[:, left] = thrice(loose[left, :], factor, 0, 1)
    second = loose[right, :] - thrice(scaled, first, 0, 0)
    out_ref[:, right] = thrice(second, factors_of(rest)[0], 0, 1)


def iterate(high, low, start, own, joint):
    rank, tokens = start.shape

    def kernel(*refs):
        iterate_kernel(*refs, joint)

    return pl.pallas_call(
        kernel,
        out_shape=jax.ShapeDtypeStruct((own.shape[1], rank), jnp.float32),
        in_specs=[pl.BlockSpec(memory_space=pltpu.VMEM)] * 4,
        out_specs=pl.BlockSpec(memory_space=pltpu.VMEM),
        scratch_shapes=[
            pltpu.VMEM((rank, tokens), jnp.float32),
            pltpu.VMEM((rank, tokens), jnp.float32),
            pltpu.VMEM((rank, rank), jnp.float32),
            pltpu.VMEM((rank // 2, rank // 2), jnp.float32),
        ],
        compiler_params=pltpu.CompilerParams(vmem_limit_bytes=40 * 2**20),
    )(high, low, start, own)


def collect_kernel(
    heads,
    hidden_ref,
    gain_ref,
    key_ref,
    value_ref,
    cosine_ref,
    sine_ref,
    basis_ref,
    high_ref,
    low_ref,
    rows_ref,
    own_ref,
    out_ref,
    whole_ref,
    token_sums,
    hidden_rows,
    gain_row,
    key_rows,
    value_rows,
    partial,
    peer_partial,
    squares,
    peer_squares,
    load_sems,
    half_sems,
    swap_sems,
    z_sems,
    x_sems,
    y_sems,
    x_half_sems,
    y_half_sems,
    core_sems,
):
    x, b, z = lax.axis_index("seq"), lax.axis_index("batch"), lax.axis_index("head")
    local, width = peer_partial.shape
    half = width // 2
    rank = whole_ref.shape[1]
    piece = width // 4
    depth = gain_row.shape[1]
    chunks = load_sems.shape[1]
    chunk = depth // chunks
    other_x, other_y = 1 - x, (b + 2) % 4
    partner = b + 1 - 2 * (b % 2)
    x_peer, y_peer, core_peer = (other_x, b, z), (x, other_y, z), (x, partner, z)
    away = pl.ds(pl.multiple_of(other_x * local, local), local)
    mine = pl.ds(pl.multiple_of(x * local, local), local)

    def nearest(turn):
        if turn == 0 or heads != 4:
            return (z + turn) % heads
        side = z // 2
        inner = z + side * (3 - 2 * z)
        place = (1 + inner, 2 - 2 * inner, 3)[turn - 1]
        return 3 * side + (1 - 2 * side) * place

    sources = [nearest(turn) for turn in range(heads)]

    def z_peer(turn):
        return (x, b, sources[turn])

    own_block = whole_ref.at[pl.ds(pl.multiple_of(z * width, width), width), :]
    basis_load = pltpu.make_async_copy(basis_ref, own_block, half_sems.at[2, 0])
    gain_load = pltpu.make_async_copy(gain_ref, gain_row, half_sems.at[2, 1])

    def span(c):
        return pl.ds(c * chunk, chunk)

    def token_load(kind, area, c):
        return pltpu.make_async_copy(
            hidden_ref.at[area, span(c)], hidden_rows.at[area, span(c)], half_sems.at[kind, c]
        )

    away_loads = [token_load(0, away, c) for c in range(chunks)]
    mine_loads = [token_load(1, mine, c) for c in range(chunks)]
    key_loads = [
        pltpu.make_async_copy(key_ref.at[span(c), :], key_rows.at[span(c), :], load_sems.at[0, c])
        for c in range(chunks)
    ]
    value_loads = [
        pltpu.make_async_copy(
            value_ref.at[span(c), :], value_rows.at[span(c), :], load_sems.at[1, c]
        )
        for c in range(chunks)
    ]
    basis_load.start()
    gain_load.start()
    loads = [load for pair in zip(away_loads, key_loads) for load in pair]
    loads += value_loads + mine_loads
    waiting = list(loads)

    def issue():
        if waiting:
            waiting.pop(0).start()

    def ready(load):
        load.wait()
        issue()

    for _ in range(6):
        issue()

    barrier = pltpu.get_barrier_semaphore()
    peers = [x_peer, y_peer, core_peer] + [z_peer(d) for d in range(1, heads)]
    for peer in peers:
        pl.semaphore_signal(barrier, inc=1, device_id=peer, device_id_type=pl.DeviceIdType.MESH)
    pl.semaphore_wait(barrier, len(peers))

    def copy(source, target, sems, peer):
        return pltpu.make_async_remote_copy(
            src_ref=source,
            dst_ref=target,
            send_sem=sems.at[0],
            recv_sem=sems.at[1],
            device_id=peer,
            device_id_type=pl.DeviceIdType.MESH,
        )

    def region(xs, bs, zs, start=0, size=width):
        row = pl.multiple_of((xs * 4 + bs) * local, local)
        column = pl.multiple_of(zs * width + start, half)
        return out_ref.at[pl.ds(row, local), pl.ds(column, size)]

    def piece_of(bs, zs):
        row = pl.multiple_of(zs * width + bs * piece, piece)
        return whole_ref.at[pl.ds(row, piece), :]

    started = []

    def send(area, sems, peer):
        going = copy(area, area, sems, peer)
        going.start()
        started.append(going)

    def arrive(area, sems, peer):
        copy(area, area, sems, peer).wait_recv()

    def send_z(area, kind, turn):
        going = pltpu.make_async_remote_copy(
            src_ref=area,
            dst_ref=area,
            send_sem=z_sems.at[kind, sources[turn], 0],
            recv_sem=z_sems.at[kind, z, 1],
            device_id=z_peer(turn),
            device_id_type=pl.DeviceIdType.MESH,
        )
        going.start()
        started.append(going)

    def spread(kind, area, middle, turn):
        s = sources[turn]
        own = area(x, b, s)
        if turn:
            arrive(own, z_sems.at[kind, s], z_peer(turn))
        send(own, x_sems.at[kind, turn], x_peer)
        send(own, y_sems.at[kind, turn], y_peer)
        send(own, core_sems.at[kind, turn, 0], core_peer)

    def relay(kind, area, middle, turn):
        s = sources[turn]
        arrive(area(other_x, b, s), x_sems.at[kind, turn], x_peer)
        beyond = area(other_x, b, s, middle, middle) if middle else area(other_x, b, s)
        send(beyond, y_half_sems.at[kind, turn], y_peer)
        send(area(other_x, b, s), core_sems.at[kind, turn, 1], core_peer)
        arrive(area(x, other_y, s), y_sems.at[kind, turn], y_peer)
        if middle:
            send(area(x, other_y, s, 0, middle), x_half_sems.at[kind, turn], x_peer)
        send(area(x, other_y, s), core_sems.at[kind, turn, 2], core_peer)

    def finish(kind, area, middle, turn):
        s = sources[turn]
        if middle:
            arrive(area(other_x, other_y, s, 0, middle), x_half_sems.at[kind, turn], x_peer)
        beyond = area(other_x, other_y, s, middle, middle) if middle else area(other_x, other_y, s)
        arrive(beyond, y_half_sems.at[kind, turn], y_peer)
        send(area(other_x, other_y, s), core_sems.at[kind, turn, 3], core_peer)

    far = (partner + 2) % 4

    def gathered(kind, area, middle, turn):
        places = [(x, partner), (other_x, partner), (x, far), (other_x, far)]
        for place, (xs, bs) in enumerate(places):
            arrive(area(xs, bs, sources[turn]), core_sems.at[kind, turn, place], core_peer)

    def spread_basis(turn):
        own = piece_of(b, sources[turn])
        arrive(own, z_sems.at[1, sources[turn]], z_peer(turn))
        send(own, y_sems.at[1, turn], y_peer)
        send(own, core_sems.at[1, turn, 0], core_peer)

    def relay_basis(turn):
        other = piece_of(other_y, sources[turn])
        arrive(other, y_sems.at[1, turn], y_peer)
        send(other, core_sems.at[1, turn, 1], core_peer)

    def gathered_basis(turn):
        arrive(piece_of(partner, sources[turn]), core_sems.at[1, turn, 0], core_peer)
        arrive(piece_of(far, sources[turn]), core_sems.at[1, turn, 1], core_peer)

    joint = [(0, region, half, turn) for turn in range(heads)]
    others = range(1, heads)
    tokens, strip = out_ref.shape[0], 256

    def accumulate(turn):
        place = pl.multiple_of(sources[turn] * width, width)
        block = out_ref[:, pl.ds(place, width)]
        basis_high, basis_low = halves_of(whole_ref[pl.ds(place, width), :])
        for start in range(0, tokens, strip):
            area = slice(start, start + strip)
            part = out_ref[area, pl.ds(place, width)]
            product = dot_of(block, part, 1, 1)
            rows = dot_of(basis_high, part, 0, 1) + dot_of(basis_low, part, 0, 1)
            if turn:
                product = product + token_sums[:, area]
                rows = rows + rows_ref[:, area]
            rows_ref[:, area] = rows
            if turn < heads - 1:
                token_sums[:, area] = product
            else:
                high, low = halves_of(product * (1.0 / tokens))
                high_ref[:, area] = high
                low_ref[:, area] = low
            if turn == 0:
                own_ref[area, :] = part

    basis_load.wait()
    for turn in range(1, heads):
        send_z(piece_of(b, z), 1, turn)

    def prepare(area, c, total):
        widened = hidden_rows[area, span(c)].astype(jnp.float32)
        scaled = (widened * gain_row[:, span(c)]).astype(jnp.bfloat16)
        hidden_rows[area, span(c)] = scaled
        squared = widened * widened
        for start in range(0, chunk, LANES):
            total = total + squared[:, start : start + LANES]
        return scaled, total

    def across(total):
        ones = jnp.ones((SUBLANES, LANES), jnp.float32)
        return exact(ones, total, 1, 1)

    def swap(source_ref, target_ref, index):
        going = copy(source_ref, target_ref, swap_sems.at[index], x_peer)
        going.start()
        return going

    gain_load.wait()
    away_total = jnp.zeros((local, LANES), jnp.float32)
    sums = jnp.zeros((local, half), jnp.float32)
    for c in range(chunks):
        ready(away_loads[c])
        scaled, away_total = prepare(away, c, away_total)
        ready(key_loads[c])
        sums = sums + dot_of(scaled, key_rows[span(c), :], 1, 0)
    partial[:, :half] = sums
    squares[...] = across(away_total)
    swaps = [
        swap(squares, peer_squares, 0),
        swap(partial.at[:, pl.ds(0, half)], peer_partial.at[:, pl.ds(0, half)], 1),
    ]
    sums = jnp.zeros((local, half), jnp.float32)
    for c in range(chunks):
        ready(value_loads[c])
        sums = sums + dot_of(hidden_rows[away, span(c)], value_rows[span(c), :], 1, 0)
    partial[:, half:] = sums
    swaps.append(swap(partial.at[:, pl.ds(half, half)], peer_partial.at[:, pl.ds(half, half)], 2))
    mine_total = jnp.zeros((local, LANES), jnp.float32)
    key_sums = jnp.zeros((local, half), jnp.float32)
    value_sums = jnp.zeros((local, half), jnp.float32)
    for c in range(chunks):
        ready(mine_loads[c])
        scaled, mine_total = prepare(mine, c, mine_total)
        key_sums = key_sums + dot_of(scaled, key_rows[span(c), :], 1, 0)
        value_sums = value_sums + dot_of(scaled, value_rows[span(c), :], 1, 0)
    own_squares = across(mine_total)
    for turn in others:
        spread_basis(turn)

    swaps[0].wait()
    eighths = jnp.full((SUBLANES, LANES), 1.0 / SUBLANES, jnp.float32)
    inverse_scale = lax.rsqrt(exact(own_squares + peer_squares[...], eighths, 0, 0) / D + EPSILON)
    row = pl.multiple_of((x * 4 + b) * local, local)
    swaps[1].wait()
    for g in range(half // HEAD_DIM):
        spot = slice(g * HEAD_DIM, (g + 1) * HEAD_DIM)
        key = (key_sums[:, spot] + peer_partial[:, spot]) * inverse_scale
        turned = key * cosine_ref[...] + pltpu.roll(key, HEAD_DIM // 2, 1) * sine_ref[...]
        column = pl.multiple_of(z * width + 2 * g * HEAD_DIM, HEAD_DIM)
        out_ref[pl.ds(row, local), pl.ds(column, HEAD_DIM)] = turned.astype(jnp.bfloat16)
    swaps[2].wait()
    for g in range(half // HEAD_DIM):
        spot = slice(g * HEAD_DIM, (g + 1) * HEAD_DIM)
        there = slice(half + g * HEAD_DIM, half + (g + 1) * HEAD_DIM)
        value = (value_sums[:, spot] + peer_partial[:, there]) * inverse_scale
        column = pl.multiple_of(z * width + (2 * g + 1) * HEAD_DIM, HEAD_DIM)
        out_ref[pl.ds(row, local), pl.ds(column, HEAD_DIM)] = value.astype(jnp.bfloat16)

    for turn in range(1, heads):
        send_z(region(x, b, z), 0, turn)
    for turn in range(len(joint) + 2):
        if turn < len(joint):
            spread(*joint[turn])
        if 1 <= turn < len(joint) + 1:
            relay(*joint[turn - 1])
        if turn == len(joint) + 1:
            for other in others:
                gathered_basis(other)
            for early in range(1, len(joint) - 2):
                gathered(*joint[early])
                accumulate(early)
        if turn >= 2:
            finish(*joint[turn - 2])
        if turn == 1:
            for other in others:
                relay_basis(other)
        if turn == 3:
            gathered(*joint[0])
            accumulate(0)
    for turn in range(max(1, len(joint) - 2), len(joint)):
        gathered(*joint[turn])
        accumulate(turn)
    for going in started:
        going.wait_send()


def collect(hidden_rows, gain, key_weight, value_weight, positions, basis, heads, tokens):
    depth = hidden_rows.shape[1]
    local = positions.shape[0]
    half, width = key_weight.shape[1], key_weight.shape[1] + value_weight.shape[1]
    half_width = HEAD_DIM // 2
    chunks = 4
    frequency = jnp.exp(
        jnp.arange(half_width, dtype=jnp.float32) * (-math.log(ROTARY_BASE) / half_width)
    )
    angles = positions.astype(jnp.float32)[:, None] * frequency[None, :]
    cosine, sine = jnp.cos(angles), jnp.sin(angles)
    dma = pltpu.SemaphoreType.DMA
    anywhere = pl.BlockSpec(memory_space=pltpu.HBM)
    inside = pl.BlockSpec(memory_space=pltpu.VMEM)
    return pl.pallas_call(
        functools.partial(collect_kernel, heads),
        out_shape=(
            jax.ShapeDtypeStruct((tokens, tokens), jnp.bfloat16),
            jax.ShapeDtypeStruct((tokens, tokens), jnp.bfloat16),
            jax.ShapeDtypeStruct((basis.shape[1], tokens), jnp.float32),
            jax.ShapeDtypeStruct((tokens, width), jnp.bfloat16),
        ),
        in_specs=[anywhere] * 4 + [inside] * 2 + [anywhere],
        out_specs=(inside,) * 4,
        scratch_shapes=[
            pltpu.VMEM((tokens, heads * width), jnp.bfloat16),
            pltpu.VMEM((heads * width, basis.shape[1]), jnp.float32),
            pltpu.VMEM((tokens, tokens), jnp.float32),
            pltpu.VMEM(hidden_rows.shape, jnp.bfloat16),
            pltpu.VMEM((1, depth), jnp.float32),
            pltpu.VMEM(key_weight.shape, jnp.bfloat16),
            pltpu.VMEM(value_weight.shape, jnp.bfloat16),
            pltpu.VMEM((local, width), jnp.float32),
            pltpu.VMEM((local, width), jnp.float32),
            pltpu.VMEM((SUBLANES, local), jnp.float32),
            pltpu.VMEM((SUBLANES, local), jnp.float32),
            dma((2, chunks)),
            dma((3, chunks)),
            dma((3, 2)),
            dma((2, heads, 2)),
            dma((2, heads, 2)),
            dma((2, heads, 2)),
            dma((2, heads, 2)),
            dma((2, heads, 2)),
            dma((2, heads, 4, 2)),
        ],
        compiler_params=pltpu.CompilerParams(
            collective_id=0, has_side_effects=True, vmem_limit_bytes=45 * 2**20
        ),
    )(
        hidden_rows,
        pltpu.with_memory_space_constraint(gain[None, :], pltpu.HBM),
        key_weight,
        value_weight,
        jnp.concatenate([cosine, cosine], axis=1),
        jnp.concatenate([-sine, sine], axis=1),
        pltpu.with_memory_space_constraint(basis, pltpu.HBM),
    )


def body(hidden, gain, key_weight, value_weight, positions, initial_basis):
    hidden_rows = hidden[0]
    local_tokens = positions.shape[1]
    seqs, batches, heads = lax.axis_size("seq"), lax.axis_size("batch"), lax.axis_size("head")
    tokens = local_tokens * seqs * batches
    if seqs == 2 and batches == 4 and tokens <= initial_basis.shape[0] * heads:
        collected = collect(
            hidden_rows,
            gain,
            key_weight,
            value_weight,
            positions[0],
            initial_basis,
            heads,
            tokens,
        )
        return iterate(*collected, initial_basis.shape[0] * heads)
    widened = hidden_rows.astype(jnp.float32)
    scaled = (widened * gain).astype(jnp.bfloat16)
    local_squares = jnp.sum(widened * widened, axis=1)
    key_columns = key_weight.shape[1]
    weights = jnp.concatenate([key_weight, value_weight], axis=1)
    own_squares = total_squares(local_squares, local_tokens)
    projected = lax.psum_scatter(
        jnp.dot(scaled, weights, preferred_element_type=jnp.float32),
        "seq",
        scatter_dimension=0,
        tiled=True,
    )
    inverse_scale = lax.rsqrt(own_squares / D + EPSILON)
    projected = projected * inverse_scale[:, None]
    key_rows = rotary(projected[:, :key_columns].reshape(local_tokens, -1, HEAD_DIM), positions[0])
    value_rows = projected[:, key_columns:].reshape(local_tokens, -1, HEAD_DIM)
    joint_rows = (
        jnp.stack([key_rows, value_rows], axis=2).reshape(local_tokens, -1).astype(jnp.bfloat16)
    )
    partial_value = lax.dot_general(
        joint_rows,
        lax.all_gather(joint_rows, "head", axis=1, tiled=True),
        (((0,), (0,)), ((), ())),
        preferred_element_type=jnp.float32,
    )
    token_total = local_tokens * lax.axis_size("seq") * lax.axis_size("batch")
    basis_block = initial_basis
    covariance = lax.psum(partial_value, ("seq", "batch")) / token_total
    for iteration in range(ITERS):
        whole_basis = whole_of(basis_block)
        images = jnp.dot(
            covariance,
            whole_basis,
            precision=lax.Precision.HIGHEST,
            preferred_element_type=jnp.float32,
        )
        gram_matrix = lax.psum(gram_of(images), "head") / whole_basis.shape[0]
        basis_block = orthonormal(images, gram_matrix)
    return basis_block


def solution(mesh):
    return jax.shard_map(
        body,
        mesh=mesh,
        in_specs=(
            P("batch", None, "seq"),
            P("seq"),
            P("seq", "head"),
            P("seq", "head"),
            P("batch", "seq"),
            P("head", None),
        ),
        out_specs=P("head", None),
        check_vma=False,
    )
```

```python
import functools
import math

import jax
import jax.numpy as jnp
from jax import lax
from jax.experimental import pallas as pl
from jax.experimental.pallas import tpu as pltpu
from jax.sharding import PartitionSpec as P

D = 16384
HEAD_DIM = 128
ITERS = 4


EPSILON = 1e-05
ROTARY_BASE = 500000.0


def rotary(head_rows, position_row):
    half_width = head_rows.shape[-1] // 2
    index_row = jnp.arange(half_width, dtype=jnp.float32)
    frequency = jnp.exp(index_row * (-math.log(ROTARY_BASE) / half_width))
    angles = position_row.astype(jnp.float32)[:, None] * frequency[None, :]
    cosine = jnp.cos(angles)[:, None, :]
    sine_part = jnp.sin(angles)[:, None, :]
    first_half = head_rows[..., :half_width]
    second_half = head_rows[..., half_width:]
    return jnp.concatenate(
        [
            first_half * cosine - second_half * sine_part,
            second_half * cosine + first_half * sine_part,
        ],
        axis=-1,
    )


def whole_of(basis_block):
    return lax.all_gather(basis_block, "head", axis=0, tiled=True)


def total_squares(local_squares, local_tokens):
    all_squares = lax.psum(local_squares, "seq")
    return lax.dynamic_slice_in_dim(all_squares, lax.axis_index("seq") * local_tokens, local_tokens)


def gram_of(images):
    return lax.dot_general(
        images,
        images,
        (((0,), (0,)), ((), ())),
        precision=lax.Precision.HIGHEST,
        preferred_element_type=jnp.float32,
    )


def orthonormal(images, gram_matrix):
    factor = jnp.linalg.cholesky(gram_matrix)
    return lax.linalg.triangular_solve(
        factor, images, left_side=False, lower=True, transpose_a=True
    )


LANES = 128
SUBLANES = 8
AHEAD = True


def dot_of(left, right, left_axis, right_axis, precision=None):
    return lax.dot_general(
        left,
        right,
        (((left_axis,), (right_axis,)), ((), ())),
        precision=precision,
        preferred_element_type=jnp.float32,
    )


def exact(left, right, left_axis, right_axis):
    return dot_of(left, right, left_axis, right_axis, lax.Precision.HIGHEST)


def halves_of(value):
    high = value.astype(jnp.bfloat16)
    return high, (value - high.astype(jnp.float32)).astype(jnp.bfloat16)


def thrice(left, right, left_axis, right_axis):
    left_high, left_low = halves_of(left)
    right_high, right_low = halves_of(right)
    return (
        dot_of(left_high, right_high, left_axis, right_axis)
        + dot_of(left_high, right_low, left_axis, right_axis)
        + dot_of(left_low, right_high, left_axis, right_axis)
    )


def inverse_factor(matrix):
    size = matrix.shape[0]
    shape = (SUBLANES, size)
    rows = lax.broadcasted_iota(jnp.int32, shape, 0)
    lanes = lax.broadcasted_iota(jnp.int32, shape, 1)
    groups = size // SUBLANES
    tiles = [matrix[SUBLANES * g : SUBLANES * (g + 1)] for g in range(groups)]
    out = []

    def row_of(value, at):
        return jnp.broadcast_to(value[at : at + 1, :], shape)

    def lane_of(value, at):
        return jnp.broadcast_to(value[:, at : at + 1], shape)

    def total(terms):
        while len(terms) > 1:
            pairs = [terms[i] + terms[i + 1] for i in range(0, len(terms) - 1, 2)]
            terms = pairs + terms[2 * len(pairs) :]
        return terms[0]

    zero = jnp.zeros(shape, jnp.float32)
    for own in range(groups):
        pivot = own * SUBLANES
        block = [lane_of(tiles[own], pivot + j) for j in range(SUBLANES)]
        if AHEAD and own:
            block = following
        last_group = own + 1 == groups
        if not last_group:
            below = [lane_of(tiles[own + 1], pivot + j) for j in range(SUBLANES)]
            if AHEAD:
                after = [lane_of(tiles[own + 1], pivot + SUBLANES + j) for j in range(SUBLANES)]
        factor = [None] * SUBLANES
        turned, weighted = [], []
        for k in range(0, SUBLANES, 2):
            one, two = block[k], block[k + 1]
            if not AHEAD:
                one, two = one + zero, two + zero
            first, cross, last = row_of(one, k), row_of(two, k), row_of(two, k + 1)
            scale = 1.0 / (first * last - cross * cross)
            mixed = cross * scale
            here, next_ = rows == k, rows == k + 1
            pair = here | next_
            first_scaled, last_scaled = first * scale, last * scale
            top = one * last_scaled - two * mixed
            low = two * first_scaled - one * mixed
            top = jnp.where(here, -last_scaled, jnp.where(next_, mixed, top))
            low = jnp.where(here, mixed, jnp.where(next_, -first_scaled, low))
            heads = {}
            for j in range(SUBLANES):
                if j in (k, k + 1):
                    continue
                x, y = row_of(block[j], k), row_of(block[j], k + 1)
                heads[j] = (x, y)
                block[j] = jnp.where(pair, 0.0, block[j]) - (top * x + low * y)
            block[k], block[k + 1] = -top, -low
            ratio = cross / first
            top_scale, low_scale = lax.rsqrt(first), lax.rsqrt(last - ratio * cross)
            ratio_scale = ratio * low_scale
            for j in range(k):
                x, y = heads[j]
                lower = y * low_scale - x * ratio_scale
                factor[j] = jnp.where(here, x * top_scale, jnp.where(next_, lower, factor[j]))
            factor[k] = jnp.where(here, top_scale, jnp.where(next_, -ratio_scale, 0.0))
            factor[k + 1] = jnp.where(next_, low_scale, 0.0)
            if AHEAD and not last_group:
                t1 = total([below[k]] + [heads[j][0] * below[j] for j in range(k)])
                t2 = total([below[k + 1]] + [heads[j][1] * below[j] for j in range(k)])
                turned += [t1, t2]
                weighted += [t1 * last_scaled - t2 * mixed, t2 * first_scaled - t1 * mixed]
        inside = (lanes >= pivot) & (lanes < pivot + SUBLANES)
        held = jnp.where(inside, jnp.where(lanes == rows + pivot, 1.0, 0.0), tiles[own])
        spread = [row_of(held, j) for j in range(SUBLANES)]
        result = total([factor[j] * spread[j] for j in range(SUBLANES)])
        out.append(jnp.where(lanes < pivot + SUBLANES, result, 0.0))
        if last_group:
            break
        mixed = total([block[j] * spread[j] for j in range(SUBLANES)])
        mixes = [row_of(mixed, j) for j in range(SUBLANES)]
        if AHEAD:
            following = [
                after[j] - total([turned[m] * row_of(weighted[m], j) for m in range(SUBLANES)])
                for j in range(SUBLANES)
            ]
        columns = [
            [below[j]] + [lane_of(tiles[g], pivot + j) for g in range(own + 2, groups)]
            for j in range(SUBLANES)
        ]
        for g in range(own + 1, groups):
            changes = [columns[j][g - own - 1] * mixes[j] for j in range(SUBLANES)]
            tiles[g] = jnp.where(inside, 0.0, tiles[g]) - total(changes)
        yield
    yield jnp.concatenate(out, axis=0)


def factors_of(*matrices):
    running = [inverse_factor(matrix) for matrix in matrices]
    for _ in range(matrices[0].shape[0] // SUBLANES):
        results = [next(each) for each in running]
    return results


def iterate_kernel(
    high_ref, low_ref, start_ref, own_ref, out_ref, rows_ref, images_ref, gram_ref, factor_ref, joint
):
    rank, tokens = start_ref.shape
    scale = 1.0 / (tokens * joint)
    left, right = slice(0, rank // 2), slice(rank // 2, rank)

    def applied(rows):
        rows_high, rows_low = halves_of(rows)
        return (
            dot_of(rows_high, high_ref[...], 1, 0)
            + dot_of(rows_high, low_ref[...], 1, 0)
            + dot_of(rows_low, high_ref[...], 1, 0)
        )

    def gram_block(rows, images):
        return thrice(rows, images, 1, 1) * scale

    def reduced(factor):
        scaled = exact(factor, gram_ref[left, right], 1, 0)
        return scaled, gram_ref[right, right] - exact(scaled, scaled, 0, 0)

    images = applied(start_ref[...])
    images_ref[...] = images
    gram = gram_block(start_ref[...], images)
    gram_ref[...] = gram
    factor_ref[...] = factors_of(gram[left, left])[0]

    def step(iteration, carry):
        factor = factor_ref[...]
        scaled, rest = reduced(factor)
        first = thrice(factor, images_ref[left, :], 1, 0)
        first_images = applied(first)
        rest_factor, next_factor = factors_of(rest, gram_block(first, first_images))
        remaining = images_ref[right, :] - thrice(scaled, first, 0, 0)
        second = thrice(rest_factor, remaining, 1, 0)
        second_images = applied(second)
        rows_ref[left, :] = first
        rows_ref[right, :] = second
        gram_ref[left, right] = gram_block(first, second_images)
        gram_ref[right, right] = gram_block(second, second_images)
        images_ref[left, :] = first_images
        images_ref[right, :] = second_images
        factor_ref[...] = next_factor
        return carry

    lax.fori_loop(0, ITERS - 1, step, 0)
    rows_high, rows_low = halves_of(rows_ref[...])
    own = own_ref[...]
    loose = (dot_of(rows_high, own, 1, 0) + dot_of(rows_low, own, 1, 0)) * (1.0 / tokens)
    factor = factor_ref[...]
    scaled, rest = reduced(factor)
    first = thrice(factor, loose[left, :], 1, 0)
    out_ref[:, left] = thrice(loose[left, :], factor, 0, 1)
    second = loose[right, :] - thrice(scaled, first, 0, 0)
    out_ref[:, right] = thrice(second, factors_of(rest)[0], 0, 1)


def iterate(high, low, start, own, joint):
    rank, tokens = start.shape

    def kernel(*refs):
        iterate_kernel(*refs, joint)

    return pl.pallas_call(
        kernel,
        out_shape=jax.ShapeDtypeStruct((own.shape[1], rank), jnp.float32),
        in_specs=[pl.BlockSpec(memory_space=pltpu.VMEM)] * 4,
        out_specs=pl.BlockSpec(memory_space=pltpu.VMEM),
        scratch_shapes=[
            pltpu.VMEM((rank, tokens), jnp.float32),
            pltpu.VMEM((rank, tokens), jnp.float32),
            pltpu.VMEM((rank, rank), jnp.float32),
            pltpu.VMEM((rank // 2, rank // 2), jnp.float32),
        ],
        compiler_params=pltpu.CompilerParams(vmem_limit_bytes=40 * 2**20),
    )(high, low, start, own)


def collect_kernel(
    heads,
    hidden_ref,
    gain_ref,
    key_ref,
    value_ref,
    cosine_ref,
    sine_ref,
    basis_ref,
    high_ref,
    low_ref,
    rows_ref,
    own_ref,
    out_ref,
    whole_ref,
    token_sums,
    hidden_rows,
    gain_row,
    key_rows,
    value_rows,
    partial,
    peer_partial,
    squares,
    peer_squares,
    load_sems,
    half_sems,
    swap_sems,
    z_sems,
    x_sems,
    y_sems,
    x_half_sems,
    y_half_sems,
    core_sems,
):
    x, b, z = lax.axis_index("seq"), lax.axis_index("batch"), lax.axis_index("head")
    local, width = peer_partial.shape
    half = width // 2
    rank = whole_ref.shape[1]
    piece = width // 4
    depth = gain_row.shape[1]
    chunks = load_sems.shape[1]
    chunk = depth // chunks
    other_x, other_y = 1 - x, (b + 2) % 4
    partner = b + 1 - 2 * (b % 2)
    x_peer, y_peer, core_peer = (other_x, b, z), (x, other_y, z), (x, partner, z)
    away = pl.ds(pl.multiple_of(other_x * local, local), local)
    mine = pl.ds(pl.multiple_of(x * local, local), local)

    def nearest(turn):
        if turn == 0 or heads != 4:
            return (z + turn) % heads
        side = z // 2
        inner = z + side * (3 - 2 * z)
        place = (1 + inner, 2 - 2 * inner, 3)[turn - 1]
        return 3 * side + (1 - 2 * side) * place

    sources = [nearest(turn) for turn in range(heads)]

    def z_peer(turn):
        return (x, b, sources[turn])

    own_block = whole_ref.at[pl.ds(pl.multiple_of(z * width, width), width), :]
    basis_load = pltpu.make_async_copy(basis_ref, own_block, half_sems.at[2, 0])
    gain_load = pltpu.make_async_copy(gain_ref, gain_row, half_sems.at[2, 1])

    def span(c):
        return pl.ds(c * chunk, chunk)

    def token_load(kind, area, c):
        return pltpu.make_async_copy(
            hidden_ref.at[area, span(c)], hidden_rows.at[area, span(c)], half_sems.at[kind, c]
        )

    away_loads = [token_load(0, away, c) for c in range(chunks)]
    mine_loads = [token_load(1, mine, c) for c in range(chunks)]
    key_loads = [
        pltpu.make_async_copy(key_ref.at[span(c), :], key_rows.at[span(c), :], load_sems.at[0, c])
        for c in range(chunks)
    ]
    value_loads = [
        pltpu.make_async_copy(
            value_ref.at[span(c), :], value_rows.at[span(c), :], load_sems.at[1, c]
        )
        for c in range(chunks)
    ]
    basis_load.start()
    gain_load.start()
    loads = [load for pair in zip(away_loads, key_loads) for load in pair]
    loads += value_loads + mine_loads
    waiting = list(loads)

    def issue():
        if waiting:
            waiting.pop(0).start()

    def ready(load):
        load.wait()
        issue()

    for _ in range(4):
        issue()

    barrier = pltpu.get_barrier_semaphore()
    peers = [x_peer, y_peer, core_peer] + [z_peer(d) for d in range(1, heads)]
    for peer in peers:
        pl.semaphore_signal(barrier, inc=1, device_id=peer, device_id_type=pl.DeviceIdType.MESH)
    pl.semaphore_wait(barrier, len(peers))

    def copy(source, target, sems, peer):
        return pltpu.make_async_remote_copy(
            src_ref=source,
            dst_ref=target,
            send_sem=sems.at[0],
            recv_sem=sems.at[1],
            device_id=peer,
            device_id_type=pl.DeviceIdType.MESH,
        )

    def region(xs, bs, zs, start=0, size=width):
        row = pl.multiple_of((xs * 4 + bs) * local, local)
        column = pl.multiple_of(zs * width + start, half)
        return out_ref.at[pl.ds(row, local), pl.ds(column, size)]

    def piece_of(bs, zs):
        row = pl.multiple_of(zs * width + bs * piece, piece)
        return whole_ref.at[pl.ds(row, piece), :]

    started = []

    def send(area, sems, peer):
        going = copy(area, area, sems, peer)
        going.start()
        started.append(going)

    def arrive(area, sems, peer):
        copy(area, area, sems, peer).wait_recv()

    def send_z(area, kind, turn):
        going = pltpu.make_async_remote_copy(
            src_ref=area,
            dst_ref=area,
            send_sem=z_sems.at[kind, sources[turn], 0],
            recv_sem=z_sems.at[kind, z, 1],
            device_id=z_peer(turn),
            device_id_type=pl.DeviceIdType.MESH,
        )
        going.start()
        started.append(going)

    def spread(kind, area, middle, turn):
        s = sources[turn]
        own = area(x, b, s)
        if turn:
            arrive(own, z_sems.at[kind, s], z_peer(turn))
        send(own, x_sems.at[kind, turn], x_peer)
        send(own, y_sems.at[kind, turn], y_peer)
        send(own, core_sems.at[kind, turn, 0], core_peer)

    def relay(kind, area, middle, turn):
        s = sources[turn]
        arrive(area(other_x, b, s), x_sems.at[kind, turn], x_peer)
        beyond = area(other_x, b, s, middle, middle) if middle else area(other_x, b, s)
        send(beyond, y_half_sems.at[kind, turn], y_peer)
        send(area(other_x, b, s), core_sems.at[kind, turn, 1], core_peer)
        arrive(area(x, other_y, s), y_sems.at[kind, turn], y_peer)
        if middle:
            send(area(x, other_y, s, 0, middle), x_half_sems.at[kind, turn], x_peer)
        send(area(x, other_y, s), core_sems.at[kind, turn, 2], core_peer)

    def finish(kind, area, middle, turn):
        s = sources[turn]
        if middle:
            arrive(area(other_x, other_y, s, 0, middle), x_half_sems.at[kind, turn], x_peer)
        beyond = area(other_x, other_y, s, middle, middle) if middle else area(other_x, other_y, s)
        arrive(beyond, y_half_sems.at[kind, turn], y_peer)
        send(area(other_x, other_y, s), core_sems.at[kind, turn, 3], core_peer)

    far = (partner + 2) % 4

    def gathered(kind, area, middle, turn):
        places = [(x, partner), (other_x, partner), (x, far), (other_x, far)]
        for place, (xs, bs) in enumerate(places):
            arrive(area(xs, bs, sources[turn]), core_sems.at[kind, turn, place], core_peer)

    def spread_basis(turn):
        own = piece_of(b, sources[turn])
        arrive(own, z_sems.at[1, sources[turn]], z_peer(turn))
        send(own, y_sems.at[1, turn], y_peer)
        send(own, core_sems.at[1, turn, 0], core_peer)

    def relay_basis(turn):
        other = piece_of(other_y, sources[turn])
        arrive(other, y_sems.at[1, turn], y_peer)
        send(other, core_sems.at[1, turn, 1], core_peer)

    def gathered_basis(turn):
        arrive(piece_of(partner, sources[turn]), core_sems.at[1, turn, 0], core_peer)
        arrive(piece_of(far, sources[turn]), core_sems.at[1, turn, 1], core_peer)

    joint = [(0, region, half, turn) for turn in range(heads)]
    others = range(1, heads)
    tokens, strip = out_ref.shape[0], 256

    def accumulate(turn):
        place = pl.multiple_of(sources[turn] * width, width)
        block = out_ref[:, pl.ds(place, width)]
        basis_high, basis_low = halves_of(whole_ref[pl.ds(place, width), :])
        for start in range(0, tokens, strip):
            area = slice(start, start + strip)
            part = out_ref[area, pl.ds(place, width)]
            product = dot_of(block, part, 1, 1)
            rows = dot_of(basis_high, part, 0, 1) + dot_of(basis_low, part, 0, 1)
            if turn:
                product = product + token_sums[:, area]
                rows = rows + rows_ref[:, area]
            rows_ref[:, area] = rows
            if turn < heads - 1:
                token_sums[:, area] = product
            else:
                high, low = halves_of(product * (1.0 / tokens))
                high_ref[:, area] = high
                low_ref[:, area] = low
            if turn == 0:
                own_ref[area, :] = part

    basis_load.wait()
    for turn in range(1, heads):
        send_z(piece_of(b, z), 1, turn)

    def prepare(area, c, total):
        widened = hidden_rows[area, span(c)].astype(jnp.float32)
        scaled = (widened * gain_row[:, span(c)]).astype(jnp.bfloat16)
        hidden_rows[area, span(c)] = scaled
        squared = widened * widened
        for start in range(0, chunk, LANES):
            total = total + squared[:, start : start + LANES]
        return scaled, total

    def across(total):
        ones = jnp.ones((SUBLANES, LANES), jnp.float32)
        return exact(ones, total, 1, 1)

    def swap(source_ref, target_ref, index):
        going = copy(source_ref, target_ref, swap_sems.at[index], x_peer)
        going.start()
        return going

    gain_load.wait()
    away_total = jnp.zeros((local, LANES), jnp.float32)
    sums = jnp.zeros((local, half), jnp.float32)
    for c in range(chunks):
        ready(away_loads[c])
        scaled, away_total = prepare(away, c, away_total)
        ready(key_loads[c])
        sums = sums + dot_of(scaled, key_rows[span(c), :], 1, 0)
    partial[:, :half] = sums
    squares[...] = across(away_total)
    swaps = [
        swap(squares, peer_squares, 0),
        swap(partial.at[:, pl.ds(0, half)], peer_partial.at[:, pl.ds(0, half)], 1),
    ]
    sums = jnp.zeros((local, half), jnp.float32)
    for c in range(chunks):
        ready(value_loads[c])
        sums = sums + dot_of(hidden_rows[away, span(c)], value_rows[span(c), :], 1, 0)
    partial[:, half:] = sums
    swaps.append(swap(partial.at[:, pl.ds(half, half)], peer_partial.at[:, pl.ds(half, half)], 2))
    mine_total = jnp.zeros((local, LANES), jnp.float32)
    key_sums = jnp.zeros((local, half), jnp.float32)
    value_sums = jnp.zeros((local, half), jnp.float32)
    for c in range(chunks):
        ready(mine_loads[c])
        scaled, mine_total = prepare(mine, c, mine_total)
        key_sums = key_sums + dot_of(scaled, key_rows[span(c), :], 1, 0)
        value_sums = value_sums + dot_of(scaled, value_rows[span(c), :], 1, 0)
    own_squares = across(mine_total)

    swaps[0].wait()
    eighths = jnp.full((SUBLANES, LANES), 1.0 / SUBLANES, jnp.float32)
    inverse_scale = lax.rsqrt(exact(own_squares + peer_squares[...], eighths, 0, 0) / D + EPSILON)
    row = pl.multiple_of((x * 4 + b) * local, local)
    swaps[1].wait()
    for g in range(half // HEAD_DIM):
        spot = slice(g * HEAD_DIM, (g + 1) * HEAD_DIM)
        key = (key_sums[:, spot] + peer_partial[:, spot]) * inverse_scale
        turned = key * cosine_ref[...] + pltpu.roll(key, HEAD_DIM // 2, 1) * sine_ref[...]
        column = pl.multiple_of(z * width + 2 * g * HEAD_DIM, HEAD_DIM)
        out_ref[pl.ds(row, local), pl.ds(column, HEAD_DIM)] = turned.astype(jnp.bfloat16)
    swaps[2].wait()
    for g in range(half // HEAD_DIM):
        spot = slice(g * HEAD_DIM, (g + 1) * HEAD_DIM)
        there = slice(half + g * HEAD_DIM, half + (g + 1) * HEAD_DIM)
        value = (value_sums[:, spot] + peer_partial[:, there]) * inverse_scale
        column = pl.multiple_of(z * width + (2 * g + 1) * HEAD_DIM, HEAD_DIM)
        out_ref[pl.ds(row, local), pl.ds(column, HEAD_DIM)] = value.astype(jnp.bfloat16)

    for turn in range(1, heads):
        send_z(region(x, b, z), 0, turn)
    for turn in range(len(joint) + 2):
        if turn < len(joint):
            spread(*joint[turn])
        if turn == 0:
            for other in others:
                spread_basis(other)
        if 1 <= turn < len(joint) + 1:
            relay(*joint[turn - 1])
        if turn == len(joint) + 1:
            for other in others:
                gathered_basis(other)
            for early in range(1, len(joint) - 2):
                gathered(*joint[early])
                accumulate(early)
        if turn >= 2:
            finish(*joint[turn - 2])
        if turn == 2:
            for other in others:
                relay_basis(other)
        if turn == 3:
            gathered(*joint[0])
            accumulate(0)
    for turn in range(max(1, len(joint) - 2), len(joint)):
        gathered(*joint[turn])
        accumulate(turn)
    for going in started:
        going.wait_send()


def collect(hidden_rows, gain, key_weight, value_weight, positions, basis, heads, tokens):
    depth = hidden_rows.shape[1]
    local = positions.shape[0]
    half, width = key_weight.shape[1], key_weight.shape[1] + value_weight.shape[1]
    half_width = HEAD_DIM // 2
    chunks = 4
    frequency = jnp.exp(
        jnp.arange(half_width, dtype=jnp.float32) * (-math.log(ROTARY_BASE) / half_width)
    )
    angles = positions.astype(jnp.float32)[:, None] * frequency[None, :]
    cosine, sine = jnp.cos(angles), jnp.sin(angles)
    dma = pltpu.SemaphoreType.DMA
    anywhere = pl.BlockSpec(memory_space=pltpu.HBM)
    inside = pl.BlockSpec(memory_space=pltpu.VMEM)
    return pl.pallas_call(
        functools.partial(collect_kernel, heads),
        out_shape=(
            jax.ShapeDtypeStruct((tokens, tokens), jnp.bfloat16),
            jax.ShapeDtypeStruct((tokens, tokens), jnp.bfloat16),
            jax.ShapeDtypeStruct((basis.shape[1], tokens), jnp.float32),
            jax.ShapeDtypeStruct((tokens, width), jnp.bfloat16),
        ),
        in_specs=[anywhere] * 4 + [inside] * 2 + [anywhere],
        out_specs=(inside,) * 4,
        scratch_shapes=[
            pltpu.VMEM((tokens, heads * width), jnp.bfloat16),
            pltpu.VMEM((heads * width, basis.shape[1]), jnp.float32),
            pltpu.VMEM((tokens, tokens), jnp.float32),
            pltpu.VMEM(hidden_rows.shape, jnp.bfloat16),
            pltpu.VMEM((1, depth), jnp.float32),
            pltpu.VMEM(key_weight.shape, jnp.bfloat16),
            pltpu.VMEM(value_weight.shape, jnp.bfloat16),
            pltpu.VMEM((local, width), jnp.float32),
            pltpu.VMEM((local, width), jnp.float32),
            pltpu.VMEM((SUBLANES, local), jnp.float32),
            pltpu.VMEM((SUBLANES, local), jnp.float32),
            dma((2, chunks)),
            dma((3, chunks)),
            dma((3, 2)),
            dma((2, heads, 2)),
            dma((2, heads, 2)),
            dma((2, heads, 2)),
            dma((2, heads, 2)),
            dma((2, heads, 2)),
            dma((2, heads, 4, 2)),
        ],
        compiler_params=pltpu.CompilerParams(
            collective_id=0, has_side_effects=True, vmem_limit_bytes=45 * 2**20
        ),
    )(
        hidden_rows,
        pltpu.with_memory_space_constraint(gain[None, :], pltpu.HBM),
        key_weight,
        value_weight,
        jnp.concatenate([cosine, cosine], axis=1),
        jnp.concatenate([-sine, sine], axis=1),
        pltpu.with_memory_space_constraint(basis, pltpu.HBM),
    )


def body(hidden, gain, key_weight, value_weight, positions, initial_basis):
    hidden_rows = hidden[0]
    local_tokens = positions.shape[1]
    seqs, batches, heads = lax.axis_size("seq"), lax.axis_size("batch"), lax.axis_size("head")
    tokens = local_tokens * seqs * batches
    if seqs == 2 and batches == 4 and tokens <= initial_basis.shape[0] * heads:
        collected = collect(
            hidden_rows,
            gain,
            key_weight,
            value_weight,
            positions[0],
            initial_basis,
            heads,
            tokens,
        )
        return iterate(*collected, initial_basis.shape[0] * heads)
    widened = hidden_rows.astype(jnp.float32)
    scaled = (widened * gain).astype(jnp.bfloat16)
    local_squares = jnp.sum(widened * widened, axis=1)
    key_columns = key_weight.shape[1]
    weights = jnp.concatenate([key_weight, value_weight], axis=1)
    own_squares = total_squares(local_squares, local_tokens)
    projected = lax.psum_scatter(
        jnp.dot(scaled, weights, preferred_element_type=jnp.float32),
        "seq",
        scatter_dimension=0,
        tiled=True,
    )
    inverse_scale = lax.rsqrt(own_squares / D + EPSILON)
    projected = projected * inverse_scale[:, None]
    key_rows = rotary(projected[:, :key_columns].reshape(local_tokens, -1, HEAD_DIM), positions[0])
    value_rows = projected[:, key_columns:].reshape(local_tokens, -1, HEAD_DIM)
    joint_rows = (
        jnp.stack([key_rows, value_rows], axis=2).reshape(local_tokens, -1).astype(jnp.bfloat16)
    )
    partial_value = lax.dot_general(
        joint_rows,
        lax.all_gather(joint_rows, "head", axis=1, tiled=True),
        (((0,), (0,)), ((), ())),
        preferred_element_type=jnp.float32,
    )
    token_total = local_tokens * lax.axis_size("seq") * lax.axis_size("batch")
    basis_block = initial_basis
    covariance = lax.psum(partial_value, ("seq", "batch")) / token_total
    for iteration in range(ITERS):
        whole_basis = whole_of(basis_block)
        images = jnp.dot(
            covariance,
            whole_basis,
            precision=lax.Precision.HIGHEST,
            preferred_element_type=jnp.float32,
        )
        gram_matrix = lax.psum(gram_of(images), "head") / whole_basis.shape[0]
        basis_block = orthonormal(images, gram_matrix)
    return basis_block


def solution(mesh):
    return jax.shard_map(
        body,
        mesh=mesh,
        in_specs=(
            P("batch", None, "seq"),
            P("seq"),
            P("seq", "head"),
            P("seq", "head"),
            P("batch", "seq"),
            P("head", None),
        ),
        out_specs=P("head", None),
        check_vma=False,
    )
```

```python
import functools
import math

import jax
import jax.numpy as jnp
from jax import lax
from jax.experimental import pallas as pl
from jax.experimental.pallas import tpu as pltpu
from jax.sharding import PartitionSpec as P

D = 16384
HEAD_DIM = 128
ITERS = 4


EPSILON = 1e-05
ROTARY_BASE = 500000.0


def rotary(head_rows, position_row):
    half_width = head_rows.shape[-1] // 2
    index_row = jnp.arange(half_width, dtype=jnp.float32)
    frequency = jnp.exp(index_row * (-math.log(ROTARY_BASE) / half_width))
    angles = position_row.astype(jnp.float32)[:, None] * frequency[None, :]
    cosine = jnp.cos(angles)[:, None, :]
    sine_part = jnp.sin(angles)[:, None, :]
    first_half = head_rows[..., :half_width]
    second_half = head_rows[..., half_width:]
    return jnp.concatenate(
        [
            first_half * cosine - second_half * sine_part,
            second_half * cosine + first_half * sine_part,
        ],
        axis=-1,
    )


def whole_of(basis_block):
    return lax.all_gather(basis_block, "head", axis=0, tiled=True)


def total_squares(local_squares, local_tokens):
    all_squares = lax.psum(local_squares, "seq")
    return lax.dynamic_slice_in_dim(all_squares, lax.axis_index("seq") * local_tokens, local_tokens)


def gram_of(images):
    return lax.dot_general(
        images,
        images,
        (((0,), (0,)), ((), ())),
        precision=lax.Precision.HIGHEST,
        preferred_element_type=jnp.float32,
    )


def orthonormal(images, gram_matrix):
    factor = jnp.linalg.cholesky(gram_matrix)
    return lax.linalg.triangular_solve(
        factor, images, left_side=False, lower=True, transpose_a=True
    )


LANES = 128
SUBLANES = 8
AHEAD = True


def dot_of(left, right, left_axis, right_axis, precision=None):
    return lax.dot_general(
        left,
        right,
        (((left_axis,), (right_axis,)), ((), ())),
        precision=precision,
        preferred_element_type=jnp.float32,
    )


def exact(left, right, left_axis, right_axis):
    return dot_of(left, right, left_axis, right_axis, lax.Precision.HIGHEST)


def halves_of(value):
    high = value.astype(jnp.bfloat16)
    return high, (value - high.astype(jnp.float32)).astype(jnp.bfloat16)


def thrice(left, right, left_axis, right_axis):
    left_high, left_low = halves_of(left)
    right_high, right_low = halves_of(right)
    return (
        dot_of(left_high, right_high, left_axis, right_axis)
        + dot_of(left_high, right_low, left_axis, right_axis)
        + dot_of(left_low, right_high, left_axis, right_axis)
    )


def inverse_factor(matrix):
    size = matrix.shape[0]
    shape = (SUBLANES, size)
    rows = lax.broadcasted_iota(jnp.int32, shape, 0)
    lanes = lax.broadcasted_iota(jnp.int32, shape, 1)
    groups = size // SUBLANES
    tiles = [matrix[SUBLANES * g : SUBLANES * (g + 1)] for g in range(groups)]
    out = []

    def row_of(value, at):
        return jnp.broadcast_to(value[at : at + 1, :], shape)

    def lane_of(value, at):
        return jnp.broadcast_to(value[:, at : at + 1], shape)

    def total(terms):
        while len(terms) > 1:
            pairs = [terms[i] + terms[i + 1] for i in range(0, len(terms) - 1, 2)]
            terms = pairs + terms[2 * len(pairs) :]
        return terms[0]

    zero = jnp.zeros(shape, jnp.float32)
    for own in range(groups):
        pivot = own * SUBLANES
        block = [lane_of(tiles[own], pivot + j) for j in range(SUBLANES)]
        if AHEAD and own:
            block = following
        last_group = own + 1 == groups
        if not last_group:
            below = [lane_of(tiles[own + 1], pivot + j) for j in range(SUBLANES)]
            if AHEAD:
                after = [lane_of(tiles[own + 1], pivot + SUBLANES + j) for j in range(SUBLANES)]
        factor = [None] * SUBLANES
        turned, weighted = [], []
        for k in range(0, SUBLANES, 2):
            one, two = block[k], block[k + 1]
            if not AHEAD:
                one, two = one + zero, two + zero
            first, cross, last = row_of(one, k), row_of(two, k), row_of(two, k + 1)
            scale = 1.0 / (first * last - cross * cross)
            mixed = cross * scale
            here, next_ = rows == k, rows == k + 1
            pair = here | next_
            first_scaled, last_scaled = first * scale, last * scale
            top = one * last_scaled - two * mixed
            low = two * first_scaled - one * mixed
            top = jnp.where(here, -last_scaled, jnp.where(next_, mixed, top))
            low = jnp.where(here, mixed, jnp.where(next_, -first_scaled, low))
            heads = {}
            for j in range(SUBLANES):
                if j in (k, k + 1):
                    continue
                x, y = row_of(block[j], k), row_of(block[j], k + 1)
                heads[j] = (x, y)
                block[j] = jnp.where(pair, 0.0, block[j]) - (top * x + low * y)
            block[k], block[k + 1] = -top, -low
            ratio = cross / first
            top_scale, low_scale = lax.rsqrt(first), lax.rsqrt(last - ratio * cross)
            ratio_scale = ratio * low_scale
            for j in range(k):
                x, y = heads[j]
                lower = y * low_scale - x * ratio_scale
                factor[j] = jnp.where(here, x * top_scale, jnp.where(next_, lower, factor[j]))
            factor[k] = jnp.where(here, top_scale, jnp.where(next_, -ratio_scale, 0.0))
            factor[k + 1] = jnp.where(next_, low_scale, 0.0)
            if AHEAD and not last_group:
                t1 = total([below[k]] + [heads[j][0] * below[j] for j in range(k)])
                t2 = total([below[k + 1]] + [heads[j][1] * below[j] for j in range(k)])
                turned += [t1, t2]
                weighted += [t1 * last_scaled - t2 * mixed, t2 * first_scaled - t1 * mixed]
        inside = (lanes >= pivot) & (lanes < pivot + SUBLANES)
        held = jnp.where(inside, jnp.where(lanes == rows + pivot, 1.0, 0.0), tiles[own])
        spread = [row_of(held, j) for j in range(SUBLANES)]
        result = total([factor[j] * spread[j] for j in range(SUBLANES)])
        out.append(jnp.where(lanes < pivot + SUBLANES, result, 0.0))
        if last_group:
            break
        mixed = total([block[j] * spread[j] for j in range(SUBLANES)])
        mixes = [row_of(mixed, j) for j in range(SUBLANES)]
        if AHEAD:
            following = [
                after[j] - total([turned[m] * row_of(weighted[m], j) for m in range(SUBLANES)])
                for j in range(SUBLANES)
            ]
        columns = [
            [below[j]] + [lane_of(tiles[g], pivot + j) for g in range(own + 2, groups)]
            for j in range(SUBLANES)
        ]
        for g in range(own + 1, groups):
            changes = [columns[j][g - own - 1] * mixes[j] for j in range(SUBLANES)]
            tiles[g] = jnp.where(inside, 0.0, tiles[g]) - total(changes)
        yield
    yield jnp.concatenate(out, axis=0)


def factors_of(*matrices):
    running = [inverse_factor(matrix) for matrix in matrices]
    for _ in range(matrices[0].shape[0] // SUBLANES):
        results = [next(each) for each in running]
    return results


def iterate_kernel(
    high_ref, low_ref, start_ref, own_ref, out_ref, rows_ref, images_ref, gram_ref, factor_ref, joint
):
    rank, tokens = start_ref.shape
    scale = 1.0 / (tokens * joint)
    left, right = slice(0, rank // 2), slice(rank // 2, rank)

    def applied(rows):
        rows_high, rows_low = halves_of(rows)
        return (
            dot_of(rows_high, high_ref[...], 1, 0)
            + dot_of(rows_high, low_ref[...], 1, 0)
            + dot_of(rows_low, high_ref[...], 1, 0)
        )

    def gram_block(rows, images):
        return thrice(rows, images, 1, 1) * scale

    def reduced(factor):
        scaled = exact(factor, gram_ref[left, right], 1, 0)
        return scaled, gram_ref[right, right] - exact(scaled, scaled, 0, 0)

    images = applied(start_ref[...])
    images_ref[...] = images
    gram = gram_block(start_ref[...], images)
    gram_ref[...] = gram
    factor_ref[...] = factors_of(gram[left, left])[0]

    def step(iteration, carry):
        factor = factor_ref[...]
        scaled, rest = reduced(factor)
        first = thrice(factor, images_ref[left, :], 1, 0)
        first_images = applied(first)
        rest_factor, next_factor = factors_of(rest, gram_block(first, first_images))
        remaining = images_ref[right, :] - thrice(scaled, first, 0, 0)
        second = thrice(rest_factor, remaining, 1, 0)
        second_images = applied(second)
        rows_ref[left, :] = first
        rows_ref[right, :] = second
        gram_ref[left, right] = gram_block(first, second_images)
        gram_ref[right, right] = gram_block(second, second_images)
        images_ref[left, :] = first_images
        images_ref[right, :] = second_images
        factor_ref[...] = next_factor
        return carry

    lax.fori_loop(0, ITERS - 1, step, 0)
    rows_high, rows_low = halves_of(rows_ref[...])
    own = own_ref[...]
    loose = (dot_of(rows_high, own, 1, 0) + dot_of(rows_low, own, 1, 0)) * (1.0 / tokens)
    factor = factor_ref[...]
    scaled, rest = reduced(factor)
    first = thrice(factor, loose[left, :], 1, 0)
    out_ref[:, left] = thrice(loose[left, :], factor, 0, 1)
    second = loose[right, :] - thrice(scaled, first, 0, 0)
    out_ref[:, right] = thrice(second, factors_of(rest)[0], 0, 1)


def iterate(high, low, start, own, joint):
    rank, tokens = start.shape

    def kernel(*refs):
        iterate_kernel(*refs, joint)

    return pl.pallas_call(
        kernel,
        out_shape=jax.ShapeDtypeStruct((own.shape[1], rank), jnp.float32),
        in_specs=[pl.BlockSpec(memory_space=pltpu.VMEM)] * 4,
        out_specs=pl.BlockSpec(memory_space=pltpu.VMEM),
        scratch_shapes=[
            pltpu.VMEM((rank, tokens), jnp.float32),
            pltpu.VMEM((rank, tokens), jnp.float32),
            pltpu.VMEM((rank, rank), jnp.float32),
            pltpu.VMEM((rank // 2, rank // 2), jnp.float32),
        ],
        compiler_params=pltpu.CompilerParams(vmem_limit_bytes=40 * 2**20),
    )(high, low, start, own)


def collect_kernel(
    heads,
    hidden_ref,
    gain_ref,
    key_ref,
    value_ref,
    cosine_ref,
    sine_ref,
    basis_ref,
    high_ref,
    low_ref,
    rows_ref,
    own_ref,
    out_ref,
    whole_ref,
    token_sums,
    hidden_rows,
    gain_row,
    key_rows,
    value_rows,
    partial,
    peer_partial,
    squares,
    peer_squares,
    load_sems,
    half_sems,
    swap_sems,
    z_sems,
    x_sems,
    y_sems,
    x_half_sems,
    y_half_sems,
    core_sems,
):
    x, b, z = lax.axis_index("seq"), lax.axis_index("batch"), lax.axis_index("head")
    local, width = peer_partial.shape
    half = width // 2
    rank = whole_ref.shape[1]
    piece = width // 8
    depth = gain_row.shape[1]
    chunks = load_sems.shape[1]
    chunk = depth // chunks
    other_x, other_y = 1 - x, (b + 2) % 4
    partner = b + 1 - 2 * (b % 2)
    x_peer, y_peer, core_peer = (other_x, b, z), (x, other_y, z), (x, partner, z)
    away = pl.ds(pl.multiple_of(other_x * local, local), local)
    mine = pl.ds(pl.multiple_of(x * local, local), local)

    def nearest(turn):
        if turn == 0 or heads != 4:
            return (z + turn) % heads
        side = z // 2
        inner = z + side * (3 - 2 * z)
        place = (1 + inner, 2 - 2 * inner, 3)[turn - 1]
        return 3 * side + (1 - 2 * side) * place

    sources = [nearest(turn) for turn in range(heads)]

    def z_peer(turn):
        return (x, b, sources[turn])

    own_block = whole_ref.at[pl.ds(pl.multiple_of(z * width, width), width), :]
    basis_load = pltpu.make_async_copy(basis_ref, own_block, half_sems.at[2, 0])
    gain_load = pltpu.make_async_copy(gain_ref, gain_row, half_sems.at[2, 1])

    def span(c):
        return pl.ds(c * chunk, chunk)

    def token_load(kind, area, c):
        return pltpu.make_async_copy(
            hidden_ref.at[area, span(c)], hidden_rows.at[area, span(c)], half_sems.at[kind, c]
        )

    away_loads = [token_load(0, away, c) for c in range(chunks)]
    mine_loads = [token_load(1, mine, c) for c in range(chunks)]
    key_loads = [
        pltpu.make_async_copy(key_ref.at[span(c), :], key_rows.at[span(c), :], load_sems.at[0, c])
        for c in range(chunks)
    ]
    value_loads = [
        pltpu.make_async_copy(
            value_ref.at[span(c), :], value_rows.at[span(c), :], load_sems.at[1, c]
        )
        for c in range(chunks)
    ]
    basis_load.start()
    gain_load.start()
    loads = [load for pair in zip(away_loads, key_loads) for load in pair]
    loads += value_loads + mine_loads
    waiting = list(loads)

    def issue():
        if waiting:
            waiting.pop(0).start()

    def ready(load):
        load.wait()
        issue()

    for _ in range(4):
        issue()

    barrier = pltpu.get_barrier_semaphore()
    peers = [x_peer, y_peer, core_peer] + [z_peer(d) for d in range(1, heads)]
    for peer in peers:
        pl.semaphore_signal(barrier, inc=1, device_id=peer, device_id_type=pl.DeviceIdType.MESH)
    pl.semaphore_wait(barrier, len(peers))

    def copy(source, target, sems, peer):
        return pltpu.make_async_remote_copy(
            src_ref=source,
            dst_ref=target,
            send_sem=sems.at[0],
            recv_sem=sems.at[1],
            device_id=peer,
            device_id_type=pl.DeviceIdType.MESH,
        )

    def region(xs, bs, zs, start=0, size=width):
        row = pl.multiple_of((xs * 4 + bs) * local, local)
        column = pl.multiple_of(zs * width + start, half)
        return out_ref.at[pl.ds(row, local), pl.ds(column, size)]

    def piece_of(xs, bs, zs, start=0, size=rank):
        row = pl.multiple_of(zs * width + (xs * 4 + bs) * piece, piece)
        return whole_ref.at[pl.ds(row, piece), pl.ds(start, size)]

    started = []

    def send(area, sems, peer):
        going = copy(area, area, sems, peer)
        going.start()
        started.append(going)

    def arrive(area, sems, peer):
        copy(area, area, sems, peer).wait_recv()

    def send_z(area, kind, turn):
        going = pltpu.make_async_remote_copy(
            src_ref=area,
            dst_ref=area,
            send_sem=z_sems.at[kind, sources[turn], 0],
            recv_sem=z_sems.at[kind, z, 1],
            device_id=z_peer(turn),
            device_id_type=pl.DeviceIdType.MESH,
        )
        going.start()
        started.append(going)

    def spread(kind, area, middle, turn):
        s = sources[turn]
        own = area(x, b, s)
        if turn:
            arrive(own, z_sems.at[kind, s], z_peer(turn))
        send(own, x_sems.at[kind, turn], x_peer)
        send(own, y_sems.at[kind, turn], y_peer)
        send(own, core_sems.at[kind, turn, 0], core_peer)

    def relay(kind, area, middle, turn):
        s = sources[turn]
        arrive(area(other_x, b, s), x_sems.at[kind, turn], x_peer)
        beyond = area(other_x, b, s, middle, middle) if middle else area(other_x, b, s)
        send(beyond, y_half_sems.at[kind, turn], y_peer)
        send(area(other_x, b, s), core_sems.at[kind, turn, 1], core_peer)
        arrive(area(x, other_y, s), y_sems.at[kind, turn], y_peer)
        if middle:
            send(area(x, other_y, s, 0, middle), x_half_sems.at[kind, turn], x_peer)
        send(area(x, other_y, s), core_sems.at[kind, turn, 2], core_peer)

    def finish(kind, area, middle, turn):
        s = sources[turn]
        if middle:
            arrive(area(other_x, other_y, s, 0, middle), x_half_sems.at[kind, turn], x_peer)
        beyond = area(other_x, other_y, s, middle, middle) if middle else area(other_x, other_y, s)
        arrive(beyond, y_half_sems.at[kind, turn], y_peer)
        send(area(other_x, other_y, s), core_sems.at[kind, turn, 3], core_peer)

    far = (partner + 2) % 4

    def gathered(kind, area, middle, turn):
        places = [(x, partner), (other_x, partner), (x, far), (other_x, far)]
        for place, (xs, bs) in enumerate(places):
            arrive(area(xs, bs, sources[turn]), core_sems.at[kind, turn, place], core_peer)

    joint = [(0, region, half, turn) for turn in range(heads)]
    pieces = [(1, piece_of, 0, turn) for turn in range(1, heads)]
    tokens, strip = out_ref.shape[0], 256

    def accumulate(turn):
        place = pl.multiple_of(sources[turn] * width, width)
        block = out_ref[:, pl.ds(place, width)]
        basis_high, basis_low = halves_of(whole_ref[pl.ds(place, width), :])
        for start in range(0, tokens, strip):
            area = slice(start, start + strip)
            part = out_ref[area, pl.ds(place, width)]
            product = dot_of(block, part, 1, 1)
            rows = dot_of(basis_high, part, 0, 1) + dot_of(basis_low, part, 0, 1)
            if turn:
                product = product + token_sums[:, area]
                rows = rows + rows_ref[:, area]
            rows_ref[:, area] = rows
            if turn < heads - 1:
                token_sums[:, area] = product
            else:
                high, low = halves_of(product * (1.0 / tokens))
                high_ref[:, area] = high
                low_ref[:, area] = low
            if turn == 0:
                own_ref[area, :] = part

    basis_load.wait()
    for turn in range(1, heads):
        send_z(piece_of(x, b, z), 1, turn)

    def prepare(area, c, total):
        widened = hidden_rows[area, span(c)].astype(jnp.float32)
        scaled = (widened * gain_row[:, span(c)]).astype(jnp.bfloat16)
        hidden_rows[area, span(c)] = scaled
        squared = widened * widened
        for start in range(0, chunk, LANES):
            total = total + squared[:, start : start + LANES]
        return scaled, total

    def across(total):
        ones = jnp.ones((SUBLANES, LANES), jnp.float32)
        return exact(ones, total, 1, 1)

    def swap(source_ref, target_ref, index):
        going = copy(source_ref, target_ref, swap_sems.at[index], x_peer)
        going.start()
        return going

    gain_load.wait()
    away_total = jnp.zeros((local, LANES), jnp.float32)
    sums = jnp.zeros((local, half), jnp.float32)
    for c in range(chunks):
        ready(away_loads[c])
        scaled, away_total = prepare(away, c, away_total)
        ready(key_loads[c])
        sums = sums + dot_of(scaled, key_rows[span(c), :], 1, 0)
    partial[:, :half] = sums
    squares[...] = across(away_total)
    swaps = [
        swap(squares, peer_squares, 0),
        swap(partial.at[:, pl.ds(0, half)], peer_partial.at[:, pl.ds(0, half)], 1),
    ]
    sums = jnp.zeros((local, half), jnp.float32)
    for c in range(chunks):
        ready(value_loads[c])
        sums = sums + dot_of(hidden_rows[away, span(c)], value_rows[span(c), :], 1, 0)
    partial[:, half:] = sums
    swaps.append(swap(partial.at[:, pl.ds(half, half)], peer_partial.at[:, pl.ds(half, half)], 2))
    for item in pieces:
        spread(*item)
    mine_total = jnp.zeros((local, LANES), jnp.float32)
    key_sums = jnp.zeros((local, half), jnp.float32)
    value_sums = jnp.zeros((local, half), jnp.float32)
    for c in range(chunks):
        ready(mine_loads[c])
        scaled, mine_total = prepare(mine, c, mine_total)
        key_sums = key_sums + dot_of(scaled, key_rows[span(c), :], 1, 0)
        value_sums = value_sums + dot_of(scaled, value_rows[span(c), :], 1, 0)
    own_squares = across(mine_total)

    swaps[0].wait()
    eighths = jnp.full((SUBLANES, LANES), 1.0 / SUBLANES, jnp.float32)
    inverse_scale = lax.rsqrt(exact(own_squares + peer_squares[...], eighths, 0, 0) / D + EPSILON)
    row = pl.multiple_of((x * 4 + b) * local, local)
    swaps[1].wait()
    for g in range(half // HEAD_DIM):
        spot = slice(g * HEAD_DIM, (g + 1) * HEAD_DIM)
        key = (key_sums[:, spot] + peer_partial[:, spot]) * inverse_scale
        turned = key * cosine_ref[...] + pltpu.roll(key, HEAD_DIM // 2, 1) * sine_ref[...]
        column = pl.multiple_of(z * width + 2 * g * HEAD_DIM, HEAD_DIM)
        out_ref[pl.ds(row, local), pl.ds(column, HEAD_DIM)] = turned.astype(jnp.bfloat16)
    swaps[2].wait()
    for g in range(half // HEAD_DIM):
        spot = slice(g * HEAD_DIM, (g + 1) * HEAD_DIM)
        there = slice(half + g * HEAD_DIM, half + (g + 1) * HEAD_DIM)
        value = (value_sums[:, spot] + peer_partial[:, there]) * inverse_scale
        column = pl.multiple_of(z * width + (2 * g + 1) * HEAD_DIM, HEAD_DIM)
        out_ref[pl.ds(row, local), pl.ds(column, HEAD_DIM)] = value.astype(jnp.bfloat16)

    for turn in range(1, heads):
        send_z(region(x, b, z), 0, turn)
    for turn in range(len(joint) + 2):
        if turn < len(joint):
            spread(*joint[turn])
        if turn == 0:
            for item in pieces:
                relay(*item)
        if 1 <= turn < len(joint) + 1:
            relay(*joint[turn - 1])
        if turn == len(joint) + 1:
            for item in pieces:
                gathered(*item)
            for early in range(1, len(joint) - 2):
                gathered(*joint[early])
                accumulate(early)
        if turn >= 2:
            finish(*joint[turn - 2])
        if turn == 1:
            for item in pieces:
                finish(*item)
        if turn == 3:
            gathered(*joint[0])
            accumulate(0)
    for turn in range(max(1, len(joint) - 2), len(joint)):
        gathered(*joint[turn])
        accumulate(turn)
    for going in started:
        going.wait_send()


def collect(hidden_rows, gain, key_weight, value_weight, positions, basis, heads, tokens):
    depth = hidden_rows.shape[1]
    local = positions.shape[0]
    half, width = key_weight.shape[1], key_weight.shape[1] + value_weight.shape[1]
    half_width = HEAD_DIM // 2
    chunks = 4
    frequency = jnp.exp(
        jnp.arange(half_width, dtype=jnp.float32) * (-math.log(ROTARY_BASE) / half_width)
    )
    angles = positions.astype(jnp.float32)[:, None] * frequency[None, :]
    cosine, sine = jnp.cos(angles), jnp.sin(angles)
    dma = pltpu.SemaphoreType.DMA
    anywhere = pl.BlockSpec(memory_space=pltpu.HBM)
    inside = pl.BlockSpec(memory_space=pltpu.VMEM)
    return pl.pallas_call(
        functools.partial(collect_kernel, heads),
        out_shape=(
            jax.ShapeDtypeStruct((tokens, tokens), jnp.bfloat16),
            jax.ShapeDtypeStruct((tokens, tokens), jnp.bfloat16),
            jax.ShapeDtypeStruct((basis.shape[1], tokens), jnp.float32),
            jax.ShapeDtypeStruct((tokens, width), jnp.bfloat16),
        ),
        in_specs=[anywhere] * 4 + [inside] * 2 + [anywhere],
        out_specs=(inside,) * 4,
        scratch_shapes=[
            pltpu.VMEM((tokens, heads * width), jnp.bfloat16),
            pltpu.VMEM((heads * width, basis.shape[1]), jnp.float32),
            pltpu.VMEM((tokens, tokens), jnp.float32),
            pltpu.VMEM(hidden_rows.shape, jnp.bfloat16),
            pltpu.VMEM((1, depth), jnp.float32),
            pltpu.VMEM(key_weight.shape, jnp.bfloat16),
            pltpu.VMEM(value_weight.shape, jnp.bfloat16),
            pltpu.VMEM((local, width), jnp.float32),
            pltpu.VMEM((local, width), jnp.float32),
            pltpu.VMEM((SUBLANES, local), jnp.float32),
            pltpu.VMEM((SUBLANES, local), jnp.float32),
            dma((2, chunks)),
            dma((3, chunks)),
            dma((3, 2)),
            dma((2, heads, 2)),
            dma((2, heads, 2)),
            dma((2, heads, 2)),
            dma((2, heads, 2)),
            dma((2, heads, 2)),
            dma((2, heads, 4, 2)),
        ],
        compiler_params=pltpu.CompilerParams(
            collective_id=0, has_side_effects=True, vmem_limit_bytes=45 * 2**20
        ),
    )(
        hidden_rows,
        pltpu.with_memory_space_constraint(gain[None, :], pltpu.HBM),
        key_weight,
        value_weight,
        jnp.concatenate([cosine, cosine], axis=1),
        jnp.concatenate([-sine, sine], axis=1),
        pltpu.with_memory_space_constraint(basis, pltpu.HBM),
    )


def body(hidden, gain, key_weight, value_weight, positions, initial_basis):
    hidden_rows = hidden[0]
    local_tokens = positions.shape[1]
    seqs, batches, heads = lax.axis_size("seq"), lax.axis_size("batch"), lax.axis_size("head")
    tokens = local_tokens * seqs * batches
    if seqs == 2 and batches == 4 and tokens <= initial_basis.shape[0] * heads:
        collected = collect(
            hidden_rows,
            gain,
            key_weight,
            value_weight,
            positions[0],
            initial_basis,
            heads,
            tokens,
        )
        return iterate(*collected, initial_basis.shape[0] * heads)
    widened = hidden_rows.astype(jnp.float32)
    scaled = (widened * gain).astype(jnp.bfloat16)
    local_squares = jnp.sum(widened * widened, axis=1)
    key_columns = key_weight.shape[1]
    weights = jnp.concatenate([key_weight, value_weight], axis=1)
    own_squares = total_squares(local_squares, local_tokens)
    projected = lax.psum_scatter(
        jnp.dot(scaled, weights, preferred_element_type=jnp.float32),
        "seq",
        scatter_dimension=0,
        tiled=True,
    )
    inverse_scale = lax.rsqrt(own_squares / D + EPSILON)
    projected = projected * inverse_scale[:, None]
    key_rows = rotary(projected[:, :key_columns].reshape(local_tokens, -1, HEAD_DIM), positions[0])
    value_rows = projected[:, key_columns:].reshape(local_tokens, -1, HEAD_DIM)
    joint_rows = (
        jnp.stack([key_rows, value_rows], axis=2).reshape(local_tokens, -1).astype(jnp.bfloat16)
    )
    partial_value = lax.dot_general(
        joint_rows,
        lax.all_gather(joint_rows, "head", axis=1, tiled=True),
        (((0,), (0,)), ((), ())),
        preferred_element_type=jnp.float32,
    )
    token_total = local_tokens * lax.axis_size("seq") * lax.axis_size("batch")
    basis_block = initial_basis
    covariance = lax.psum(partial_value, ("seq", "batch")) / token_total
    for iteration in range(ITERS):
        whole_basis = whole_of(basis_block)
        images = jnp.dot(
            covariance,
            whole_basis,
            precision=lax.Precision.HIGHEST,
            preferred_element_type=jnp.float32,
        )
        gram_matrix = lax.psum(gram_of(images), "head") / whole_basis.shape[0]
        basis_block = orthonormal(images, gram_matrix)
    return basis_block


def solution(mesh):
    return jax.shard_map(
        body,
        mesh=mesh,
        in_specs=(
            P("batch", None, "seq"),
            P("seq"),
            P("seq", "head"),
            P("seq", "head"),
            P("batch", "seq"),
            P("head", None),
        ),
        out_specs=P("head", None),
        check_vma=False,
    )
```

```python
import functools
import math

import jax
import jax.numpy as jnp
from jax import lax
from jax.experimental import pallas as pl
from jax.experimental.pallas import tpu as pltpu
from jax.sharding import PartitionSpec as P

D = 16384
HEAD_DIM = 128
ITERS = 4


EPSILON = 1e-05
ROTARY_BASE = 500000.0


def rotary(head_rows, position_row):
    half_width = head_rows.shape[-1] // 2
    index_row = jnp.arange(half_width, dtype=jnp.float32)
    frequency = jnp.exp(index_row * (-math.log(ROTARY_BASE) / half_width))
    angles = position_row.astype(jnp.float32)[:, None] * frequency[None, :]
    cosine = jnp.cos(angles)[:, None, :]
    sine_part = jnp.sin(angles)[:, None, :]
    first_half = head_rows[..., :half_width]
    second_half = head_rows[..., half_width:]
    return jnp.concatenate(
        [
            first_half * cosine - second_half * sine_part,
            second_half * cosine + first_half * sine_part,
        ],
        axis=-1,
    )


def whole_of(basis_block):
    return lax.all_gather(basis_block, "head", axis=0, tiled=True)


def total_squares(local_squares, local_tokens):
    all_squares = lax.psum(local_squares, "seq")
    return lax.dynamic_slice_in_dim(all_squares, lax.axis_index("seq") * local_tokens, local_tokens)


def gram_of(images):
    return lax.dot_general(
        images,
        images,
        (((0,), (0,)), ((), ())),
        precision=lax.Precision.HIGHEST,
        preferred_element_type=jnp.float32,
    )


def orthonormal(images, gram_matrix):
    factor = jnp.linalg.cholesky(gram_matrix)
    return lax.linalg.triangular_solve(
        factor, images, left_side=False, lower=True, transpose_a=True
    )


LANES = 128
SUBLANES = 8
AHEAD = True


def dot_of(left, right, left_axis, right_axis, precision=None):
    return lax.dot_general(
        left,
        right,
        (((left_axis,), (right_axis,)), ((), ())),
        precision=precision,
        preferred_element_type=jnp.float32,
    )


def exact(left, right, left_axis, right_axis):
    return dot_of(left, right, left_axis, right_axis, lax.Precision.HIGHEST)


def halves_of(value):
    high = value.astype(jnp.bfloat16)
    return high, (value - high.astype(jnp.float32)).astype(jnp.bfloat16)


def thrice(left, right, left_axis, right_axis):
    left_high, left_low = halves_of(left)
    right_high, right_low = halves_of(right)
    return (
        dot_of(left_high, right_high, left_axis, right_axis)
        + dot_of(left_high, right_low, left_axis, right_axis)
        + dot_of(left_low, right_high, left_axis, right_axis)
    )


def inverse_factor(matrix):
    size = matrix.shape[0]
    shape = (SUBLANES, size)
    rows = lax.broadcasted_iota(jnp.int32, shape, 0)
    lanes = lax.broadcasted_iota(jnp.int32, shape, 1)
    groups = size // SUBLANES
    tiles = [matrix[SUBLANES * g : SUBLANES * (g + 1)] for g in range(groups)]
    out = []

    def row_of(value, at):
        return jnp.broadcast_to(value[at : at + 1, :], shape)

    def lane_of(value, at):
        return jnp.broadcast_to(value[:, at : at + 1], shape)

    def total(terms):
        while len(terms) > 1:
            pairs = [terms[i] + terms[i + 1] for i in range(0, len(terms) - 1, 2)]
            terms = pairs + terms[2 * len(pairs) :]
        return terms[0]

    zero = jnp.zeros(shape, jnp.float32)
    for own in range(groups):
        pivot = own * SUBLANES
        block = [lane_of(tiles[own], pivot + j) for j in range(SUBLANES)]
        if AHEAD and own:
            block = following
        last_group = own + 1 == groups
        if not last_group:
            below = [lane_of(tiles[own + 1], pivot + j) for j in range(SUBLANES)]
            if AHEAD:
                after = [lane_of(tiles[own + 1], pivot + SUBLANES + j) for j in range(SUBLANES)]
        factor = [None] * SUBLANES
        turned, weighted = [], []
        for k in range(0, SUBLANES, 2):
            one, two = block[k], block[k + 1]
            if not AHEAD:
                one, two = one + zero, two + zero
            first, cross, last = row_of(one, k), row_of(two, k), row_of(two, k + 1)
            scale = 1.0 / (first * last - cross * cross)
            mixed = cross * scale
            here, next_ = rows == k, rows == k + 1
            pair = here | next_
            first_scaled, last_scaled = first * scale, last * scale
            top = one * last_scaled - two * mixed
            low = two * first_scaled - one * mixed
            top = jnp.where(here, -last_scaled, jnp.where(next_, mixed, top))
            low = jnp.where(here, mixed, jnp.where(next_, -first_scaled, low))
            heads = {}
            for j in range(SUBLANES):
                if j in (k, k + 1):
                    continue
                x, y = row_of(block[j], k), row_of(block[j], k + 1)
                heads[j] = (x, y)
                block[j] = jnp.where(pair, 0.0, block[j]) - (top * x + low * y)
            block[k], block[k + 1] = -top, -low
            ratio = cross / first
            top_scale, low_scale = lax.rsqrt(first), lax.rsqrt(last - ratio * cross)
            ratio_scale = ratio * low_scale
            for j in range(k):
                x, y = heads[j]
                lower = y * low_scale - x * ratio_scale
                factor[j] = jnp.where(here, x * top_scale, jnp.where(next_, lower, factor[j]))
            factor[k] = jnp.where(here, top_scale, jnp.where(next_, -ratio_scale, 0.0))
            factor[k + 1] = jnp.where(next_, low_scale, 0.0)
            if AHEAD and not last_group:
                t1 = total([below[k]] + [heads[j][0] * below[j] for j in range(k)])
                t2 = total([below[k + 1]] + [heads[j][1] * below[j] for j in range(k)])
                turned += [t1, t2]
                weighted += [t1 * last_scaled - t2 * mixed, t2 * first_scaled - t1 * mixed]
        inside = (lanes >= pivot) & (lanes < pivot + SUBLANES)
        held = jnp.where(inside, jnp.where(lanes == rows + pivot, 1.0, 0.0), tiles[own])
        spread = [row_of(held, j) for j in range(SUBLANES)]
        result = total([factor[j] * spread[j] for j in range(SUBLANES)])
        out.append(jnp.where(lanes < pivot + SUBLANES, result, 0.0))
        if last_group:
            break
        mixed = total([block[j] * spread[j] for j in range(SUBLANES)])
        mixes = [row_of(mixed, j) for j in range(SUBLANES)]
        if AHEAD:
            following = [
                after[j] - total([turned[m] * row_of(weighted[m], j) for m in range(SUBLANES)])
                for j in range(SUBLANES)
            ]
        columns = [
            [below[j]] + [lane_of(tiles[g], pivot + j) for g in range(own + 2, groups)]
            for j in range(SUBLANES)
        ]
        for g in range(own + 1, groups):
            changes = [columns[j][g - own - 1] * mixes[j] for j in range(SUBLANES)]
            tiles[g] = jnp.where(inside, 0.0, tiles[g]) - total(changes)
        yield
    yield jnp.concatenate(out, axis=0)


def factors_of(*matrices):
    running = [inverse_factor(matrix) for matrix in matrices]
    for _ in range(matrices[0].shape[0] // SUBLANES):
        results = [next(each) for each in running]
    return results


def iterate_kernel(
    high_ref, low_ref, start_ref, own_ref, out_ref, rows_ref, images_ref, gram_ref, factor_ref, joint
):
    rank, tokens = start_ref.shape
    scale = 1.0 / (tokens * joint)
    left, right = slice(0, rank // 2), slice(rank // 2, rank)

    def applied(rows):
        rows_high, rows_low = halves_of(rows)
        return (
            dot_of(rows_high, high_ref[...], 1, 0)
            + dot_of(rows_high, low_ref[...], 1, 0)
            + dot_of(rows_low, high_ref[...], 1, 0)
        )

    def gram_block(rows, images):
        return thrice(rows, images, 1, 1) * scale

    def reduced(factor):
        scaled = exact(factor, gram_ref[left, right], 1, 0)
        return scaled, gram_ref[right, right] - exact(scaled, scaled, 0, 0)

    images = applied(start_ref[...])
    images_ref[...] = images
    gram = gram_block(start_ref[...], images)
    gram_ref[...] = gram
    factor_ref[...] = factors_of(gram[left, left])[0]

    def step(iteration, carry):
        factor = factor_ref[...]
        scaled, rest = reduced(factor)
        first = thrice(factor, images_ref[left, :], 1, 0)
        first_images = applied(first)
        rest_factor, next_factor = factors_of(rest, gram_block(first, first_images))
        remaining = images_ref[right, :] - thrice(scaled, first, 0, 0)
        second = thrice(rest_factor, remaining, 1, 0)
        second_images = applied(second)
        rows_ref[left, :] = first
        rows_ref[right, :] = second
        gram_ref[left, right] = gram_block(first, second_images)
        gram_ref[right, right] = gram_block(second, second_images)
        images_ref[left, :] = first_images
        images_ref[right, :] = second_images
        factor_ref[...] = next_factor
        return carry

    lax.fori_loop(0, ITERS - 1, step, 0)
    rows_high, rows_low = halves_of(rows_ref[...])
    own = own_ref[...]
    loose = (dot_of(rows_high, own, 1, 0) + dot_of(rows_low, own, 1, 0)) * (1.0 / tokens)
    factor = factor_ref[...]
    scaled, rest = reduced(factor)
    first = thrice(factor, loose[left, :], 1, 0)
    out_ref[:, left] = thrice(loose[left, :], factor, 0, 1)
    second = loose[right, :] - thrice(scaled, first, 0, 0)
    out_ref[:, right] = thrice(second, factors_of(rest)[0], 0, 1)


def iterate(high, low, start, own, joint):
    rank, tokens = start.shape

    def kernel(*refs):
        iterate_kernel(*refs, joint)

    return pl.pallas_call(
        kernel,
        out_shape=jax.ShapeDtypeStruct((own.shape[1], rank), jnp.float32),
        in_specs=[pl.BlockSpec(memory_space=pltpu.VMEM)] * 4,
        out_specs=pl.BlockSpec(memory_space=pltpu.VMEM),
        scratch_shapes=[
            pltpu.VMEM((rank, tokens), jnp.float32),
            pltpu.VMEM((rank, tokens), jnp.float32),
            pltpu.VMEM((rank, rank), jnp.float32),
            pltpu.VMEM((rank // 2, rank // 2), jnp.float32),
        ],
        compiler_params=pltpu.CompilerParams(vmem_limit_bytes=40 * 2**20),
    )(high, low, start, own)


def collect_kernel(
    heads,
    hidden_ref,
    gain_ref,
    key_ref,
    value_ref,
    cosine_ref,
    sine_ref,
    basis_ref,
    high_ref,
    low_ref,
    rows_ref,
    own_ref,
    out_ref,
    whole_ref,
    token_sums,
    hidden_rows,
    gain_row,
    key_rows,
    value_rows,
    partial,
    peer_partial,
    squares,
    peer_squares,
    load_sems,
    half_sems,
    swap_sems,
    z_sems,
    x_sems,
    y_sems,
    x_half_sems,
    y_half_sems,
    core_sems,
):
    x, b, z = lax.axis_index("seq"), lax.axis_index("batch"), lax.axis_index("head")
    local, width = peer_partial.shape
    half = width // 2
    rank = whole_ref.shape[1]
    piece = width // 8
    depth = gain_row.shape[1]
    chunks = load_sems.shape[1]
    chunk = depth // chunks
    other_x, other_y = 1 - x, (b + 2) % 4
    partner = b + 1 - 2 * (b % 2)
    x_peer, y_peer, core_peer = (other_x, b, z), (x, other_y, z), (x, partner, z)
    away = pl.ds(pl.multiple_of(other_x * local, local), local)
    mine = pl.ds(pl.multiple_of(x * local, local), local)

    def nearest(turn):
        if turn == 0 or heads != 4:
            return (z + turn) % heads
        side = z // 2
        inner = z + side * (3 - 2 * z)
        place = (1 + inner, 2 - 2 * inner, 3)[turn - 1]
        return 3 * side + (1 - 2 * side) * place

    sources = [nearest(turn) for turn in range(heads)]

    def z_peer(turn):
        return (x, b, sources[turn])

    own_block = whole_ref.at[pl.ds(pl.multiple_of(z * width, width), width), :]
    basis_load = pltpu.make_async_copy(basis_ref, own_block, half_sems.at[2, 0])
    gain_load = pltpu.make_async_copy(gain_ref, gain_row, half_sems.at[2, 1])

    def span(c):
        return pl.ds(c * chunk, chunk)

    def token_load(kind, area, c):
        return pltpu.make_async_copy(
            hidden_ref.at[area, span(c)], hidden_rows.at[area, span(c)], half_sems.at[kind, c]
        )

    away_loads = [token_load(0, away, c) for c in range(chunks)]
    mine_loads = [token_load(1, mine, c) for c in range(chunks)]
    key_loads = [
        pltpu.make_async_copy(key_ref.at[span(c), :], key_rows.at[span(c), :], load_sems.at[0, c])
        for c in range(chunks)
    ]
    value_loads = [
        pltpu.make_async_copy(
            value_ref.at[span(c), :], value_rows.at[span(c), :], load_sems.at[1, c]
        )
        for c in range(chunks)
    ]
    basis_load.start()
    gain_load.start()
    loads = [load for pair in zip(away_loads, key_loads) for load in pair]
    loads += value_loads + mine_loads
    waiting = list(loads)

    def issue():
        if waiting:
            waiting.pop(0).start()

    def ready(load):
        load.wait()
        issue()

    for _ in range(6):
        issue()

    barrier = pltpu.get_barrier_semaphore()
    peers = [x_peer, y_peer, core_peer] + [z_peer(d) for d in range(1, heads)]
    for peer in peers:
        pl.semaphore_signal(barrier, inc=1, device_id=peer, device_id_type=pl.DeviceIdType.MESH)
    pl.semaphore_wait(barrier, len(peers))

    def copy(source, target, sems, peer):
        return pltpu.make_async_remote_copy(
            src_ref=source,
            dst_ref=target,
            send_sem=sems.at[0],
            recv_sem=sems.at[1],
            device_id=peer,
            device_id_type=pl.DeviceIdType.MESH,
        )

    def region(xs, bs, zs, start=0, size=width):
        row = pl.multiple_of((xs * 4 + bs) * local, local)
        column = pl.multiple_of(zs * width + start, half)
        return out_ref.at[pl.ds(row, local), pl.ds(column, size)]

    def piece_of(xs, bs, zs, start=0, size=rank):
        row = pl.multiple_of(zs * width + (xs * 4 + bs) * piece, piece)
        return whole_ref.at[pl.ds(row, piece), pl.ds(start, size)]

    started = []

    def send(area, sems, peer):
        going = copy(area, area, sems, peer)
        going.start()
        started.append(going)

    def arrive(area, sems, peer):
        copy(area, area, sems, peer).wait_recv()

    def send_z(area, kind, turn):
        going = pltpu.make_async_remote_copy(
            src_ref=area,
            dst_ref=area,
            send_sem=z_sems.at[kind, sources[turn], 0],
            recv_sem=z_sems.at[kind, z, 1],
            device_id=z_peer(turn),
            device_id_type=pl.DeviceIdType.MESH,
        )
        going.start()
        started.append(going)

    def spread(kind, area, middle, turn):
        s = sources[turn]
        own = area(x, b, s)
        if turn:
            arrive(own, z_sems.at[kind, s], z_peer(turn))
        send(own, x_sems.at[kind, turn], x_peer)
        send(own, y_sems.at[kind, turn], y_peer)
        send(own, core_sems.at[kind, turn, 0], core_peer)

    def relay(kind, area, middle, turn):
        s = sources[turn]
        arrive(area(other_x, b, s), x_sems.at[kind, turn], x_peer)
        beyond = area(other_x, b, s, middle, middle) if middle else area(other_x, b, s)
        send(beyond, y_half_sems.at[kind, turn], y_peer)
        send(area(other_x, b, s), core_sems.at[kind, turn, 1], core_peer)
        arrive(area(x, other_y, s), y_sems.at[kind, turn], y_peer)
        if middle:
            send(area(x, other_y, s, 0, middle), x_half_sems.at[kind, turn], x_peer)
        send(area(x, other_y, s), core_sems.at[kind, turn, 2], core_peer)

    def finish(kind, area, middle, turn):
        s = sources[turn]
        if middle:
            arrive(area(other_x, other_y, s, 0, middle), x_half_sems.at[kind, turn], x_peer)
        beyond = area(other_x, other_y, s, middle, middle) if middle else area(other_x, other_y, s)
        arrive(beyond, y_half_sems.at[kind, turn], y_peer)
        send(area(other_x, other_y, s), core_sems.at[kind, turn, 3], core_peer)

    far = (partner + 2) % 4

    def gathered(kind, area, middle, turn):
        places = [(x, partner), (other_x, partner), (x, far), (other_x, far)]
        for place, (xs, bs) in enumerate(places):
            arrive(area(xs, bs, sources[turn]), core_sems.at[kind, turn, place], core_peer)

    joint = [(0, region, half, turn) for turn in range(heads)]
    pieces = [(1, piece_of, 0, turn) for turn in range(1, heads)]
    tokens, strip = out_ref.shape[0], 256

    def accumulate(turn):
        place = pl.multiple_of(sources[turn] * width, width)
        block = out_ref[:, pl.ds(place, width)]
        basis_high, basis_low = halves_of(whole_ref[pl.ds(place, width), :])
        for start in range(0, tokens, strip):
            area = slice(start, start + strip)
            part = out_ref[area, pl.ds(place, width)]
            product = dot_of(block, part, 1, 1)
            rows = dot_of(basis_high, part, 0, 1) + dot_of(basis_low, part, 0, 1)
            if turn:
                product = product + token_sums[:, area]
                rows = rows + rows_ref[:, area]
            rows_ref[:, area] = rows
            if turn < heads - 1:
                token_sums[:, area] = product
            else:
                high, low = halves_of(product * (1.0 / tokens))
                high_ref[:, area] = high
                low_ref[:, area] = low
            if turn == 0:
                own_ref[area, :] = part

    basis_load.wait()
    for turn in range(1, heads):
        send_z(piece_of(x, b, z), 1, turn)

    def prepare(area, c, total):
        widened = hidden_rows[area, span(c)].astype(jnp.float32)
        scaled = (widened * gain_row[:, span(c)]).astype(jnp.bfloat16)
        hidden_rows[area, span(c)] = scaled
        squared = widened * widened
        for start in range(0, chunk, LANES):
            total = total + squared[:, start : start + LANES]
        return scaled, total

    def across(total):
        ones = jnp.ones((SUBLANES, LANES), jnp.float32)
        return exact(ones, total, 1, 1)

    def swap(source_ref, target_ref, index):
        going = copy(source_ref, target_ref, swap_sems.at[index], x_peer)
        going.start()
        return going

    gain_load.wait()
    away_total = jnp.zeros((local, LANES), jnp.float32)
    sums = jnp.zeros((local, half), jnp.float32)
    for c in range(chunks):
        ready(away_loads[c])
        scaled, away_total = prepare(away, c, away_total)
        ready(key_loads[c])
        sums = sums + dot_of(scaled, key_rows[span(c), :], 1, 0)
    partial[:, :half] = sums
    squares[...] = across(away_total)
    swaps = [
        swap(squares, peer_squares, 0),
        swap(partial.at[:, pl.ds(0, half)], peer_partial.at[:, pl.ds(0, half)], 1),
    ]
    sums = jnp.zeros((local, half), jnp.float32)
    for c in range(chunks):
        ready(value_loads[c])
        sums = sums + dot_of(hidden_rows[away, span(c)], value_rows[span(c), :], 1, 0)
    partial[:, half:] = sums
    swaps.append(swap(partial.at[:, pl.ds(half, half)], peer_partial.at[:, pl.ds(half, half)], 2))
    for item in pieces:
        spread(*item)
    mine_total = jnp.zeros((local, LANES), jnp.float32)
    key_sums = jnp.zeros((local, half), jnp.float32)
    value_sums = jnp.zeros((local, half), jnp.float32)
    for c in range(chunks):
        ready(mine_loads[c])
        scaled, mine_total = prepare(mine, c, mine_total)
        key_sums = key_sums + dot_of(scaled, key_rows[span(c), :], 1, 0)
        value_sums = value_sums + dot_of(scaled, value_rows[span(c), :], 1, 0)
    own_squares = across(mine_total)

    swaps[0].wait()
    eighths = jnp.full((SUBLANES, LANES), 1.0 / SUBLANES, jnp.float32)
    inverse_scale = lax.rsqrt(exact(own_squares + peer_squares[...], eighths, 0, 0) / D + EPSILON)
    row = pl.multiple_of((x * 4 + b) * local, local)
    swaps[1].wait()
    for g in range(half // HEAD_DIM):
        spot = slice(g * HEAD_DIM, (g + 1) * HEAD_DIM)
        key = (key_sums[:, spot] + peer_partial[:, spot]) * inverse_scale
        turned = key * cosine_ref[...] + pltpu.roll(key, HEAD_DIM // 2, 1) * sine_ref[...]
        column = pl.multiple_of(z * width + 2 * g * HEAD_DIM, HEAD_DIM)
        out_ref[pl.ds(row, local), pl.ds(column, HEAD_DIM)] = turned.astype(jnp.bfloat16)
    swaps[2].wait()
    for g in range(half // HEAD_DIM):
        spot = slice(g * HEAD_DIM, (g + 1) * HEAD_DIM)
        there = slice(half + g * HEAD_DIM, half + (g + 1) * HEAD_DIM)
        value = (value_sums[:, spot] + peer_partial[:, there]) * inverse_scale
        column = pl.multiple_of(z * width + (2 * g + 1) * HEAD_DIM, HEAD_DIM)
        out_ref[pl.ds(row, local), pl.ds(column, HEAD_DIM)] = value.astype(jnp.bfloat16)

    for turn in range(1, heads):
        send_z(region(x, b, z), 0, turn)
    for turn in range(len(joint) + 2):
        if turn < len(joint):
            spread(*joint[turn])
        if turn == 0:
            for item in pieces:
                relay(*item)
        if 1 <= turn < len(joint) + 1:
            relay(*joint[turn - 1])
        if turn == len(joint) + 1:
            for item in pieces:
                gathered(*item)
            for early in range(1, len(joint) - 2):
                gathered(*joint[early])
                accumulate(early)
        if turn >= 2:
            finish(*joint[turn - 2])
        if turn == 1:
            for item in pieces:
                finish(*item)
        if turn == 3:
            gathered(*joint[0])
            accumulate(0)
    for turn in range(max(1, len(joint) - 2), len(joint)):
        gathered(*joint[turn])
        accumulate(turn)
    for going in started:
        going.wait_send()


def collect(hidden_rows, gain, key_weight, value_weight, positions, basis, heads, tokens):
    depth = hidden_rows.shape[1]
    local = positions.shape[0]
    half, width = key_weight.shape[1], key_weight.shape[1] + value_weight.shape[1]
    half_width = HEAD_DIM // 2
    chunks = 4
    frequency = jnp.exp(
        jnp.arange(half_width, dtype=jnp.float32) * (-math.log(ROTARY_BASE) / half_width)
    )
    angles = positions.astype(jnp.float32)[:, None] * frequency[None, :]
    cosine, sine = jnp.cos(angles), jnp.sin(angles)
    dma = pltpu.SemaphoreType.DMA
    anywhere = pl.BlockSpec(memory_space=pltpu.HBM)
    inside = pl.BlockSpec(memory_space=pltpu.VMEM)
    return pl.pallas_call(
        functools.partial(collect_kernel, heads),
        out_shape=(
            jax.ShapeDtypeStruct((tokens, tokens), jnp.bfloat16),
            jax.ShapeDtypeStruct((tokens, tokens), jnp.bfloat16),
            jax.ShapeDtypeStruct((basis.shape[1], tokens), jnp.float32),
            jax.ShapeDtypeStruct((tokens, width), jnp.bfloat16),
        ),
        in_specs=[anywhere] * 4 + [inside] * 2 + [anywhere],
        out_specs=(inside,) * 4,
        scratch_shapes=[
            pltpu.VMEM((tokens, heads * width), jnp.bfloat16),
            pltpu.VMEM((heads * width, basis.shape[1]), jnp.float32),
            pltpu.VMEM((tokens, tokens), jnp.float32),
            pltpu.VMEM(hidden_rows.shape, jnp.bfloat16),
            pltpu.VMEM((1, depth), jnp.float32),
            pltpu.VMEM(key_weight.shape, jnp.bfloat16),
            pltpu.VMEM(value_weight.shape, jnp.bfloat16),
            pltpu.VMEM((local, width), jnp.float32),
            pltpu.VMEM((local, width), jnp.float32),
            pltpu.VMEM((SUBLANES, local), jnp.float32),
            pltpu.VMEM((SUBLANES, local), jnp.float32),
            dma((2, chunks)),
            dma((3, chunks)),
            dma((3, 2)),
            dma((2, heads, 2)),
            dma((2, heads, 2)),
            dma((2, heads, 2)),
            dma((2, heads, 2)),
            dma((2, heads, 2)),
            dma((2, heads, 4, 2)),
        ],
        compiler_params=pltpu.CompilerParams(
            collective_id=0, has_side_effects=True, vmem_limit_bytes=45 * 2**20
        ),
    )(
        hidden_rows,
        pltpu.with_memory_space_constraint(gain[None, :], pltpu.HBM),
        key_weight,
        value_weight,
        jnp.concatenate([cosine, cosine], axis=1),
        jnp.concatenate([-sine, sine], axis=1),
        pltpu.with_memory_space_constraint(basis, pltpu.HBM),
    )


def body(hidden, gain, key_weight, value_weight, positions, initial_basis):
    hidden_rows = hidden[0]
    local_tokens = positions.shape[1]
    seqs, batches, heads = lax.axis_size("seq"), lax.axis_size("batch"), lax.axis_size("head")
    tokens = local_tokens * seqs * batches
    if seqs == 2 and batches == 4 and tokens <= initial_basis.shape[0] * heads:
        collected = collect(
            hidden_rows,
            gain,
            key_weight,
            value_weight,
            positions[0],
            initial_basis,
            heads,
            tokens,
        )
        return iterate(*collected, initial_basis.shape[0] * heads)
    widened = hidden_rows.astype(jnp.float32)
    scaled = (widened * gain).astype(jnp.bfloat16)
    local_squares = jnp.sum(widened * widened, axis=1)
    key_columns = key_weight.shape[1]
    weights = jnp.concatenate([key_weight, value_weight], axis=1)
    own_squares = total_squares(local_squares, local_tokens)
    projected = lax.psum_scatter(
        jnp.dot(scaled, weights, preferred_element_type=jnp.float32),
        "seq",
        scatter_dimension=0,
        tiled=True,
    )
    inverse_scale = lax.rsqrt(own_squares / D + EPSILON)
    projected = projected * inverse_scale[:, None]
    key_rows = rotary(projected[:, :key_columns].reshape(local_tokens, -1, HEAD_DIM), positions[0])
    value_rows = projected[:, key_columns:].reshape(local_tokens, -1, HEAD_DIM)
    joint_rows = (
        jnp.stack([key_rows, value_rows], axis=2).reshape(local_tokens, -1).astype(jnp.bfloat16)
    )
    partial_value = lax.dot_general(
        joint_rows,
        lax.all_gather(joint_rows, "head", axis=1, tiled=True),
        (((0,), (0,)), ((), ())),
        preferred_element_type=jnp.float32,
    )
    token_total = local_tokens * lax.axis_size("seq") * lax.axis_size("batch")
    basis_block = initial_basis
    covariance = lax.psum(partial_value, ("seq", "batch")) / token_total
    for iteration in range(ITERS):
        whole_basis = whole_of(basis_block)
        images = jnp.dot(
            covariance,
            whole_basis,
            precision=lax.Precision.HIGHEST,
            preferred_element_type=jnp.float32,
        )
        gram_matrix = lax.psum(gram_of(images), "head") / whole_basis.shape[0]
        basis_block = orthonormal(images, gram_matrix)
    return basis_block


def solution(mesh):
    return jax.shard_map(
        body,
        mesh=mesh,
        in_specs=(
            P("batch", None, "seq"),
            P("seq"),
            P("seq", "head"),
            P("seq", "head"),
            P("batch", "seq"),
            P("head", None),
        ),
        out_specs=P("head", None),
        check_vma=False,
    )
```
